32 devices in a mesh: gx: 4 (over y, x), gy: 4 (over z), gz: 2 (over core).
Axes of the slice: x: 2, y: 2, z: 4, core: 2. Of those that a mesh axis runs over, the one named last changes fastest.
Arguments:
- src_fields: float32 [1024, 1080], P(('gx', 'gy', 'gz')), may hold values from -6 to 6
- owner_peer: int32 [1024, 8, 1], P(('gx', 'gy', 'gz')), may hold values from 0 to 15; in each aligned block of 256 rows (0 to 255, 256 to 511, ..., all dimensions but the last counted through in order) at most 18 rows name the same one
- src_local: int32 [1024, 8], P(('gx', 'gy', 'gz')), may hold values from 0 to 31
- jac: float32 [1024, 4096], P(('gx', 'gy', 'gz')), may hold values from 0.25 to 4
Outputs:
- remapped: float32 [1024, 1080], P(('gx', 'gy', 'gz'))
- nodal_accel: float32 [1024, 648], P(('gx', 'gy', 'gz'))
The draws below stay inside these ranges and needn't reach their ends.
Inputs may be any that keep to these rules, and one draw needn't show every extreme that they name: owner_peer[r, k, 0] is the index, within the 16 devices that share target r's gz index (gx-major), of the device owning intersection k's source element; among the 256 intersections of one device's targets at most 18 name the same device, and some device reaches 18 in every draw.
All inputs are finite; a program needn't handle non-finite values.
Results may differ from the reference program's by a relative error of at most 0.0002.
Values sent between devices are 32-bit elements; how exact they have to be, the bound alone decides.
No kernel may reach another device: no remote copies, remote signals or barrier semaphores. Data moves between devices by JAX's collectives and lax.ppermute only.
A program may use at most 64 MiB of HBM per device.

```python
import math
import jax
import jax.numpy as jnp
import numpy as np
from jax import lax

EX = 4
EY = 4
EZ = 2
FIELDS = 5
NB = 216
QP = 512
OVL = 8
E_DEV = 32
GROUP = 16
CAP = 18
ELEMS = 1024
N_GX = 4
N_GY = 4
N_GZ = 2


def touch_ends(entries, stream_key, low, top_value):
    spot = [jax.random.randint(jax.random.fold_in(stream_key, axis), (), 0, length) for axis, length in enumerate(entries.shape)]
    longest = entries.shape.index(max(entries.shape))
    next_to = spot[:longest] + [(spot[longest] + 1) % entries.shape[longest]] + spot[longest + 1:]
    return entries.at[tuple(spot)].set(low).at[tuple(next_to)].set(top_value)


def levels(rng, shape, cuts, smallest, top_value):
    level = 1.0
    for dim, blocks in cuts:
        heights = jax.random.uniform(jax.random.fold_in(jax.random.fold_in(rng, 6), dim), (blocks,), jnp.float32, smallest / len(cuts), top_value / len(cuts))
        level = level * jnp.repeat(jnp.exp(heights), shape[dim] // blocks).reshape((-1,) + (1,) * (len(shape) - 1 - dim))
    return level


def assign_block(own_key, own, number, rows, count, top, most, slope):
    order = jax.random.permutation(own_key, count)
    heavy_load, ordinary = load_shares(count, rows * top, most, slope, True), load_shares(count, rows * top, most, slope, False)
    places = jnp.arange(count)

    def named(tallies, rotation):
        used = int((tallies > 0).sum())
        fixed = max(1, used // 4)
        passed = fixed + (places - fixed + rotation * (used - fixed)) % max(1, count - fixed)
        return jnp.zeros((count,), jnp.int32).at[order[jnp.where(places < fixed, places, passed)]].set(jnp.asarray(tallies, jnp.int32))

    tallies = jnp.where(number % 4 == 0, named(heavy_load, number // 4), named(ordinary, number - number // 4 - 1))
    mixed = jax.random.permutation(jax.random.fold_in(own, 3), count)
    source_of, sink = mixed[0:count // 2 * 2:2], mixed[1:count // 2 * 2:2]
    slack = jnp.minimum(tallies[source_of] - 1, most - tallies[sink]) // 2
    slack = jnp.where((source_of == order[0]) | (sink == order[0]) | (tallies[sink] == 0), 0, jnp.maximum(slack, 0))
    passed = jax.random.randint(jax.random.fold_in(own, 4), (count // 2,), 0, 1 << 20) % (slack + 1)
    tallies = tallies.at[source_of].add(-passed).at[sink].add(passed)
    members = jnp.searchsorted(jnp.cumsum(tallies), jnp.arange(rows * top), side="right").astype(jnp.int32)
    listing = members.reshape(top, rows).T
    listing = listing[jax.random.permutation(jax.random.fold_in(own, 1), rows)]
    rotation = jax.random.randint(jax.random.fold_in(own, 2), (rows, 1), 0, top)
    return jnp.take_along_axis(listing, (jnp.arange(top)[None, :] + rotation) % top, axis=1)


def load_shares(amount, total, most, slope, full):
    weights = [(1 << 20) // math.isqrt(standing ** slope) + 1 for standing in range(1, amount + 1)]
    largest = most if full else min(most, max(-(-total // amount), total * weights[0] // sum(weights)))
    least = 1 if total - largest >= amount - 1 else 0
    holding, rest = [largest] + [least] * (amount - 1), total - largest - least * (amount - 1)
    while rest > 0:
        free = [i for i in range(1, amount) if holding[i] < largest] or [i for i in range(1, amount) if holding[i] < most]
        pool, remaining = sum([weights[i] for i in free]), rest
        for i in free:
            extra = min(most - holding[i], max(1, remaining * weights[i] // pool), rest)
            holding[i] = holding[i] + extra
            rest = rest - extra
    return np.array(holding)


def centred(stream_key, shape, width, reach, split=(), kind=jnp.bfloat16):
    drawn = jax.random.normal(stream_key, shape, jnp.float32) * width
    if len(split) > 0:
        drawn = levels(stream_key, shape, split, -0.22, 0.18) * drawn
    return jnp.clip(drawn, min=-reach, max=reach).astype(kind)


def setup_inputs(seed: int = 0) -> dict:
    key_of = jax.random.split(jax.random.key(seed), 5)
    src_fields = centred(key_of[0], (ELEMS, FIELDS * NB), 1.0, 6.0, ((0, 32),), jnp.float32)
    owner_peer_keys = jax.random.split(jax.random.fold_in(key_of[1], 1), ELEMS * OVL // (8 * E_DEV))
    owner_peer_turns = jax.random.permutation(jax.random.fold_in(key_of[1], 3), ELEMS * OVL // (8 * E_DEV))
    owner_peer = jax.vmap(lambda own, number: assign_block(jax.random.fold_in(key_of[1], 2), own, number, 8 * E_DEV, GROUP, 1, CAP, 2))(owner_peer_keys, owner_peer_turns).reshape((ELEMS, OVL, 1))
    src_local = touch_ends(jax.random.randint(key_of[2], (ELEMS, OVL), 0, E_DEV), jax.random.fold_in(key_of[2], 1), 0, E_DEV - 1).astype(jnp.int32)
    jac = jnp.clip(jnp.exp(math.log(4.0) - 2.7725887 * jax.random.uniform(key_of[3], (ELEMS, OVL * QP), jnp.float32) ** levels(key_of[3], (ELEMS, OVL * QP), ((0, 32),), -0.2, 0.2)), 0.25, 4.0)
    return {"src_fields": src_fields, "owner_peer": owner_peer, "src_local": src_local, "jac": jac}


def bern_table(points):
    cols = [math.comb(5, i) * points ** i * (1.0 - points) ** (5 - i) for i in range(6)]
    return np.stack(cols, -1)


def remap_tables():
    mids = (np.arange(8) + 0.5) / 16.0
    src_one = []
    tgt_one = []
    for bit in range(2):
        target_pts = bit * 0.5 + mids
        source_pts = target_pts + 0.5 - bit
        src_one.append(bern_table(source_pts).T)
        tgt_one.append(bern_table(target_pts) / 16.0)
    source_list = []
    project_list = []
    for intersection in range(8):
        bit_x, bit_y, bit_z = (intersection >> 2) & 1, (intersection >> 1) & 1, intersection & 1
        source_list.append(np.kron(src_one[bit_x], np.kron(src_one[bit_y], src_one[bit_z])))
        project_list.append(np.kron(tgt_one[bit_x], np.kron(tgt_one[bit_y], tgt_one[bit_z])))
    return jnp.asarray(np.stack(source_list), jnp.float32), jnp.asarray(np.stack(project_list), jnp.float32)


def lower_integral(first, second):
    if first < 0 or first > 4:
        return 0.0
    return math.comb(4, first) * math.comb(5, second) / (10.0 * math.comb(9, first + second))


def force_table():
    mass_one = np.zeros((6, 6))
    grad_one = np.zeros((6, 6))
    for left in range(6):
        for right in range(6):
            mass_one[left, right] = math.comb(5, left) * math.comb(5, right) / (11.0 * math.comb(10, left + right))
            grad_one[left, right] = 5.0 * (lower_integral(left - 1, right) - lower_integral(left, right))
    grad_x = np.kron(grad_one, np.kron(mass_one, mass_one))
    grad_y = np.kron(mass_one, np.kron(grad_one, mass_one))
    grad_z = np.kron(mass_one, np.kron(mass_one, grad_one))
    joined = np.concatenate([grad_x.T, grad_y.T, grad_z.T], 1) * 8.0
    return jnp.asarray(joined, jnp.float32)


def remap_block(fetch_rows, weights, source_tab, project_tab, force_tab):
    count = weights.shape[0]
    hi = lax.Precision.HIGHEST
    total = jnp.zeros((count * FIELDS, NB), jnp.float32)
    for intersection in range(OVL):
        rows = fetch_rows(intersection).reshape(count * FIELDS, NB)
        values = jnp.dot(rows, source_tab[intersection], precision=hi)
        scaled = values.reshape(count, FIELDS, QP) * weights[:, None, intersection * QP:(intersection + 1) * QP]
        total = total + jnp.dot(scaled.reshape(count * FIELDS, QP), project_tab[intersection], precision=hi)
    lumped = jnp.dot(weights, project_tab.reshape(OVL * QP, NB), precision=hi)
    fields = total.reshape(count, FIELDS, NB) / lumped[:, None, :]
    pressure = fields[:, 0, :] * fields[:, 1, :]
    force = jnp.dot(pressure, force_tab, precision=hi)
    parts = jnp.concatenate([force.reshape(count, 3, NB), lumped[:, None, :]], 1)
    return fields.reshape(count, FIELDS * NB), parts


def spread(field, elem_axis, node_axis):
    moved = jnp.moveaxis(field, (elem_axis, node_axis), (-2, -1))
    count = moved.shape[-2]
    lead = moved.shape[:-2]
    lower = moved[..., :5].reshape(lead + (5 * count,))
    upper = jnp.concatenate([jnp.zeros(lead + (count, 4), moved.dtype), moved[..., 5:]], -1).reshape(lead + (5 * count,))
    spec = [(0, 0)] * len(lead)
    lattice = jnp.pad(lower, spec + [(0, 1)]) + jnp.pad(upper, spec + [(1, 0)])
    return jnp.moveaxis(lattice, -1, elem_axis)


def unspread(lattice, axis):
    moved = jnp.moveaxis(lattice, axis, -1)
    count = (moved.shape[-1] - 1) // 5
    lead = moved.shape[:-1]
    lower = moved[..., :5 * count].reshape(lead + (count, 5))
    last = moved[..., 5::5][..., None]
    nodes = jnp.concatenate([lower, last], -1)
    return jnp.moveaxis(nodes, -2, axis)


def reference(src_fields, owner_peer, src_local, jac):
    source_tab, project_tab = remap_tables()
    force_tab = force_table()
    blocks = ELEMS // E_DEV
    row_ids = jnp.arange(ELEMS, dtype=jnp.int32)
    zpos = (row_ids // E_DEV) % N_GZ
    source_row = (owner_peer[:, :, 0] * N_GZ + zpos[:, None]) * E_DEV + src_local

    def one_block(packed):
        index_rows, weights = packed

        def fetch_rows(intersection):
            return jnp.take(src_fields, index_rows[:, intersection], axis=0)

        return remap_block(fetch_rows, weights, source_tab, project_tab, force_tab)

    fields, parts = lax.map(one_block, (source_row.reshape(blocks, E_DEV, OVL), jac.reshape(blocks, E_DEV, OVL * QP)))
    remapped = fields.reshape(ELEMS, FIELDS * NB)
    grid = parts.reshape(N_GX, N_GY, N_GZ, EX, EY, EZ, 4, 6, 6, 6)
    grid = jnp.transpose(grid, (6, 0, 3, 1, 4, 2, 5, 7, 8, 9)).reshape(4, N_GX * EX, N_GY * EY, N_GZ * EZ, 6, 6, 6)
    lattice = spread(spread(spread(grid, 1, 4), 2, 4), 3, 4)
    accel = lattice[:3] / lattice[3:4]
    back = unspread(unspread(unspread(accel, 1), 2), 3)
    back = back.reshape(3, N_GX, EX, N_GY, EY, N_GZ, EZ, NB)
    nodal_accel = jnp.transpose(back, (1, 3, 5, 2, 4, 6, 0, 7)).reshape(ELEMS, 3 * NB)
    return remapped, nodal_accel
```

```python
import math

import jax
import jax.numpy as jnp
import numpy as np
from jax import lax
from jax.experimental import pallas as pl
from jax.experimental.pallas import tpu as pltpu
from jax.sharding import PartitionSpec as P

EX = 4
EY = 4
EZ = 2
FIELDS = 5
NB = 216
QP = 512
OVL = 8
PAD = 256
BF = jnp.bfloat16
F32 = jnp.float32


def bern_table(points):
    cols = [math.comb(5, i) * points**i * (1.0 - points) ** (5 - i) for i in range(6)]
    return np.stack(cols, -1)


def three_way(table):
    parts = []
    rest = np.asarray(table, np.float32)
    for _ in range(3):
        part = rest.astype(jnp.bfloat16)
        parts.append(part)
        rest = rest - part.astype(np.float32)
    return parts


def factor_rows():
    mids = (np.arange(8) + 0.5) / 16.0
    point = np.arange(QP)
    out = []
    for stride in (64, 8, 1):
        for bit in range(2):
            points = bit * 0.5 + mids + 0.5 - bit
            rows = np.zeros((8, QP), np.float32)
            rows[:6] = bern_table(points).T[:, point // stride % 8]
            out.append(np.concatenate(three_way(rows) + [np.zeros((8, QP), jnp.bfloat16)], 0))
    return jnp.asarray(np.stack(out), BF)


def lower_integral(first, second):
    if first < 0 or first > 4:
        return 0.0
    return math.comb(4, first) * math.comb(5, second) / (10.0 * math.comb(9, first + second))


def force_table():
    mass_one = np.zeros((6, 6))
    grad_one = np.zeros((6, 6))
    for left in range(6):
        for right in range(6):
            mass_one[left, right] = (
                math.comb(5, left) * math.comb(5, right) / (11.0 * math.comb(10, left + right))
            )
            grad_one[left, right] = 5.0 * (
                lower_integral(left - 1, right) - lower_integral(left, right)
            )
    grad_x = np.kron(grad_one, np.kron(mass_one, mass_one))
    grad_y = np.kron(mass_one, np.kron(grad_one, mass_one))
    grad_z = np.kron(mass_one, np.kron(mass_one, grad_one))
    joined = np.zeros((NB, 3 * PAD), np.float32)
    for c, grad in enumerate((grad_x, grad_y, grad_z)):
        joined[:, c * PAD : c * PAD + NB] = grad.T * 8.0
    high, low, _ = three_way(joined)
    return jnp.asarray(high, BF), jnp.asarray(low, BF)


def split(value):
    high = value.astype(BF)
    return high, (value - high.astype(F32)).astype(BF)


def dot(a, b, dims=((1,), (0,))):
    return lax.dot_general(a, b, (dims, ((), ())), preferred_element_type=F32)


def dot3(a, b, dims=((1,), (0,))):
    return dot(a[0], b[0], dims) + (dot(a[0], b[1], dims) + dot(a[1], b[0], dims))


NT = ((1,), (1,))


def prep_kernel(rows_ref, jac_ref, high_ref, low_ref, lumped_ref):
    coef = lax.broadcasted_iota(jnp.int32, (NB, 32), 0)
    col = lax.broadcasted_iota(jnp.int32, (NB, 32), 1)
    factors = []
    for d, stride in enumerate((36, 6, 1)):
        hit = (coef // stride % 6 == col % 8) & (col < 24)
        pick = jnp.where(hit, 1.0, 0.0).astype(BF)
        factors.append([dot(pick, rows_ref[2 * d + bit]) for bit in range(2)])
    for k in range(OVL):
        table = factors[0][k >> 2 & 1] * factors[1][k >> 1 & 1] * factors[2][k & 1]
        high, low = split(table)
        high_ref[k] = high
        low_ref[k] = low
    total = jnp.zeros((jac_ref.shape[0], NB), F32)
    for k in range(OVL):
        weights = split(jac_ref[:, k * QP : (k + 1) * QP])
        total = total + dot3(weights, (high_ref[7 - k], low_ref[7 - k]), NT)
    lumped_ref[...] = total


def main_kernel(slots, index_ref, jac_ref, high_ref, low_ref, lumped_ref, fhigh_ref, flow_ref, *rest):
    shards = rest[:slots]
    fields_ref, parts_ref, first_ref, last_ref, picked_high, picked_low = rest[slots:]
    elems = jac_ref.shape[0]
    rows = elems * slots
    lane = lax.broadcasted_iota(jnp.int32, (elems, rows), 1)
    hot = [
        jnp.where(index_ref[:, k : k + 1] == lane, 1.0, 0.0).astype(BF) for k in range(OVL)
    ]
    hot = jnp.concatenate(hot, 0)
    step = 8
    for s in range(0, slots, step):
        group = jnp.concatenate([r[...] for r in shards[s : s + step]], 0)
        high, low = split(group)
        part = hot[:, s * elems : s * elems + group.shape[0]]
        add_high = dot(part, high)
        add_low = dot(part, low)
        if s == 0:
            picked_high[...] = add_high
            picked_low[...] = add_low
        else:
            picked_high[...] += add_high
            picked_low[...] += add_low
    total = jnp.zeros((FIELDS * elems, NB), F32)
    for k in range(OVL):
        at = slice(k * elems, (k + 1) * elems)
        source = tuple(
            jnp.concatenate(
                [ref[at, f * NB : (f + 1) * NB] for f in range(FIELDS)], 0
            ).astype(BF)
            for ref in (picked_high, picked_low)
        )
        values = dot3(source, (high_ref[k], low_ref[k]))
        weights = jac_ref[:, k * QP : (k + 1) * QP]
        scaled = values * jnp.concatenate([weights] * FIELDS, 0)
        total = total + dot3(split(scaled), (high_ref[7 - k], low_ref[7 - k]), NT)
    lumped = lumped_ref[...]
    fields = [total[f * elems : (f + 1) * elems] / lumped for f in range(FIELDS)]
    for f in range(FIELDS):
        fields_ref[:, f * NB : (f + 1) * NB] = fields[f]
    pressure = fields[0] * fields[1]
    force = dot3(split(pressure), (fhigh_ref[...], flow_ref[...]))
    mass = jnp.concatenate([lumped * (1.0 / 4096.0), jnp.zeros((elems, PAD - NB), F32)], 1)
    parts = jnp.concatenate([force, mass], 1)
    parts_ref[...] = parts
    width = EY * EZ
    first_ref[...] = parts[:width]
    last_ref[...] = parts[-width:]


def face_add(parts, before, after, shift, stride):
    comps = []
    elems = parts.shape[0]
    lane = lax.broadcasted_iota(jnp.int32, (elems, PAD), 1)
    spot = lane // stride % 6
    inside = lane < NB
    for c in range(4):
        at = slice(c * PAD, (c + 1) * PAD)
        low = pltpu.roll(before[:, at], PAD - shift, 1)
        high = pltpu.roll(after[:, at], shift, 1)
        low = jnp.where((spot == 0) & inside, low, 0.0)
        high = jnp.where((spot == 5) & inside, high, 0.0)
        comps.append(parts[:, at] + (low + high))
    return jnp.concatenate(comps, 1)


def x_kernel(parts_ref, before_ref, after_ref, out_ref, first_ref, last_ref):
    parts = parts_ref[...]
    width = EY * EZ
    before = jnp.concatenate([before_ref[...], parts[:-width]], 0)
    after = jnp.concatenate([parts[width:], after_ref[...]], 0)
    parts = face_add(parts, before, after, 180, 36)
    out_ref[...] = parts
    for x in range(EX):
        base = x * width
        first_ref[x * EZ : (x + 1) * EZ] = parts[base : base + EZ]
        last_ref[x * EZ : (x + 1) * EZ] = parts[base + width - EZ : base + width]


def y_kernel(parts_ref, before_ref, after_ref, out_ref):
    parts = parts_ref[...]
    width = EY * EZ
    before = []
    after = []
    for x in range(EX):
        base = x * width
        near = slice(x * EZ, (x + 1) * EZ)
        before += [before_ref[near], parts[base : base + width - EZ]]
        after += [parts[base + EZ : base + width], after_ref[near]]
    before = jnp.concatenate(before, 0)
    after = jnp.concatenate(after, 0)
    out_ref[...] = face_add(parts, before, after, 30, 6)


def z_kernel(spot_ref, parts_ref, before_ref, after_ref, out_ref):
    parts = parts_ref[...]
    elems = parts.shape[0]
    odd = lax.broadcasted_iota(jnp.int32, parts.shape, 0) % EZ == EZ - 1
    has_before = spot_ref[0] > 0
    has_after = spot_ref[0] < spot_ref[1] - 1
    far_before = jnp.where(has_before, pltpu.roll(before_ref[...], elems - 1, 0), 0.0)
    far_after = jnp.where(has_after, pltpu.roll(after_ref[...], 1, 0), 0.0)
    before = jnp.where(odd, pltpu.roll(parts, 1, 0), far_before)
    after = jnp.where(odd, far_after, pltpu.roll(parts, elems - 1, 0))
    parts = face_add(parts, before, after, 5, 1)
    mass = parts[:, 3 * PAD :]
    for c in range(3):
        accel = parts[:, c * PAD : c * PAD + NB] / mass[:, :NB]
        out_ref[:, c * NB : (c + 1) * NB] = accel


VM = pl.BlockSpec(memory_space=pltpu.VMEM)
SM = pl.BlockSpec(memory_space=pltpu.SMEM)


def call(kernel, shapes, specs, scratch=(), cost=None):
    return pl.pallas_call(
        kernel,
        out_shape=shapes,
        in_specs=specs,
        out_specs=jax.tree.map(lambda _: VM, shapes),
        scratch_shapes=scratch,
        cost_estimate=cost,
        compiler_params=pltpu.CompilerParams(vmem_limit_bytes=48 << 20),
    )


def partner(count, step):
    if count & (count - 1) == 0:
        return [(i, i ^ step) for i in range(count)]
    return [(i, (i + step) % count) for i in range(count)]


def slot_of(owner, me, count):
    if count & (count - 1) == 0:
        return owner ^ me
    return (me - owner) % count


def shape(dims, dtype=F32):
    return jax.ShapeDtypeStruct(dims, dtype)


def per_device(src_fields, owner_peer, src_local, jac):
    n_x = lax.axis_size("gx")
    n_y = lax.axis_size("gy")
    n_z = lax.axis_size("gz")
    elems = src_fields.shape[0]
    column = [src_fields]
    for step in range(1, n_y):
        column.append(lax.ppermute(src_fields, "gy", partner(n_y, step)))
    planes = [column]
    for step in range(1, n_x):
        planes.append([lax.ppermute(c, "gx", partner(n_x, step)) for c in column])
    shards = [piece for plane in planes for piece in plane]
    owner = owner_peer[:, :, 0]
    slot = slot_of(owner // n_y, lax.axis_index("gx"), n_x) * n_y
    slot = slot + slot_of(owner % n_y, lax.axis_index("gy"), n_y)
    index = slot * elems + src_local
    fhigh, flow = force_table()
    high, low, lumped = call(
        prep_kernel,
        (shape((OVL, NB, QP), BF), shape((OVL, NB, QP), BF), shape((elems, NB))),
        [VM, VM],
        cost=pl.CostEstimate(flops=4_000_000_000, bytes_accessed=8_000_000, transcendentals=0),
    )(factor_rows(), jac)
    face = EY * EZ
    fields, parts, first, last = call(
        lambda *refs: main_kernel(len(shards), *refs),
        (
            shape((elems, FIELDS * NB)),
            shape((elems, 4 * PAD)),
            shape((face, 4 * PAD)),
            shape((face, 4 * PAD)),
        ),
        [VM] * (7 + len(shards)),
        [pltpu.VMEM((OVL * elems, FIELDS * NB), F32)] * 2,
    )(index, jac, high, low, lumped, fhigh, flow, *shards)

    def halo(first, last, axis, count):
        up = [(i, i + 1) for i in range(count - 1)]
        down = [(i + 1, i) for i in range(count - 1)]
        return lax.ppermute(last, axis, up), lax.ppermute(first, axis, down)

    before, after = halo(first, last, "gx", n_x)
    parts, first, last = call(
        x_kernel,
        (
            shape((elems, 4 * PAD)),
            shape((EX * EZ, 4 * PAD)),
            shape((EX * EZ, 4 * PAD)),
        ),
        [VM] * 3,
    )(parts, before, after)
    before, after = halo(first, last, "gy", n_y)
    parts = call(y_kernel, shape((elems, 4 * PAD)), [VM] * 3)(parts, before, after)
    if n_z == 2:
        before = after = lax.ppermute(parts, "gz", [(0, 1), (1, 0)])
    else:
        before, after = halo(parts, parts, "gz", n_z)
    spot = jnp.stack([lax.axis_index("gz"), jnp.int32(n_z)])
    accel = call(z_kernel, shape((elems, 3 * NB)), [SM] + [VM] * 3)(spot, parts, before, after)
    return fields, accel


def solution(mesh):
    placed = (
        P(("gx", "gy", "gz"), None),
        P(("gx", "gy", "gz"), None, None),
        P(("gx", "gy", "gz"), None),
        P(("gx", "gy", "gz"), None),
    )
    return jax.shard_map(
        per_device,
        mesh=mesh,
        in_specs=placed,
        out_specs=(P(("gx", "gy", "gz"), None), P(("gx", "gy", "gz"), None)),
        check_vma=False,
    )
```

```python
import math

import jax
import jax.numpy as jnp
import numpy as np
from jax import lax
from jax.experimental import pallas as pl
from jax.experimental.pallas import tpu as pltpu
from jax.sharding import PartitionSpec as P

EX = 4
EY = 4
EZ = 2
FIELDS = 5
NB = 216
QP = 512
OVL = 8
PAD = 256
CUT = 512
BF = jnp.bfloat16
F32 = jnp.float32


def bern_table(points):
    cols = [math.comb(5, i) * points**i * (1.0 - points) ** (5 - i) for i in range(6)]
    return np.stack(cols, -1)


def three_way(table):
    parts = []
    rest = np.asarray(table, np.float32)
    for _ in range(3):
        part = rest.astype(jnp.bfloat16)
        parts.append(part)
        rest = rest - part.astype(np.float32)
    return parts


def factor_rows():
    mids = (np.arange(8) + 0.5) / 16.0
    point = np.arange(QP)
    out = []
    for stride in (64, 8, 1):
        for bit in range(2):
            points = bit * 0.5 + mids + 0.5 - bit
            rows = np.zeros((8, QP), np.float32)
            rows[:6] = bern_table(points).T[:, point // stride % 8]
            out.append(np.concatenate(three_way(rows) + [np.zeros((8, QP), jnp.bfloat16)], 0))
    return jnp.asarray(np.stack(out), BF)


def lower_integral(first, second):
    if first < 0 or first > 4:
        return 0.0
    return math.comb(4, first) * math.comb(5, second) / (10.0 * math.comb(9, first + second))


def force_table():
    mass_one = np.zeros((6, 6))
    grad_one = np.zeros((6, 6))
    for left in range(6):
        for right in range(6):
            mass_one[left, right] = (
                math.comb(5, left) * math.comb(5, right) / (11.0 * math.comb(10, left + right))
            )
            grad_one[left, right] = 5.0 * (
                lower_integral(left - 1, right) - lower_integral(left, right)
            )
    grad_x = np.kron(grad_one, np.kron(mass_one, mass_one))
    grad_y = np.kron(mass_one, np.kron(grad_one, mass_one))
    grad_z = np.kron(mass_one, np.kron(mass_one, grad_one))
    joined = np.zeros((NB, 3 * PAD), np.float32)
    for c, grad in enumerate((grad_x, grad_y, grad_z)):
        joined[:, c * PAD : c * PAD + NB] = grad.T * 8.0
    high, low, _ = three_way(joined)
    return jnp.asarray(high, BF), jnp.asarray(low, BF)


def split(value):
    high = value.astype(BF)
    return high, (value - high.astype(F32)).astype(BF)


def dot(a, b, dims=((1,), (0,))):
    return lax.dot_general(a, b, (dims, ((), ())), preferred_element_type=F32)


def dot3(a, b, dims=((1,), (0,))):
    return dot(a[0], b[0], dims) + (dot(a[0], b[1], dims) + dot(a[1], b[0], dims))


NT = ((1,), (1,))


def prep_kernel(rows_ref, jac_ref, high_ref, low_ref, lumped_ref):
    coef = lax.broadcasted_iota(jnp.int32, (NB, 32), 0)
    col = lax.broadcasted_iota(jnp.int32, (NB, 32), 1)
    factors = []
    for d, stride in enumerate((36, 6, 1)):
        hit = (coef // stride % 6 == col % 8) & (col < 24)
        pick = jnp.where(hit, 1.0, 0.0).astype(BF)
        factors.append([dot(pick, rows_ref[2 * d + bit]) for bit in range(2)])
    for k in range(OVL):
        table = factors[0][k >> 2 & 1] * factors[1][k >> 1 & 1] * factors[2][k & 1]
        high, low = split(table)
        high_ref[k] = high
        low_ref[k] = low
    total = jnp.zeros((jac_ref.shape[0], NB), F32)
    for k in range(OVL):
        weights = split(jac_ref[:, k * QP : (k + 1) * QP])
        total = total + dot3(weights, (high_ref[7 - k], low_ref[7 - k]), NT)
    lumped_ref[...] = total


def hits(index_ref, wanted):
    elems = index_ref.shape[0]
    out = []
    for k in range(OVL):
        column = jnp.broadcast_to(index_ref[:, k : k + 1], (elems, wanted.shape[1]))
        out.append(jnp.where(column == wanted, 1.0, 0.0))
    return out


def packing(mask, capacity, elems, owners):
    width = owners * elems
    row = lax.broadcasted_iota(jnp.int32, (width, width), 0)
    col = lax.broadcasted_iota(jnp.int32, (width, width), 1)
    earlier = jnp.where((row // elems == col // elems) & (row < col), 1.0, 0.0).astype(BF)
    rank = dot(jnp.broadcast_to(mask, (8, width)).astype(BF), earlier)[:1]
    slots = owners * capacity
    spot = lax.broadcasted_iota(jnp.int32, (slots, width), 0)
    lane = lax.broadcasted_iota(jnp.int32, (slots, width), 1)
    wanted = (lane // elems * capacity).astype(F32) + rank
    hit = (spot.astype(F32) == wanted) & (jnp.broadcast_to(mask, (slots, width)) > 0.5)
    return jnp.where(hit, 1.0, 0.0).astype(BF)


def index_kernel(owners, capacity, index_ref, ids_ref, *mask_refs):
    elems = index_ref.shape[0]
    width = owners * elems
    lane = lax.broadcasted_iota(jnp.int32, (elems, (1 + len(mask_refs)) * width), 1)
    named = sum(hits(index_ref, lane))
    named = jnp.sum(named, 0, keepdims=True)
    mask = jnp.where(named > 0.5, 1.0, 0.0)
    ids_ref[:, :width] = lane[:1, :width]
    local = lax.broadcasted_iota(jnp.int32, (8, width), 1) + 1
    slots = owners * capacity
    for s, mask_ref in enumerate(mask_refs):
        part = mask[:, (s + 1) * width : (s + 2) * width]
        mask_ref[...] = jnp.broadcast_to(part, mask_ref.shape)
        order = packing(part, capacity, elems, owners)
        ids = dot(local.astype(F32).astype(BF), order, NT)[:1].astype(jnp.int32)
        ids = jnp.where(ids > 0, ids + ((s + 1) * width - 1), -1)
        ids_ref[:, width + s * slots : width + (s + 1) * slots] = ids


def pack_kernel(owners, capacity, count, *refs):
    masks = refs[:count]
    column = refs[count : count + owners]
    outs = refs[count + owners :]
    elems = column[0].shape[0]
    rows = jnp.concatenate([ref[...] for ref in column], 0)
    high = rows.astype(BF)
    rest = rows - high.astype(F32)
    middle, low = split(rest)
    order = jnp.concatenate(
        [packing(mask[:1], capacity, elems, owners) for mask in masks], 0
    )
    packed = (dot(order, high) + dot(order, middle)) + dot(order, low)
    slots = owners * capacity
    for s in range(count):
        part = packed[s * slots : (s + 1) * slots]
        outs[2 * s][...] = part[:, :CUT]
        outs[2 * s + 1][...] = part[:, CUT:]


def pick(hot, pieces, outs):
    rows = jnp.concatenate(pieces, 0)
    high, low = split(rows)
    outs[0][...] = dot(hot, high)
    outs[1][...] = dot(hot, low)


def project(count, offset, picked, jac_ref, high_ref, low_ref):
    elems = jac_ref.shape[0]
    size = count * elems
    total = jnp.zeros((size, NB), F32)

    def apply(pair, table, dims=((1,), (0,))):
        both = dot(jnp.concatenate(pair, 0), high_ref[table], dims)
        return both[:size] + (both[size:] + dot(pair[0], low_ref[table], dims))

    for k in range(OVL):
        at = slice(k * elems, (k + 1) * elems)
        source = tuple(
            jnp.concatenate(
                [ref[at, offset + f * NB : offset + (f + 1) * NB] for f in range(count)], 0
            ).astype(BF)
            for ref in picked
        )
        values = apply(source, k)
        weights = jac_ref[:, k * QP : (k + 1) * QP]
        scaled = values * jnp.concatenate([weights] * count, 0)
        total = total + apply(split(scaled), 7 - k, NT)
    return total


def send_faces(parity_even, first, last, send_ref, back_ref):
    send_ref[...] = jnp.where(parity_even, last, first)
    back_ref[...] = jnp.where(parity_even, first, last)


def take_faces(spot_ref, axis, got, back):
    me, count = spot_ref[axis], spot_ref[axis + 3]
    even = me % 2 == 0
    before = jnp.where(even, back, got)
    after = jnp.where(even, got, back)
    return jnp.where(me > 0, before, 0.0), jnp.where(me < count - 1, after, 0.0)


def lead_kernel(owners, count, spot_ref, ids_ref, index_ref, jac_ref, high_ref, low_ref, lumped_ref, fhigh_ref, flow_ref, *rest):
    column = rest[:owners]
    packed = rest[owners : owners + count]
    fields_ref, parts_ref, send_ref, back_ref, picked_high, picked_low = rest[owners + count :]
    elems = jac_ref.shape[0]
    hot = jnp.concatenate(hits(index_ref, ids_ref[...]), 0).astype(BF)
    pieces = [ref[:, :CUT] for ref in column] + [ref[...] for ref in packed]
    picked = (picked_high, picked_low)
    pick(hot, pieces, picked)
    total = project(2, 0, picked, jac_ref, high_ref, low_ref)
    lumped = lumped_ref[...]
    fields = [total[f * elems : (f + 1) * elems] / lumped for f in range(2)]
    for f in range(2):
        fields_ref[:, f * NB : (f + 1) * NB] = fields[f]
    pressure = fields[0] * fields[1]
    force = dot3(split(pressure), (fhigh_ref[...], flow_ref[...]))
    mass = jnp.concatenate([lumped * (1.0 / 4096.0), jnp.zeros((elems, PAD - NB), F32)], 1)
    parts = jnp.concatenate([force, mass], 1)
    parts_ref[...] = parts
    width = EY * EZ
    send_faces(spot_ref[0] % 2 == 0, parts[:width], parts[-width:], send_ref, back_ref)


def tail_kernel(owners, count, ids_ref, index_ref, jac_ref, high_ref, low_ref, lumped_ref, lead_ref, *rest):
    column = rest[:owners]
    packed = rest[owners : owners + 2 * count]
    fields_ref, picked_high, picked_low = rest[owners + 2 * count :]
    elems = jac_ref.shape[0]
    hot = jnp.concatenate(hits(index_ref, ids_ref[...]), 0).astype(BF)
    start = CUT - 128
    pieces = [ref[:, start:] for ref in column]
    for s in range(count):
        pieces.append(jnp.concatenate([packed[2 * s][:, start:], packed[2 * s + 1][...]], 1))
    picked = (picked_high, picked_low)
    pick(hot, pieces, picked)
    total = project(3, 2 * NB - start, picked, jac_ref, high_ref, low_ref)
    lumped = lumped_ref[...]
    fields_ref[:, : 2 * NB] = lead_ref[...]
    for f in range(3):
        fields_ref[:, (f + 2) * NB : (f + 3) * NB] = total[f * elems : (f + 1) * elems] / lumped


def face_add(parts, before, after, shift, stride):
    comps = []
    elems = parts.shape[0]
    lane = lax.broadcasted_iota(jnp.int32, (elems, PAD), 1)
    spot = lane // stride % 6
    inside = lane < NB
    for c in range(4):
        at = slice(c * PAD, (c + 1) * PAD)
        low = pltpu.roll(before[:, at], PAD - shift, 1)
        high = pltpu.roll(after[:, at], shift, 1)
        low = jnp.where((spot == 0) & inside, low, 0.0)
        high = jnp.where((spot == 5) & inside, high, 0.0)
        comps.append(parts[:, at] + (low + high))
    return jnp.concatenate(comps, 1)


def x_kernel(spot_ref, parts_ref, got_ref, turn_ref, out_ref, send_ref, back_ref):
    parts = parts_ref[...]
    width = EY * EZ
    before, after = take_faces(spot_ref, 0, got_ref[...], turn_ref[...])
    before = jnp.concatenate([before, parts[:-width]], 0)
    after = jnp.concatenate([parts[width:], after], 0)
    parts = face_add(parts, before, after, 180, 36)
    out_ref[...] = parts
    first = [parts[x * width : x * width + EZ] for x in range(EX)]
    last = [parts[(x + 1) * width - EZ : (x + 1) * width] for x in range(EX)]
    first, last = jnp.concatenate(first, 0), jnp.concatenate(last, 0)
    send_faces(spot_ref[1] % 2 == 0, first, last, send_ref, back_ref)


def y_kernel(spot_ref, parts_ref, got_ref, turn_ref, out_ref):
    parts = parts_ref[...]
    width = EY * EZ
    far_before, far_after = take_faces(spot_ref, 1, got_ref[...], turn_ref[...])
    before = []
    after = []
    for x in range(EX):
        base = x * width
        near = slice(x * EZ, (x + 1) * EZ)
        before += [far_before[near], parts[base : base + width - EZ]]
        after += [parts[base + EZ : base + width], far_after[near]]
    before = jnp.concatenate(before, 0)
    after = jnp.concatenate(after, 0)
    out_ref[...] = face_add(parts, before, after, 30, 6)


def z_kernel(spot_ref, parts_ref, before_ref, after_ref, out_ref):
    parts = parts_ref[...]
    elems = parts.shape[0]
    odd = lax.broadcasted_iota(jnp.int32, parts.shape, 0) % EZ == EZ - 1
    has_before = spot_ref[2] > 0
    has_after = spot_ref[2] < spot_ref[5] - 1
    far_before = jnp.where(has_before, pltpu.roll(before_ref[...], elems - 1, 0), 0.0)
    far_after = jnp.where(has_after, pltpu.roll(after_ref[...], 1, 0), 0.0)
    before = jnp.where(odd, pltpu.roll(parts, 1, 0), far_before)
    after = jnp.where(odd, far_after, pltpu.roll(parts, elems - 1, 0))
    parts = face_add(parts, before, after, 5, 1)
    mass = parts[:, 3 * PAD :]
    for c in range(3):
        accel = parts[:, c * PAD : c * PAD + NB] / mass[:, :NB]
        out_ref[:, c * NB : (c + 1) * NB] = accel


VM = pl.BlockSpec(memory_space=pltpu.VMEM)
SM = pl.BlockSpec(memory_space=pltpu.SMEM)


def call(kernel, shapes, specs, scratch=(), cost=None):
    return pl.pallas_call(
        kernel,
        out_shape=shapes,
        in_specs=specs,
        out_specs=jax.tree.map(lambda _: VM, shapes),
        scratch_shapes=scratch,
        cost_estimate=cost,
        compiler_params=pltpu.CompilerParams(vmem_limit_bytes=48 << 20),
    )


def partner(count, step):
    if count & (count - 1) == 0:
        return [(i, i ^ step) for i in range(count)]
    return [(i, (i + step) % count) for i in range(count)]


def slot_of(owner, me, count):
    if count & (count - 1) == 0:
        return owner ^ me
    return (me - owner) % count


def shape(dims, dtype=F32):
    return jax.ShapeDtypeStruct(dims, dtype)


def swap_faces(send, back, axis, count):
    near = [(i, i ^ 1) for i in range(count)]
    across = [(i, (i + 1) % count if i % 2 else (i - 1) % count) for i in range(count)]
    return lax.ppermute(send, axis, near), lax.ppermute(back, axis, across)


def per_device(src_fields, owner_peer, src_local, jac):
    n_x = lax.axis_size("gx")
    n_y = lax.axis_size("gy")
    n_z = lax.axis_size("gz")
    me = [lax.axis_index(axis) for axis in ("gx", "gy", "gz")]
    elems = src_fields.shape[0]
    width = src_fields.shape[1]
    capacity = max(2, 9 * elems // (n_x * n_y))
    slots = n_y * capacity
    column = [src_fields]
    for step in range(1, n_y):
        column.append(lax.ppermute(src_fields, "gy", partner(n_y, step)))
    owner = owner_peer[:, :, 0]
    slot = slot_of(owner // n_y, me[0], n_x) * n_y + slot_of(owner % n_y, me[1], n_y)
    index = slot * elems + src_local
    spot = jnp.stack(me + [jnp.int32(n_x), jnp.int32(n_y), jnp.int32(n_z)])
    ids, *masks = call(
        lambda *refs: index_kernel(n_y, capacity, *refs),
        (shape((1, n_y * elems + (n_x - 1) * slots), jnp.int32),)
        + (shape((8, n_y * elems)),) * (n_x - 1),
        [VM],
    )(index)
    asked = [
        lax.ppermute(mask, "gx", partner(n_x, step + 1)) for step, mask in enumerate(masks)
    ]
    fhigh, flow = force_table()
    high, low, lumped = call(
        prep_kernel,
        (shape((OVL, NB, QP), BF), shape((OVL, NB, QP), BF), shape((elems, NB))),
        [VM, VM],
        cost=pl.CostEstimate(flops=4_000_000_000, bytes_accessed=8_000_000, transcendentals=0),
    )(factor_rows(), jac)
    packed = call(
        lambda *refs: pack_kernel(n_y, capacity, n_x - 1, *refs),
        (shape((slots, CUT)), shape((slots, width - CUT))) * (n_x - 1),
        [VM] * (n_x - 1 + n_y),
    )(*asked, *column)
    arrived = []
    for part in range(2):
        for step in range(1, n_x):
            piece = packed[2 * (step - 1) + part]
            arrived.append(lax.ppermute(piece, "gx", partner(n_x, step)))
    early, late = arrived[: n_x - 1], arrived[n_x - 1 :]
    face = shape((EY * EZ, 4 * PAD))
    whole = shape((elems, 4 * PAD))
    lead, parts, send, back = call(
        lambda *refs: lead_kernel(n_y, n_x - 1, *refs),
        (shape((elems, 2 * NB)), whole, face, face),
        [SM] + [VM] * (8 + n_y + n_x - 1),
        [pltpu.VMEM((OVL * elems, CUT), F32)] * 2,
    )(spot, ids, index, jac, high, low, lumped, fhigh, flow, *column, *early)
    got, turn = swap_faces(send, back, "gx", n_x)
    fields = call(
        lambda *refs: tail_kernel(n_y, n_x - 1, *refs),
        shape((elems, width)),
        [VM] * (7 + n_y + 2 * (n_x - 1)),
        [pltpu.VMEM((OVL * elems, width - CUT + 128), F32)] * 2,
        cost=pl.CostEstimate(flops=4_000_000_000, bytes_accessed=8_000_000, transcendentals=0),
    )(
        ids, index, jac, high, low, lumped, lead, *column,
        *[piece for pair in zip(early, late) for piece in pair],
    )
    face = shape((EX * EZ, 4 * PAD))
    parts, send, back = call(x_kernel, (whole, face, face), [SM] + [VM] * 3)(
        spot, parts, got, turn
    )
    got, turn = swap_faces(send, back, "gy", n_y)
    got, turn, fields = lax.optimization_barrier((got, turn, fields))
    parts = call(y_kernel, whole, [SM] + [VM] * 3)(spot, parts, got, turn)
    if n_z == 2:
        before = after = lax.ppermute(parts, "gz", [(0, 1), (1, 0)])
    else:
        before = lax.ppermute(parts, "gz", [(i, i + 1) for i in range(n_z - 1)])
        after = lax.ppermute(parts, "gz", [(i + 1, i) for i in range(n_z - 1)])
    accel = call(z_kernel, shape((elems, 3 * NB)), [SM] + [VM] * 3)(spot, parts, before, after)
    return fields, accel


def solution(mesh):
    placed = (
        P(("gx", "gy", "gz"), None),
        P(("gx", "gy", "gz"), None, None),
        P(("gx", "gy", "gz"), None),
        P(("gx", "gy", "gz"), None),
    )
    return jax.shard_map(
        per_device,
        mesh=mesh,
        in_specs=placed,
        out_specs=(P(("gx", "gy", "gz"), None), P(("gx", "gy", "gz"), None)),
        check_vma=False,
    )
```

```python
import math

import jax
import jax.numpy as jnp
import numpy as np
from jax import lax
from jax.experimental import pallas as pl
from jax.experimental.pallas import tpu as pltpu
from jax.sharding import PartitionSpec as P

EX = 4
EY = 4
EZ = 2
FIELDS = 5
NB = 216
QP = 512
OVL = 8
PAD = 256
CUT = 512
BF = jnp.bfloat16
F32 = jnp.float32


def bern_table(points):
    cols = [math.comb(5, i) * points**i * (1.0 - points) ** (5 - i) for i in range(6)]
    return np.stack(cols, -1)


def three_way(table):
    parts = []
    rest = np.asarray(table, np.float32)
    for _ in range(3):
        part = rest.astype(jnp.bfloat16)
        parts.append(part)
        rest = rest - part.astype(np.float32)
    return parts


def factor_rows():
    mids = (np.arange(8) + 0.5) / 16.0
    point = np.arange(QP)
    out = []
    for stride in (64, 8, 1):
        for bit in range(2):
            points = bit * 0.5 + mids + 0.5 - bit
            rows = np.zeros((8, QP), np.float32)
            rows[:6] = bern_table(points).T[:, point // stride % 8]
            out.append(np.concatenate(three_way(rows) + [np.zeros((8, QP), jnp.bfloat16)], 0))
    return jnp.asarray(np.stack(out), BF)


def lower_integral(first, second):
    if first < 0 or first > 4:
        return 0.0
    return math.comb(4, first) * math.comb(5, second) / (10.0 * math.comb(9, first + second))


def force_table():
    mass_one = np.zeros((6, 6))
    grad_one = np.zeros((6, 6))
    for left in range(6):
        for right in range(6):
            mass_one[left, right] = (
                math.comb(5, left) * math.comb(5, right) / (11.0 * math.comb(10, left + right))
            )
            grad_one[left, right] = 5.0 * (
                lower_integral(left - 1, right) - lower_integral(left, right)
            )
    grad_x = np.kron(grad_one, np.kron(mass_one, mass_one))
    grad_y = np.kron(mass_one, np.kron(grad_one, mass_one))
    grad_z = np.kron(mass_one, np.kron(mass_one, grad_one))
    joined = np.zeros((NB, 3 * PAD), np.float32)
    for c, grad in enumerate((grad_x, grad_y, grad_z)):
        joined[:, c * PAD : c * PAD + NB] = grad.T * 8.0
    high, low, _ = three_way(joined)
    return jnp.asarray(high, BF), jnp.asarray(low, BF)


def split(value):
    high = value.astype(BF)
    return high, (value - high.astype(F32)).astype(BF)


def dot(a, b, dims=((1,), (0,))):
    return lax.dot_general(a, b, (dims, ((), ())), preferred_element_type=F32)


def dot3(a, b, dims=((1,), (0,))):
    return dot(a[0], b[0], dims) + (dot(a[0], b[1], dims) + dot(a[1], b[0], dims))


NT = ((1,), (1,))


def prep_kernel(rows_ref, high_ref, low_ref):
    coef = lax.broadcasted_iota(jnp.int32, (NB, 32), 0)
    col = lax.broadcasted_iota(jnp.int32, (NB, 32), 1)
    factors = []
    for d, stride in enumerate((36, 6, 1)):
        hit = (coef // stride % 6 == col % 8) & (col < 24)
        pick = jnp.where(hit, 1.0, 0.0).astype(BF)
        factors.append([dot(pick, rows_ref[2 * d + bit]) for bit in range(2)])
    for k in range(OVL):
        table = factors[0][k >> 2 & 1] * factors[1][k >> 1 & 1] * factors[2][k & 1]
        high, low = split(table)
        high_ref[k] = high
        low_ref[k] = low


def hits(index_ref, wanted, spans):
    elems = index_ref.shape[0]
    out = []
    for k in spans:
        column = jnp.broadcast_to(index_ref[:, k : k + 1], (elems, wanted.shape[1]))
        out.append(jnp.where(column == wanted, 1.0, 0.0))
    return out


def packing(mask, capacity, elems, owners):
    width = owners * elems
    row = lax.broadcasted_iota(jnp.int32, (width, width), 0)
    col = lax.broadcasted_iota(jnp.int32, (width, width), 1)
    earlier = jnp.where((row // elems == col // elems) & (row < col), 1.0, 0.0).astype(BF)
    rank = dot(jnp.broadcast_to(mask, (8, width)).astype(BF), earlier)[:1]
    slots = owners * capacity
    spot = lax.broadcasted_iota(jnp.int32, (slots, width), 0)
    lane = lax.broadcasted_iota(jnp.int32, (slots, width), 1)
    wanted = (lane // elems * capacity).astype(F32) + rank
    hit = (spot.astype(F32) == wanted) & (jnp.broadcast_to(mask, (slots, width)) > 0.5)
    return jnp.where(hit, 1.0, 0.0).astype(BF)


def index_kernel(owners, capacity, index_ref, ids_ref, *mask_refs):
    elems = index_ref.shape[0]
    width = owners * elems
    lane = lax.broadcasted_iota(jnp.int32, (elems, (1 + len(mask_refs)) * width), 1)
    named = sum(hits(index_ref, lane, range(OVL)))
    named = jnp.sum(named, 0, keepdims=True)
    mask = jnp.where(named > 0.5, 1.0, 0.0)
    ids_ref[:, :width] = lane[:1, :width]
    local = lax.broadcasted_iota(jnp.int32, (8, width), 1) + 1
    slots = owners * capacity
    for s, mask_ref in enumerate(mask_refs):
        part = mask[:, (s + 1) * width : (s + 2) * width]
        mask_ref[...] = jnp.broadcast_to(part, mask_ref.shape)
        order = packing(part, capacity, elems, owners)
        ids = dot(local.astype(F32).astype(BF), order, NT)[:1].astype(jnp.int32)
        ids = jnp.where(ids > 0, ids + ((s + 1) * width - 1), -1)
        ids_ref[:, width + s * slots : width + (s + 1) * slots] = ids


def fetch(pairs, sems):
    copies = [
        pltpu.make_async_copy(source, target, sems.at[n]) for n, (source, target) in enumerate(pairs)
    ]
    for copy in copies:
        copy.start()
    return copies


def finish(copies):
    for copy in copies:
        copy.wait()


def pack_kernel(owners, capacity, count, *refs):
    masks = refs[:count]
    column = refs[count : count + owners]
    outs = refs[count + owners : 3 * count + owners]
    rows_ref, mask_ref, sems = refs[3 * count + owners :]
    elems = column[0].shape[0]
    pairs = [(ref, mask_ref.at[s]) for s, ref in enumerate(masks)]
    pairs += [(ref, rows_ref.at[n * elems : (n + 1) * elems]) for n, ref in enumerate(column)]
    copies = fetch(pairs, sems)
    finish(copies[:count])
    order = jnp.concatenate(
        [packing(mask_ref[s][:1], capacity, elems, owners) for s in range(count)], 0
    )
    finish(copies[count:])
    rows = rows_ref[...]
    high = rows.astype(BF)
    rest = rows - high.astype(F32)
    middle, low = split(rest)
    packed = (dot(order, high) + dot(order, middle)) + dot(order, low)
    slots = owners * capacity
    for s in range(count):
        part = packed[s * slots : (s + 1) * slots]
        outs[2 * s][...] = part[:, :CUT]
        outs[2 * s + 1][...] = part[:, CUT:]


def pick(hot, rows, outs):
    high, low = split(rows)
    outs[0][...] = dot(hot, high)
    outs[1][...] = dot(hot, low)


def project(spans, offset, picked, jac_ref, high_ref, low_ref, ready, extra):
    elems = jac_ref.shape[0]
    count = (picked[0].shape[1] - offset) // NB
    size = count * elems
    total = None

    def apply(pair, table, dims=((1,), (0,))):
        size = pair[0].shape[0]
        both = dot(jnp.concatenate(pair, 0), high_ref[table], dims)
        return both[:size] + (both[size:] + dot(pair[0], low_ref[table], dims))

    for n, k in enumerate(spans):
        at = slice(n * elems, (n + 1) * elems)
        source = tuple(
            jnp.concatenate(
                [ref[at, offset + f * NB : offset + (f + 1) * NB] for f in range(count)], 0
            ).astype(BF)
            for ref in picked
        )
        ready(k)
        values = apply(source, k)
        weights = jac_ref[:, k * QP : (k + 1) * QP]
        scaled = values * jnp.concatenate([weights] * count, 0)
        if extra:
            scaled = jnp.concatenate([scaled, weights], 0)
        ready(7 - k)
        part = apply(split(scaled), 7 - k, NT)
        total = part if total is None else total + part
    return total


def send_faces(even, first, last, send_ref, back_ref):
    send_ref[...] = jnp.where(even, last, first)
    back_ref[...] = jnp.where(even, first, last)


def take_faces(axis, got, back):
    me, count = lax.axis_index(axis), lax.axis_size(axis)
    even = me % 2 == 0
    before = jnp.where(even, back, got)
    after = jnp.where(even, got, back)
    return jnp.where(me > 0, before, 0.0), jnp.where(me < count - 1, after, 0.0)


def once(copies):
    waited = set()

    def ready(n):
        if n not in waited:
            waited.add(n)
            finish(copies[n])

    return ready


def lead_kernel(owners, count, *refs):
    ids, index, jac, high, low, fhigh, flow = refs[:7]
    column = refs[7 : 7 + owners]
    packed = refs[7 + owners : 7 + owners + count]
    refs = refs[7 + owners + count :]
    fields_ref, lumped_ref, parts_ref, send_ref, back_ref = refs[:5]
    ids_ref, index_ref, jac_ref, high_ref, low_ref, fhigh_ref, flow_ref, rows_ref = refs[5:13]
    picked = refs[13:15]
    sems = refs[15]
    elems = jac_ref.shape[0]
    slots = packed[0].shape[0]
    pairs = [(ids, ids_ref), (index, index_ref)]
    base = 0
    for ref in column:
        pairs.append((ref.at[:, :CUT], rows_ref.at[base : base + elems]))
        base += elems
    for ref in packed:
        pairs.append((ref, rows_ref.at[base : base + slots]))
        base += slots
    gathered = len(pairs)
    pairs += [(jac, jac_ref), (fhigh, fhigh_ref), (flow, flow_ref)]
    for k in range(OVL):
        for ref, target in ((high, high_ref), (low, low_ref)):
            pairs.append((ref.at[k], target.at[k]))
    copies = fetch(pairs, sems)
    tables = copies[gathered + 3 :]
    finish(copies[:2])
    hot = jnp.concatenate(hits(index_ref, ids_ref[...], range(OVL)), 0).astype(BF)
    finish(copies[2:gathered])
    pick(hot, rows_ref[...], picked)
    finish(copies[gathered : gathered + 3])
    ready = once([tables[2 * k : 2 * k + 2] for k in range(OVL)])
    total = project(range(OVL), 0, picked, jac_ref, high_ref, low_ref, ready, True)
    lumped = total[2 * elems :]
    lumped_ref[...] = lumped
    fields = [total[f * elems : (f + 1) * elems] / lumped for f in range(2)]
    for f in range(2):
        fields_ref[:, f * NB : (f + 1) * NB] = fields[f]
    pressure = fields[0] * fields[1]
    force = dot3(split(pressure), (fhigh_ref[...], flow_ref[...]))
    mass = jnp.concatenate([lumped * (1.0 / 4096.0), jnp.zeros((elems, PAD - NB), F32)], 1)
    parts = jnp.concatenate([force, mass], 1)
    parts_ref[...] = parts
    width = EY * EZ
    even = lax.axis_index("gx") % 2 == 0
    send_faces(even, parts[:width], parts[-width:], send_ref, back_ref)


def tail_kernel(owners, count, half, *refs):
    ids, index, jac, high, low = refs[:5]
    column = refs[5 : 5 + owners]
    packed = refs[5 + owners : 5 + owners + 2 * count]
    refs = refs[5 + owners + 2 * count :]
    if half:
        sum_in, lumped_in, lead_in = refs[:3]
        refs = refs[3:]
    out_ref = refs[0]
    ids_ref, index_ref, jac_ref, high_ref, low_ref, rows_ref, picked_high, picked_low = refs[1:9]
    sems = refs[9]
    elems = jac_ref.shape[0]
    slots = packed[0].shape[0]
    start = CUT - 128
    spans = range(OVL // 2 * half, OVL // 2 * (half + 1))
    pairs = [(ids, ids_ref), (index, index_ref)]
    base = 0
    for ref in column:
        pairs.append((ref.at[:, start:], rows_ref.at[base : base + elems]))
        base += elems
    for s in range(count):
        near, far = packed[2 * s : 2 * s + 2]
        pairs.append((near.at[:, start:], rows_ref.at[base : base + slots, :128]))
        pairs.append((far, rows_ref.at[base : base + slots, 128:]))
        base += slots
    gathered = len(pairs)
    pairs.append((jac, jac_ref))
    if half:
        sum_ref, lumped_ref, lead_ref = refs[10:]
        pairs += [(sum_in, sum_ref), (lumped_in, lumped_ref), (lead_in, lead_ref)]
    more = len(pairs)
    for k in range(OVL):
        for ref, target in ((high, high_ref), (low, low_ref)):
            pairs.append((ref.at[k], target.at[k]))
    copies = fetch(pairs, sems)
    finish(copies[:2])
    hot = jnp.concatenate(hits(index_ref, ids_ref[...], spans), 0).astype(BF)
    finish(copies[2:gathered])
    picked = (picked_high, picked_low)
    pick(hot, rows_ref[...], picked)
    finish(copies[gathered:more])
    tables = copies[more:]
    ready = once([tables[2 * k : 2 * k + 2] for k in range(OVL)])
    total = project(spans, 2 * NB - start, picked, jac_ref, high_ref, low_ref, ready, False)
    if half == 0:
        out_ref[...] = total
        return
    total = total + sum_ref[...]
    lumped = lumped_ref[...]
    out_ref[:, : 2 * NB] = lead_ref[...]
    for f in range(3):
        out_ref[:, (f + 2) * NB : (f + 3) * NB] = total[f * elems : (f + 1) * elems] / lumped


def face_add(parts, before, after, shift, stride):
    comps = []
    elems = parts.shape[0]
    lane = lax.broadcasted_iota(jnp.int32, (elems, PAD), 1)
    spot = lane // stride % 6
    inside = lane < NB
    for c in range(4):
        at = slice(c * PAD, (c + 1) * PAD)
        low = pltpu.roll(before[:, at], PAD - shift, 1)
        high = pltpu.roll(after[:, at], shift, 1)
        low = jnp.where((spot == 0) & inside, low, 0.0)
        high = jnp.where((spot == 5) & inside, high, 0.0)
        comps.append(parts[:, at] + (low + high))
    return jnp.concatenate(comps, 1)


def x_kernel(parts_ref, got_ref, turn_ref, out_ref, send_ref, back_ref):
    parts = parts_ref[...]
    width = EY * EZ
    before, after = take_faces("gx", got_ref[...], turn_ref[...])
    before = jnp.concatenate([before, parts[:-width]], 0)
    after = jnp.concatenate([parts[width:], after], 0)
    parts = face_add(parts, before, after, 180, 36)
    out_ref[...] = parts
    first = [parts[x * width : x * width + EZ] for x in range(EX)]
    last = [parts[(x + 1) * width - EZ : (x + 1) * width] for x in range(EX)]
    first, last = jnp.concatenate(first, 0), jnp.concatenate(last, 0)
    send_faces(lax.axis_index("gy") % 2 == 0, first, last, send_ref, back_ref)


def y_kernel(parts_ref, got_ref, turn_ref, out_ref):
    parts = parts_ref[...]
    width = EY * EZ
    far_before, far_after = take_faces("gy", got_ref[...], turn_ref[...])
    before = []
    after = []
    for x in range(EX):
        base = x * width
        near = slice(x * EZ, (x + 1) * EZ)
        before += [far_before[near], parts[base : base + width - EZ]]
        after += [parts[base + EZ : base + width], far_after[near]]
    before = jnp.concatenate(before, 0)
    after = jnp.concatenate(after, 0)
    out_ref[...] = face_add(parts, before, after, 30, 6)


def z_kernel(parts_ref, before_ref, after_ref, out_ref):
    parts = parts_ref[...]
    elems = parts.shape[0]
    odd = lax.broadcasted_iota(jnp.int32, parts.shape, 0) % EZ == EZ - 1
    has_before = lax.axis_index("gz") > 0
    has_after = lax.axis_index("gz") < lax.axis_size("gz") - 1
    far_before = jnp.where(has_before, pltpu.roll(before_ref[...], elems - 1, 0), 0.0)
    far_after = jnp.where(has_after, pltpu.roll(after_ref[...], 1, 0), 0.0)
    before = jnp.where(odd, pltpu.roll(parts, 1, 0), far_before)
    after = jnp.where(odd, far_after, pltpu.roll(parts, elems - 1, 0))
    parts = face_add(parts, before, after, 5, 1)
    mass = parts[:, 3 * PAD :]
    for c in range(3):
        accel = parts[:, c * PAD : c * PAD + NB] / mass[:, :NB]
        out_ref[:, c * NB : (c + 1) * NB] = accel


VM = pl.BlockSpec(memory_space=pltpu.VMEM)
HB = pl.BlockSpec(memory_space=pl.ANY)


def call(kernel, shapes, specs, scratch=(), cost=None):
    return pl.pallas_call(
        kernel,
        out_shape=shapes,
        in_specs=specs,
        out_specs=jax.tree.map(lambda _: VM, shapes),
        scratch_shapes=scratch,
        cost_estimate=cost,
        compiler_params=pltpu.CompilerParams(vmem_limit_bytes=56 << 20),
    )


def partner(count, step):
    if count & (count - 1) == 0:
        return [(i, i ^ step) for i in range(count)]
    return [(i, (i + step) % count) for i in range(count)]


def slot_of(owner, me, count):
    if count & (count - 1) == 0:
        return owner ^ me
    return (me - owner) % count


def shape(dims, dtype=F32):
    return jax.ShapeDtypeStruct(dims, dtype)


def swap_faces(send, back, axis, count):
    near = [(i, i ^ 1) for i in range(count)]
    across = [(i, (i + 1) % count if i % 2 else (i - 1) % count) for i in range(count)]
    return lax.ppermute(send, axis, near), lax.ppermute(back, axis, across)


def per_device(src_fields, owner_peer, src_local, jac):
    n_x = lax.axis_size("gx")
    n_y = lax.axis_size("gy")
    n_z = lax.axis_size("gz")
    me = [lax.axis_index(axis) for axis in ("gx", "gy", "gz")]
    elems = src_fields.shape[0]
    width = src_fields.shape[1]
    capacity = max(2, 9 * elems // (n_x * n_y))
    slots = n_y * capacity
    column = [src_fields]
    for step in range(1, n_y):
        column.append(lax.ppermute(src_fields, "gy", partner(n_y, step)))
    owner = owner_peer[:, :, 0]
    slot = slot_of(owner // n_y, me[0], n_x) * n_y + slot_of(owner % n_y, me[1], n_y)
    index = slot * elems + src_local
    total = n_y * elems + (n_x - 1) * slots
    ids, *masks = call(
        lambda *refs: index_kernel(n_y, capacity, *refs),
        (shape((1, total), jnp.int32),) + (shape((8, n_y * elems)),) * (n_x - 1),
        [VM],
    )(index)
    asked = [
        lax.ppermute(mask, "gx", partner(n_x, step + 1)) for step, mask in enumerate(masks)
    ]
    fhigh, flow = force_table()
    table = shape((OVL, NB, QP), BF)
    heavy = pl.CostEstimate(flops=2_000_000_000, bytes_accessed=8_000_000, transcendentals=0)
    high, low = call(prep_kernel, (table, table), [VM], cost=heavy)(factor_rows())
    asked, high, low = lax.optimization_barrier((asked, high, low))
    packed = call(
        lambda *refs: pack_kernel(n_y, capacity, n_x - 1, *refs),
        (shape((slots, CUT)), shape((slots, width - CUT))) * (n_x - 1),
        [HB] * (n_x - 1 + n_y),
        [
            pltpu.VMEM((n_y * elems, width), F32),
            pltpu.VMEM((n_x - 1, 8, n_y * elems), F32),
            pltpu.SemaphoreType.DMA((n_x - 1 + n_y,)),
        ],
    )(*asked, *column)
    arrived = []
    for part in range(2):
        for step in range(1, n_x):
            piece = packed[2 * (step - 1) + part]
            arrived.append(lax.ppermute(piece, "gx", partner(n_x, step)))
    early, late = arrived[: n_x - 1], arrived[n_x - 1 :]
    face = shape((EY * EZ, 4 * PAD))
    whole = shape((elems, 4 * PAD))
    scratch = [
        pltpu.VMEM((1, total), jnp.int32),
        pltpu.VMEM(index.shape, jnp.int32),
        pltpu.VMEM(jac.shape, F32),
        pltpu.VMEM(table.shape, BF),
        pltpu.VMEM(table.shape, BF),
    ]
    lead, lumped, parts, send, back = call(
        lambda *refs: lead_kernel(n_y, n_x - 1, *refs),
        (shape((elems, 2 * NB)), shape((elems, NB)), whole, face, face),
        [HB] * (7 + n_y + n_x - 1),
        scratch
        + [
            pltpu.VMEM(fhigh.shape, BF),
            pltpu.VMEM(flow.shape, BF),
            pltpu.VMEM((total, CUT), F32),
            pltpu.VMEM((OVL * elems, CUT), F32),
            pltpu.VMEM((OVL * elems, CUT), F32),
            pltpu.SemaphoreType.DMA((5 + 2 * OVL + n_y + n_x - 1,)),
        ],
    )(ids, index, jac, high, low, fhigh, flow, *column, *early)
    got, turn = swap_faces(send, back, "gx", n_x)
    pieces = (*column, *[piece for pair in zip(early, late) for piece in pair])
    wide = width - CUT + 128
    tails = scratch + [
        pltpu.VMEM((total, wide), F32),
        pltpu.VMEM((OVL // 2 * elems, wide), F32),
        pltpu.VMEM((OVL // 2 * elems, wide), F32),
        pltpu.SemaphoreType.DMA((6 + 2 * OVL + n_y + 2 * (n_x - 1),)),
    ]
    rest = FIELDS - 2
    partial = call(
        lambda *refs: tail_kernel(n_y, n_x - 1, 0, *refs),
        shape((rest * elems, NB)),
        [HB] * (5 + len(pieces)),
        tails,
        heavy,
    )(ids, index, jac, high, low, *pieces)
    got, turn, partial = lax.optimization_barrier((got, turn, partial))
    face = shape((EX * EZ, 4 * PAD))
    parts, send, back = call(x_kernel, (whole, face, face), [VM] * 3)(parts, got, turn)
    got, turn = swap_faces(send, back, "gy", n_y)
    fields = call(
        lambda *refs: tail_kernel(n_y, n_x - 1, 1, *refs),
        shape((elems, width)),
        [HB] * (8 + len(pieces)),
        tails
        + [
            pltpu.VMEM((rest * elems, NB), F32),
            pltpu.VMEM((elems, NB), F32),
            pltpu.VMEM((elems, 2 * NB), F32),
        ],
        heavy,
    )(ids, index, jac, high, low, *pieces, partial, lumped, lead)
    got, turn, fields = lax.optimization_barrier((got, turn, fields))
    parts = call(y_kernel, whole, [VM] * 3)(parts, got, turn)
    if n_z == 2:
        before = after = lax.ppermute(parts, "gz", [(0, 1), (1, 0)])
    else:
        before = lax.ppermute(parts, "gz", [(i, i + 1) for i in range(n_z - 1)])
        after = lax.ppermute(parts, "gz", [(i + 1, i) for i in range(n_z - 1)])
    accel = call(z_kernel, shape((elems, 3 * NB)), [VM] * 3)(parts, before, after)
    return fields, accel


def solution(mesh):
    placed = (
        P(("gx", "gy", "gz"), None),
        P(("gx", "gy", "gz"), None, None),
        P(("gx", "gy", "gz"), None),
        P(("gx", "gy", "gz"), None),
    )
    return jax.shard_map(
        per_device,
        mesh=mesh,
        in_specs=placed,
        out_specs=(P(("gx", "gy", "gz"), None), P(("gx", "gy", "gz"), None)),
        check_vma=False,
    )
```

```python
import math

import jax
import jax.numpy as jnp
import numpy as np
from jax import lax
from jax.experimental import pallas as pl
from jax.experimental.pallas import tpu as pltpu
from jax.sharding import PartitionSpec as P

EX = 4
EY = 4
EZ = 2
FIELDS = 5
NB = 216
QP = 512
OVL = 8
PAD = 256
CUT = 512
BF = jnp.bfloat16
F32 = jnp.float32


def bern_table(points):
    cols = [math.comb(5, i) * points**i * (1.0 - points) ** (5 - i) for i in range(6)]
    return np.stack(cols, -1)


def three_way(table):
    parts = []
    rest = np.asarray(table, np.float32)
    for _ in range(3):
        part = rest.astype(jnp.bfloat16)
        parts.append(part)
        rest = rest - part.astype(np.float32)
    return parts


def factor_rows():
    mids = (np.arange(8) + 0.5) / 16.0
    point = np.arange(QP)
    out = []
    for stride in (64, 8, 1):
        for bit in range(2):
            points = bit * 0.5 + mids + 0.5 - bit
            rows = np.zeros((8, QP), np.float32)
            rows[:6] = bern_table(points).T[:, point // stride % 8]
            out.append(np.concatenate(three_way(rows) + [np.zeros((8, QP), jnp.bfloat16)], 0))
    return jnp.asarray(np.stack(out), BF)


def lower_integral(first, second):
    if first < 0 or first > 4:
        return 0.0
    return math.comb(4, first) * math.comb(5, second) / (10.0 * math.comb(9, first + second))


def force_table():
    mass_one = np.zeros((6, 6))
    grad_one = np.zeros((6, 6))
    for left in range(6):
        for right in range(6):
            mass_one[left, right] = (
                math.comb(5, left) * math.comb(5, right) / (11.0 * math.comb(10, left + right))
            )
            grad_one[left, right] = 5.0 * (
                lower_integral(left - 1, right) - lower_integral(left, right)
            )
    grad_x = np.kron(grad_one, np.kron(mass_one, mass_one))
    grad_y = np.kron(mass_one, np.kron(grad_one, mass_one))
    grad_z = np.kron(mass_one, np.kron(mass_one, grad_one))
    joined = np.zeros((NB, 3 * PAD), np.float32)
    for c, grad in enumerate((grad_x, grad_y, grad_z)):
        joined[:, c * PAD : c * PAD + NB] = grad.T * 8.0
    high, low, _ = three_way(joined)
    return jnp.asarray(high, BF), jnp.asarray(low, BF)


def split(value):
    high = value.astype(BF)
    return high, (value - high.astype(F32)).astype(BF)


def dot(a, b, dims=((1,), (0,))):
    return lax.dot_general(a, b, (dims, ((), ())), preferred_element_type=F32)


def dot3(a, b, dims=((1,), (0,))):
    return dot(a[0], b[0], dims) + (dot(a[0], b[1], dims) + dot(a[1], b[0], dims))


NT = ((1,), (1,))


def prep_kernel(rows_ref, high_ref, low_ref):
    coef = lax.broadcasted_iota(jnp.int32, (NB, 32), 0)
    col = lax.broadcasted_iota(jnp.int32, (NB, 32), 1)
    factors = []
    for d, stride in enumerate((36, 6, 1)):
        hit = (coef // stride % 6 == col % 8) & (col < 24)
        pick = jnp.where(hit, 1.0, 0.0).astype(BF)
        factors.append([dot(pick, rows_ref[2 * d + bit]) for bit in range(2)])
    for k in range(OVL):
        table = factors[0][k >> 2 & 1] * factors[1][k >> 1 & 1] * factors[2][k & 1]
        high, low = split(table)
        high_ref[k] = high
        low_ref[k] = low


def hits(index_ref, wanted, spans):
    elems = index_ref.shape[0]
    out = []
    for k in spans:
        column = jnp.broadcast_to(index_ref[:, k : k + 1], (elems, wanted.shape[1]))
        out.append(jnp.where(column == wanted, 1.0, 0.0))
    return out


def packing(mask, capacity, elems, owners):
    width = owners * elems
    row = lax.broadcasted_iota(jnp.int32, (width, width), 0)
    col = lax.broadcasted_iota(jnp.int32, (width, width), 1)
    earlier = jnp.where((row // elems == col // elems) & (row < col), 1.0, 0.0).astype(BF)
    rank = dot(jnp.broadcast_to(mask, (8, width)).astype(BF), earlier)[:1]
    slots = owners * capacity
    spot = lax.broadcasted_iota(jnp.int32, (slots, width), 0)
    lane = lax.broadcasted_iota(jnp.int32, (slots, width), 1)
    wanted = (lane // elems * capacity).astype(F32) + rank
    hit = (spot.astype(F32) == wanted) & (jnp.broadcast_to(mask, (slots, width)) > 0.5)
    return jnp.where(hit, 1.0, 0.0).astype(BF)


def index_kernel(owners, capacity, index_ref, ids_ref, *mask_refs):
    elems = index_ref.shape[0]
    width = owners * elems
    lane = lax.broadcasted_iota(jnp.int32, (elems, (1 + len(mask_refs)) * width), 1)
    named = sum(hits(index_ref, lane, range(OVL)))
    named = jnp.sum(named, 0, keepdims=True)
    mask = jnp.where(named > 0.5, 1.0, 0.0)
    ids_ref[:, :width] = lane[:1, :width]
    local = lax.broadcasted_iota(jnp.int32, (8, width), 1) + 1
    slots = owners * capacity
    for s, mask_ref in enumerate(mask_refs):
        part = mask[:, (s + 1) * width : (s + 2) * width]
        mask_ref[...] = jnp.broadcast_to(part, mask_ref.shape)
        order = packing(part, capacity, elems, owners)
        ids = dot(local.astype(F32).astype(BF), order, NT)[:1].astype(jnp.int32)
        ids = jnp.where(ids > 0, ids + ((s + 1) * width - 1), -1)
        ids_ref[:, width + s * slots : width + (s + 1) * slots] = ids


def pack_kernel(owners, capacity, count, *refs):
    masks = refs[:count]
    column = refs[count : count + owners]
    outs = refs[count + owners :]
    elems = column[0].shape[0]
    order = jnp.concatenate(
        [packing(mask[:1], capacity, elems, owners) for mask in masks], 0
    )
    rows = jnp.concatenate([ref[...] for ref in column], 0)
    high = rows.astype(BF)
    rest = rows - high.astype(F32)
    middle, low = split(rest)
    packed = (dot(order, high) + dot(order, middle)) + dot(order, low)
    slots = owners * capacity
    for s in range(count):
        part = packed[s * slots : (s + 1) * slots]
        outs[2 * s][...] = part[:, :CUT]
        outs[2 * s + 1][...] = part[:, CUT:]


def pick(hot, rows, outs):
    high, low = split(rows)
    outs[0][...] = dot(hot, high)
    outs[1][...] = dot(hot, low)


def project(spans, offset, picked, jac_ref, high_ref, low_ref, extra):
    elems = jac_ref.shape[0]
    count = (picked[0].shape[1] - offset) // NB
    total = None

    def apply(pair, table, dims=((1,), (0,))):
        size = pair[0].shape[0]
        both = dot(jnp.concatenate(pair, 0), high_ref[table], dims)
        return both[:size] + (both[size:] + dot(pair[0], low_ref[table], dims))

    for n, k in enumerate(spans):
        at = slice(n * elems, (n + 1) * elems)
        source = tuple(
            jnp.concatenate(
                [ref[at, offset + f * NB : offset + (f + 1) * NB] for f in range(count)], 0
            ).astype(BF)
            for ref in picked
        )
        values = apply(source, k)
        weights = jac_ref[:, k * QP : (k + 1) * QP]
        scaled = values * jnp.concatenate([weights] * count, 0)
        if extra:
            scaled = jnp.concatenate([scaled, weights], 0)
        part = apply(split(scaled), 7 - k, NT)
        total = part if total is None else total + part
    return total


def send_faces(even, first, last, send_ref, back_ref):
    send_ref[...] = jnp.where(even, last, first)
    back_ref[...] = jnp.where(even, first, last)


def take_faces(axis, got, back):
    me, count = lax.axis_index(axis), lax.axis_size(axis)
    even = me % 2 == 0
    before = jnp.where(even, back, got)
    after = jnp.where(even, got, back)
    return jnp.where(me > 0, before, 0.0), jnp.where(me < count - 1, after, 0.0)


def lead_kernel(owners, count, ids_ref, index_ref, jac_ref, high_ref, low_ref, fhigh_ref, flow_ref, *refs):
    column = refs[:owners]
    packed = refs[owners : owners + count]
    refs = refs[owners + count :]
    fields_ref, lumped_ref, parts_ref, send_ref, back_ref, *picked = refs
    elems = jac_ref.shape[0]
    hot = jnp.concatenate(hits(index_ref, ids_ref[...], range(OVL)), 0).astype(BF)
    rows = [ref[:, :CUT] for ref in column] + [ref[...] for ref in packed]
    pick(hot, jnp.concatenate(rows, 0), picked)
    total = project(range(OVL), 0, picked, jac_ref, high_ref, low_ref, True)
    lumped = total[2 * elems :]
    lumped_ref[...] = lumped
    fields = [total[f * elems : (f + 1) * elems] / lumped for f in range(2)]
    for f in range(2):
        fields_ref[:, f * NB : (f + 1) * NB] = fields[f]
    pressure = fields[0] * fields[1]
    force = dot3(split(pressure), (fhigh_ref[...], flow_ref[...]))
    mass = jnp.concatenate([lumped * (1.0 / 4096.0), jnp.zeros((elems, PAD - NB), F32)], 1)
    parts = jnp.concatenate([force, mass], 1)
    parts_ref[...] = parts
    width = EY * EZ
    even = lax.axis_index("gx") % 2 == 0
    send_faces(even, parts[:width], parts[-width:], send_ref, back_ref)


def tail_kernel(owners, count, half, ids_ref, index_ref, jac_ref, high_ref, low_ref, *refs):
    column = refs[:owners]
    packed = refs[owners : owners + 2 * count]
    refs = refs[owners + 2 * count :]
    if half:
        sum_ref, lumped_ref, lead_ref, *refs = refs
    out_ref, *picked = refs
    elems = jac_ref.shape[0]
    start = CUT - 128
    spans = range(OVL // 2 * half, OVL // 2 * (half + 1))
    hot = jnp.concatenate(hits(index_ref, ids_ref[...], spans), 0).astype(BF)
    rows = [ref[:, start:] for ref in column]
    for s in range(count):
        near, far = packed[2 * s : 2 * s + 2]
        rows.append(jnp.concatenate([near[:, start:], far[...]], 1))
    pick(hot, jnp.concatenate(rows, 0), picked)
    total = project(spans, 2 * NB - start, picked, jac_ref, high_ref, low_ref, False)
    if half == 0:
        out_ref[...] = total
        return
    total = total + sum_ref[...]
    lumped = lumped_ref[...]
    out_ref[:, : 2 * NB] = lead_ref[...]
    for f in range(3):
        out_ref[:, (f + 2) * NB : (f + 3) * NB] = total[f * elems : (f + 1) * elems] / lumped


def face_add(parts, before, after, shift, stride):
    comps = []
    elems = parts.shape[0]
    lane = lax.broadcasted_iota(jnp.int32, (elems, PAD), 1)
    spot = lane // stride % 6
    inside = lane < NB
    for c in range(4):
        at = slice(c * PAD, (c + 1) * PAD)
        low = pltpu.roll(before[:, at], PAD - shift, 1)
        high = pltpu.roll(after[:, at], shift, 1)
        low = jnp.where((spot == 0) & inside, low, 0.0)
        high = jnp.where((spot == 5) & inside, high, 0.0)
        comps.append(parts[:, at] + (low + high))
    return jnp.concatenate(comps, 1)


def x_kernel(parts_ref, got_ref, turn_ref, out_ref, send_ref, back_ref):
    parts = parts_ref[...]
    width = EY * EZ
    before, after = take_faces("gx", got_ref[...], turn_ref[...])
    before = jnp.concatenate([before, parts[:-width]], 0)
    after = jnp.concatenate([parts[width:], after], 0)
    parts = face_add(parts, before, after, 180, 36)
    out_ref[...] = parts
    first = [parts[x * width : x * width + EZ] for x in range(EX)]
    last = [parts[(x + 1) * width - EZ : (x + 1) * width] for x in range(EX)]
    first, last = jnp.concatenate(first, 0), jnp.concatenate(last, 0)
    send_faces(lax.axis_index("gy") % 2 == 0, first, last, send_ref, back_ref)


def y_kernel(parts_ref, got_ref, turn_ref, out_ref):
    parts = parts_ref[...]
    width = EY * EZ
    far_before, far_after = take_faces("gy", got_ref[...], turn_ref[...])
    before = []
    after = []
    for x in range(EX):
        base = x * width
        near = slice(x * EZ, (x + 1) * EZ)
        before += [far_before[near], parts[base : base + width - EZ]]
        after += [parts[base + EZ : base + width], far_after[near]]
    before = jnp.concatenate(before, 0)
    after = jnp.concatenate(after, 0)
    out_ref[...] = face_add(parts, before, after, 30, 6)


def z_kernel(parts_ref, before_ref, after_ref, out_ref):
    parts = parts_ref[...]
    elems = parts.shape[0]
    odd = lax.broadcasted_iota(jnp.int32, parts.shape, 0) % EZ == EZ - 1
    has_before = lax.axis_index("gz") > 0
    has_after = lax.axis_index("gz") < lax.axis_size("gz") - 1
    far_before = jnp.where(has_before, pltpu.roll(before_ref[...], elems - 1, 0), 0.0)
    far_after = jnp.where(has_after, pltpu.roll(after_ref[...], 1, 0), 0.0)
    before = jnp.where(odd, pltpu.roll(parts, 1, 0), far_before)
    after = jnp.where(odd, far_after, pltpu.roll(parts, elems - 1, 0))
    parts = face_add(parts, before, after, 5, 1)
    mass = parts[:, 3 * PAD :]
    for c in range(3):
        accel = parts[:, c * PAD : c * PAD + NB] / mass[:, :NB]
        out_ref[:, c * NB : (c + 1) * NB] = accel


VM = pl.BlockSpec(memory_space=pltpu.VMEM)


def call(kernel, shapes, specs, scratch=(), cost=None):
    return pl.pallas_call(
        kernel,
        out_shape=shapes,
        in_specs=specs,
        out_specs=jax.tree.map(lambda _: VM, shapes),
        scratch_shapes=scratch,
        cost_estimate=cost,
        compiler_params=pltpu.CompilerParams(vmem_limit_bytes=16 << 20),
    )


def partner(count, step):
    if count & (count - 1) == 0:
        return [(i, i ^ step) for i in range(count)]
    return [(i, (i + step) % count) for i in range(count)]


def slot_of(owner, me, count):
    if count & (count - 1) == 0:
        return owner ^ me
    return (me - owner) % count


def shape(dims, dtype=F32):
    return jax.ShapeDtypeStruct(dims, dtype)


def swap_faces(piece, back, axis, count):
    near = [(i, i ^ 1) for i in range(count)]
    across = [(i, (i + 1) % count if i % 2 else (i - 1) % count) for i in range(count)]
    return lax.ppermute(piece, axis, near), lax.ppermute(back, axis, across)


def per_device(src_fields, owner_peer, src_local, jac):
    n_x = lax.axis_size("gx")
    n_y = lax.axis_size("gy")
    n_z = lax.axis_size("gz")
    me = [lax.axis_index(axis) for axis in ("gx", "gy")]
    elems = src_fields.shape[0]
    width = src_fields.shape[1]
    capacity = max(2, 9 * elems // (n_x * n_y))
    slots = n_y * capacity
    column = [src_fields]
    for step in range(1, n_y):
        column.append(lax.ppermute(src_fields, "gy", partner(n_y, step)))
    owner = owner_peer[:, :, 0]
    slot = slot_of(owner // n_y, me[0], n_x) * n_y + slot_of(owner % n_y, me[1], n_y)
    index = slot * elems + src_local
    total = n_y * elems + (n_x - 1) * slots
    ids, *masks = call(
        lambda *refs: index_kernel(n_y, capacity, *refs),
        (shape((1, total), jnp.int32),) + (shape((8, n_y * elems)),) * (n_x - 1),
        [VM],
    )(index)
    asked = [lax.ppermute(mask, "gx", partner(n_x, step + 1)) for step, mask in enumerate(masks)]
    fhigh, flow = force_table()
    table = shape((OVL, NB, QP), BF)
    heavy = pl.CostEstimate(flops=2_000_000_000, bytes_accessed=8_000_000, transcendentals=0)
    high, low = call(prep_kernel, (table, table), [VM], cost=heavy)(factor_rows())
    asked, high, low = lax.optimization_barrier((asked, high, low))
    packed = call(
        lambda *refs: pack_kernel(n_y, capacity, n_x - 1, *refs),
        (shape((slots, CUT)), shape((slots, width - CUT))) * (n_x - 1),
        [VM] * (n_x - 1 + n_y),
    )(*asked, *column)
    early, late = [
        [
            lax.ppermute(packed[2 * step - 2 + part], "gx", partner(n_x, step))
            for step in range(1, n_x)
        ]
        for part in range(2)
    ]
    face = shape((EY * EZ, 4 * PAD))
    whole = shape((elems, 4 * PAD))
    lead, lumped, parts, piece, back = call(
        lambda *refs: lead_kernel(n_y, n_x - 1, *refs),
        (shape((elems, 2 * NB)), shape((elems, NB)), whole, face, face),
        [VM] * (7 + n_y + n_x - 1),
        [pltpu.VMEM((OVL * elems, CUT), F32)] * 2,
    )(ids, index, jac, high, low, fhigh, flow, *column, *early)
    got, turn = swap_faces(piece, back, "gx", n_x)
    pieces = (*column, *[piece for pair in zip(early, late) for piece in pair])
    tails = [pltpu.VMEM((OVL // 2 * elems, width - CUT + 128), F32)] * 2
    partial = call(
        lambda *refs: tail_kernel(n_y, n_x - 1, 0, *refs),
        shape(((FIELDS - 2) * elems, NB)),
        [VM] * (5 + len(pieces)),
        tails,
        heavy,
    )(ids, index, jac, high, low, *pieces)
    got, turn, partial = lax.optimization_barrier((got, turn, partial))
    face = shape((EX * EZ, 4 * PAD))
    parts, piece, back = call(x_kernel, (whole, face, face), [VM] * 3)(parts, got, turn)
    got, turn = swap_faces(piece, back, "gy", n_y)
    fields = call(
        lambda *refs: tail_kernel(n_y, n_x - 1, 1, *refs),
        shape((elems, width)),
        [VM] * (8 + len(pieces)),
        tails,
        heavy,
    )(ids, index, jac, high, low, *pieces, partial, lumped, lead)
    got, turn, fields = lax.optimization_barrier((got, turn, fields))
    parts = call(y_kernel, whole, [VM] * 3)(parts, got, turn)
    if n_z == 2:
        before = after = lax.ppermute(parts, "gz", [(0, 1), (1, 0)])
    else:
        before = lax.ppermute(parts, "gz", [(i, i + 1) for i in range(n_z - 1)])
        after = lax.ppermute(parts, "gz", [(i + 1, i) for i in range(n_z - 1)])
    accel = call(z_kernel, shape((elems, 3 * NB)), [VM] * 3)(parts, before, after)
    return fields, accel


def solution(mesh):
    rows = ("gx", "gy", "gz")
    placed = (P(rows, None), P(rows, None, None), P(rows, None), P(rows, None))

    return jax.shard_map(
        per_device,
        mesh=mesh,
        in_specs=placed,
        out_specs=(P(rows, None), P(rows, None)),
        check_vma=False,
    )
```

```python
import math

import jax
import jax.numpy as jnp
import numpy as np
from jax import lax
from jax.experimental import pallas as pl
from jax.experimental.pallas import tpu as pltpu
from jax.sharding import PartitionSpec as P

EX = 4
EY = 4
EZ = 2
FIELDS = 5
NB = 216
QP = 512
OVL = 8
PAD = 256
CUT = 512
BF = jnp.bfloat16
F32 = jnp.float32


def three_way(table):
    parts = []
    rest = np.asarray(table, np.float32)
    for _ in range(3):
        part = rest.astype(jnp.bfloat16)
        parts.append(part)
        rest = rest - part.astype(np.float32)
    return parts


def lower_integral(first, second):
    if first < 0 or first > 4:
        return 0.0
    return math.comb(4, first) * math.comb(5, second) / (10.0 * math.comb(9, first + second))


def force_table():
    mass_one = np.zeros((6, 6))
    grad_one = np.zeros((6, 6))
    for left in range(6):
        for right in range(6):
            mass_one[left, right] = (
                math.comb(5, left) * math.comb(5, right) / (11.0 * math.comb(10, left + right))
            )
            grad_one[left, right] = 5.0 * (
                lower_integral(left - 1, right) - lower_integral(left, right)
            )
    grad_x = np.kron(grad_one, np.kron(mass_one, mass_one))
    grad_y = np.kron(mass_one, np.kron(grad_one, mass_one))
    grad_z = np.kron(mass_one, np.kron(mass_one, grad_one))
    joined = np.zeros((NB, 3 * PAD), np.float32)
    for c, grad in enumerate((grad_x, grad_y, grad_z)):
        joined[:, c * PAD : c * PAD + NB] = grad.T * 8.0
    high, low, _ = three_way(joined)
    return jnp.asarray(high, BF), jnp.asarray(low, BF)


def split(value):
    high = value.astype(BF)
    return high, (value - high.astype(F32)).astype(BF)


def dot(a, b, dims=((1,), (0,))):
    return lax.dot_general(a, b, (dims, ((), ())), preferred_element_type=F32)


def dot3(a, b, dims=((1,), (0,))):
    return dot(a[0], b[0], dims) + (dot(a[0], b[1], dims) + dot(a[1], b[0], dims))


NT = ((1,), (1,))


def bern_rows(stride, bit):
    row = lax.broadcasted_iota(jnp.int32, (8, QP), 0)
    point = lax.broadcasted_iota(jnp.int32, (8, QP), 1) // stride % 8
    u = point.astype(F32) * (1.0 / 16.0) + (1.0 / 32.0 + 0.5 - 0.5 * bit)
    value = jnp.zeros((8, QP), F32)
    for i in range(6):
        value = jnp.where(row == i, float(math.comb(5, i)), value)
    for n in range(5):
        value = value * jnp.where(row > n, u, 1.0 - u)
    return value


def prep_kernel(high_ref, low_ref):
    coef = lax.broadcasted_iota(jnp.int32, (NB, 24), 0)
    col = lax.broadcasted_iota(jnp.int32, (NB, 24), 1)
    factors = []
    for stride, spacing in ((36, 64), (6, 8), (1, 1)):
        pick = jnp.where(coef // stride % 6 == col % 8, 1.0, 0.0).astype(BF)
        pair = []
        for bit in range(2):
            rows = bern_rows(spacing, bit)
            high = rows.astype(BF)
            middle, low = split(rows - high.astype(F32))
            parts = [part.astype(F32) for part in (high, middle, low)]
            pair.append(dot(pick, jnp.concatenate(parts, 0).astype(BF)))
        factors.append(pair)
    for k in range(OVL):
        table = factors[0][k >> 2 & 1] * factors[1][k >> 1 & 1] * factors[2][k & 1]
        high, low = split(table)
        high_ref[k] = high
        low_ref[k] = low


def hits(index_ref, wanted, spans):
    elems = index_ref.shape[0]
    out = []
    for k in spans:
        column = jnp.broadcast_to(index_ref[:, k : k + 1], (elems, wanted.shape[1]))
        out.append(jnp.where(column == wanted, 1.0, 0.0))
    return out


def packing(mask, capacity, elems, owners):
    width = owners * elems
    row = lax.broadcasted_iota(jnp.int32, (width, width), 0)
    col = lax.broadcasted_iota(jnp.int32, (width, width), 1)
    earlier = jnp.where((row // elems == col // elems) & (row < col), 1.0, 0.0).astype(BF)
    rank = dot(jnp.broadcast_to(mask, (8, width)).astype(BF), earlier)[:1]
    slots = owners * capacity
    spot = lax.broadcasted_iota(jnp.int32, (slots, width), 0)
    lane = lax.broadcasted_iota(jnp.int32, (slots, width), 1)
    wanted = (lane // elems * capacity).astype(F32) + rank
    hit = (spot.astype(F32) == wanted) & (jnp.broadcast_to(mask, (slots, width)) > 0.5)
    return jnp.where(hit, 1.0, 0.0).astype(BF)


def front_kernel(owners, capacity, rows, owner, local, near_ref, far_ref, ids_ref, index_ref, *refs):
    *mask_refs, owner_ref, local_ref, sems = refs
    pairs = (
        (owner, owner_ref),
        (local, local_ref),
        (rows.at[:, :CUT], near_ref),
        (rows.at[:, CUT:], far_ref),
    )
    copies = [
        pltpu.make_async_copy(source, target, sems.at[n]) for n, (source, target) in enumerate(pairs)
    ]
    for copy in copies:
        copy.start()
    elems = owner.shape[1]
    copies[0].wait()
    copies[1].wait()
    owner = owner_ref[...]
    outer = slot_of(owner // owners, lax.axis_index("gx"), lax.axis_size("gx"))
    inner = slot_of(owner % owners, lax.axis_index("gy"), owners)
    index_ref[...] = ((outer * owners + inner) * elems + local_ref[...]).T
    width = owners * elems
    lane = lax.broadcasted_iota(jnp.int32, (elems, (1 + len(mask_refs)) * width), 1)
    named = sum(hits(index_ref, lane, range(OVL)))
    named = jnp.sum(named, 0, keepdims=True)
    mask = jnp.where(named > 0.5, 1.0, 0.0)
    ids_ref[:, :width] = lane[:1, :width]
    local = lax.broadcasted_iota(jnp.int32, (8, width), 1) + 1
    slots = owners * capacity
    for s, mask_ref in enumerate(mask_refs):
        part = mask[:, (s + 1) * width : (s + 2) * width]
        mask_ref[...] = jnp.broadcast_to(part, mask_ref.shape)
        order = packing(part, capacity, elems, owners)
        ids = dot(local.astype(F32).astype(BF), order, NT)[:1].astype(jnp.int32)
        ids = jnp.where(ids > 0, ids + ((s + 1) * width - 1), -1)
        ids_ref[:, width + s * slots : width + (s + 1) * slots] = ids
    copies[2].wait()
    copies[3].wait()


def lanes_of(pieces, width, part):
    span = slice(0, CUT) if part == 0 else slice(CUT, width)
    return [ref[:, span] if ref.shape[1] == width else ref[...] for ref in pieces]


def pack_kernel(owners, capacity, count, width, part, *refs):
    masks = refs[:count]
    column = refs[count : count + owners]
    outs = refs[count + owners :]
    elems = column[0].shape[0]
    order = jnp.concatenate(
        [packing(mask[:1], capacity, elems, owners) for mask in masks], 0
    )
    rows = jnp.concatenate(lanes_of(column, width, part), 0)
    high = rows.astype(BF)
    rest = rows - high.astype(F32)
    middle, low = split(rest)
    packed = (dot(order, high) + dot(order, middle)) + dot(order, low)
    slots = owners * capacity
    for s in range(count):
        outs[s][...] = packed[s * slots : (s + 1) * slots]


def pick(hot, rows, outs):
    high, low = split(rows)
    outs[0][...] = dot(hot, high)
    outs[1][...] = dot(hot, low)


def mirror():
    row = lax.broadcasted_iota(jnp.int32, (NB, NB), 0)
    col = lax.broadcasted_iota(jnp.int32, (NB, NB), 1)
    return jnp.where(row + col // 36 * 72 == col + 180, 1.0, 0.0).astype(BF)


def project(offset, picked, jac_ref, high_ref, low_ref, extra):
    elems = jac_ref.shape[0]
    count = (picked[0].shape[1] - offset) // NB
    half = OVL // 2
    flip = mirror()

    def apply(pair, table, dims=((1,), (0,))):
        size = pair[0].shape[0]
        both = dot(jnp.concatenate(pair, 0), high_ref[table], dims)
        return both[:size] + (both[size:] + dot(pair[0], low_ref[table], dims))

    def fields_of(ref, first, last):
        at = slice(first * elems, last * elems)
        return [
            ref[at, offset + f * NB : offset + (f + 1) * NB].astype(BF) for f in range(count)
        ]

    turned = jnp.concatenate([x for ref in picked for x in fields_of(ref, 0, half)], 0)
    turned = dot(turned, flip).astype(BF)
    total = None
    for n in range(half):
        source = []
        for m, ref in enumerate(picked):
            rows = fields_of(ref, half + n, half + n + 1)
            for f in range(count):
                base = ((m * count + f) * half + n) * elems
                rows.append(turned[base : base + elems])
            source.append(jnp.concatenate(rows, 0))
        values = apply(source, half + n)
        weights = jac_ref[:, (half + n) * QP : (half + n + 1) * QP]
        other = [
            pltpu.roll(jac_ref[:, base : base + 128], 64, 1)
            for base in range((n + 1) * QP - 128, n * QP - 128, -128)
        ]
        other = jnp.concatenate(other, 1)
        scaled = values * jnp.concatenate([weights] * count + [other] * count, 0)
        if extra:
            scaled = jnp.concatenate([scaled, weights, other], 0)
        part = apply(split(scaled), half - 1 - n, NT)
        total = part if total is None else total + part
    own = [total[: count * elems]]
    turned = [total[count * elems : 2 * count * elems]]
    if extra:
        own.append(total[2 * count * elems : (2 * count + 1) * elems])
        turned.append(total[(2 * count + 1) * elems :])
    own, turned = jnp.concatenate(own, 0), jnp.concatenate(turned, 0)
    high = turned.astype(BF)
    middle, low = split(turned - high.astype(F32))
    size = turned.shape[0]
    back = dot(jnp.concatenate([high, middle, low], 0), flip)
    return own + ((back[:size] + back[size : 2 * size]) + back[2 * size :])


def send_faces(even, first, last, send_ref, back_ref):
    send_ref[...] = jnp.where(even, last, first)
    back_ref[...] = jnp.where(even, first, last)


def take_faces(axis, got, back):
    me, count = lax.axis_index(axis), lax.axis_size(axis)
    even = me % 2 == 0
    before = jnp.where(even, back, got)
    after = jnp.where(even, got, back)
    return jnp.where(me > 0, before, 0.0), jnp.where(me < count - 1, after, 0.0)


def lead_kernel(owners, count, ids_ref, index_ref, jac_ref, high_ref, low_ref, fhigh_ref, flow_ref, *refs):
    column = refs[:owners]
    packed = refs[owners : owners + count]
    refs = refs[owners + count :]
    fields_ref, lumped_ref, parts_ref, send_ref, back_ref, *picked = refs
    elems = jac_ref.shape[0]
    hot = jnp.concatenate(hits(index_ref, ids_ref[...], range(OVL)), 0).astype(BF)
    rows = lanes_of((*column, *packed), NB * FIELDS, 0)
    pick(hot, jnp.concatenate(rows, 0), picked)
    total = project(0, picked, jac_ref, high_ref, low_ref, True)
    lumped = total[2 * elems :]
    lumped_ref[...] = lumped
    fields = [total[f * elems : (f + 1) * elems] / lumped for f in range(2)]
    for f in range(2):
        fields_ref[:, f * NB : (f + 1) * NB] = fields[f]
    pressure = fields[0] * fields[1]
    force = dot3(split(pressure), (fhigh_ref[...], flow_ref[...]))
    mass = jnp.concatenate([lumped * (1.0 / 4096.0), jnp.zeros((elems, PAD - NB), F32)], 1)
    parts = jnp.concatenate([force, mass], 1)
    parts_ref[...] = parts
    width = EY * EZ
    even = lax.axis_index("gx") % 2 == 0
    send_faces(even, parts[:width], parts[-width:], send_ref, back_ref)


def tail_kernel(count, ids_ref, index_ref, jac_ref, high_ref, low_ref, lumped_ref, lead_ref, *refs):
    near, far = refs[:count], refs[count : 2 * count]
    out_ref, *picked = refs[2 * count :]
    elems = jac_ref.shape[0]
    start = CUT - 128
    hot = jnp.concatenate(hits(index_ref, ids_ref[...], range(OVL)), 0).astype(BF)
    rows = []
    for a, b in zip(near, far):
        if a.shape[1] == NB * FIELDS:
            rows.append(a[:, start:])
        else:
            rows.append(jnp.concatenate([a[:, start:], b[...]], 1))
    pick(hot, jnp.concatenate(rows, 0), picked)
    total = project(2 * NB - start, picked, jac_ref, high_ref, low_ref, False)
    lumped = lumped_ref[...]
    out_ref[:, : 2 * NB] = lead_ref[...]
    for f in range(3):
        out_ref[:, (f + 2) * NB : (f + 3) * NB] = total[f * elems : (f + 1) * elems] / lumped


def face_add(parts, before, after, shift, stride):
    comps = []
    elems = parts.shape[0]
    lane = lax.broadcasted_iota(jnp.int32, (elems, PAD), 1)
    spot = lane // stride % 6
    inside = lane < NB
    for c in range(4):
        at = slice(c * PAD, (c + 1) * PAD)
        low = pltpu.roll(before[:, at], PAD - shift, 1)
        high = pltpu.roll(after[:, at], shift, 1)
        low = jnp.where((spot == 0) & inside, low, 0.0)
        high = jnp.where((spot == 5) & inside, high, 0.0)
        comps.append(parts[:, at] + (low + high))
    return jnp.concatenate(comps, 1)


def x_kernel(parts_ref, got_ref, turn_ref, out_ref, send_ref, back_ref):
    parts = parts_ref[...]
    width = EY * EZ
    before, after = take_faces("gx", got_ref[...], turn_ref[...])
    before = jnp.concatenate([before, parts[:-width]], 0)
    after = jnp.concatenate([parts[width:], after], 0)
    parts = face_add(parts, before, after, 180, 36)
    out_ref[...] = parts
    first = [parts[x * width : x * width + EZ] for x in range(EX)]
    last = [parts[(x + 1) * width - EZ : (x + 1) * width] for x in range(EX)]
    first, last = jnp.concatenate(first, 0), jnp.concatenate(last, 0)
    send_faces(lax.axis_index("gy") % 2 == 0, first, last, send_ref, back_ref)


def y_kernel(parts_ref, got_ref, turn_ref, out_ref):
    parts = parts_ref[...]
    width = EY * EZ
    far_before, far_after = take_faces("gy", got_ref[...], turn_ref[...])
    before = []
    after = []
    for x in range(EX):
        base = x * width
        near = slice(x * EZ, (x + 1) * EZ)
        before += [far_before[near], parts[base : base + width - EZ]]
        after += [parts[base + EZ : base + width], far_after[near]]
    before = jnp.concatenate(before, 0)
    after = jnp.concatenate(after, 0)
    out_ref[...] = face_add(parts, before, after, 30, 6)


def z_kernel(parts_ref, before_ref, after_ref, out_ref):
    parts = parts_ref[...]
    elems = parts.shape[0]
    odd = lax.broadcasted_iota(jnp.int32, parts.shape, 0) % EZ == EZ - 1
    has_before = lax.axis_index("gz") > 0
    has_after = lax.axis_index("gz") < lax.axis_size("gz") - 1
    far_before = jnp.where(has_before, pltpu.roll(before_ref[...], elems - 1, 0), 0.0)
    far_after = jnp.where(has_after, pltpu.roll(after_ref[...], 1, 0), 0.0)
    before = jnp.where(odd, pltpu.roll(parts, 1, 0), far_before)
    after = jnp.where(odd, far_after, pltpu.roll(parts, elems - 1, 0))
    parts = face_add(parts, before, after, 5, 1)
    mass = parts[:, 3 * PAD :]
    for c in range(3):
        accel = parts[:, c * PAD : c * PAD + NB] / mass[:, :NB]
        out_ref[:, c * NB : (c + 1) * NB] = accel


VM = pl.BlockSpec(memory_space=pltpu.VMEM)
HB = pl.BlockSpec(memory_space=pltpu.HBM)


def call(kernel, shapes, specs, scratch=(), cost=None):
    return pl.pallas_call(
        kernel,
        out_shape=shapes,
        in_specs=specs,
        out_specs=jax.tree.map(lambda _: VM, shapes),
        scratch_shapes=scratch,
        cost_estimate=cost,
        compiler_params=pltpu.CompilerParams(vmem_limit_bytes=16 << 20),
    )


def partner(count, step):
    if count & (count - 1) == 0:
        return [(i, i ^ step) for i in range(count)]
    return [(i, (i + step) % count) for i in range(count)]


def slot_of(owner, me, count):
    if count & (count - 1) == 0:
        return owner ^ me
    return (me - owner) % count


def shape(dims, dtype=F32):
    return jax.ShapeDtypeStruct(dims, dtype)


def swap_faces(piece, back, axis, count):
    near = [(i, i ^ 1) for i in range(count)]
    across = [(i, (i + 1) % count if i % 2 else (i - 1) % count) for i in range(count)]
    return lax.ppermute(piece, axis, near), lax.ppermute(back, axis, across)


def per_device(src_fields, owner_peer, src_local, jac):
    n_x = lax.axis_size("gx")
    n_y = lax.axis_size("gy")
    n_z = lax.axis_size("gz")
    elems = src_fields.shape[0]
    width = src_fields.shape[1]
    capacity = max(2, 9 * elems // (n_x * n_y))
    slots = n_y * capacity
    nearest = lax.ppermute(src_fields, "gy", partner(n_y, 1))
    total = n_y * elems + (n_x - 1) * slots
    turned = (OVL, elems)
    own_a, own_b, ids, index, *masks = call(
        lambda *refs: front_kernel(n_y, capacity, *refs),
        (
            shape((elems, CUT)),
            shape((elems, width - CUT)),
            shape((1, total), jnp.int32),
            shape(src_local.shape, jnp.int32),
        )
        + (shape((8, n_y * elems)),) * (n_x - 1),
        [HB] * 3,
        [pltpu.VMEM(turned, jnp.int32)] * 2 + [pltpu.SemaphoreType.DMA((4,))],
    )(*[
        pltpu.with_memory_space_constraint(operand, pltpu.HBM)
        for operand in (src_fields, owner_peer[:, :, 0].T, src_local.T)
    ])
    columns = [
        [piece, nearest] + [lax.ppermute(piece, "gy", partner(n_y, step)) for step in range(2, n_y)]
        for piece in (own_a, own_b)
    ]
    fhigh, flow = force_table()
    table = shape((OVL, NB, QP), BF)
    heavy = pl.CostEstimate(flops=2_000_000_000, bytes_accessed=8_000_000, transcendentals=0)
    high, low = call(prep_kernel, (table, table), [], cost=heavy)()
    asked = [lax.ppermute(mask, "gx", partner(n_x, step + 1)) for step, mask in enumerate(masks)]
    gathered = []
    for part in range(2):
        span = (CUT, width - CUT)[part]
        packed = call(
            lambda *refs: pack_kernel(n_y, capacity, n_x - 1, width, part, *refs),
            (shape((slots, span)),) * (n_x - 1),
            [VM] * (n_x - 1 + n_y),
        )(*asked, *columns[part])
        arrived = [
            lax.ppermute(piece, "gx", partner(n_x, step + 1))
            for step, piece in enumerate(packed)
        ]
        gathered.append(columns[part] + arrived)
    near, far = gathered
    face = shape((EY * EZ, 4 * PAD))
    whole = shape((elems, 4 * PAD))
    lead, lumped, parts, piece, back = call(
        lambda *refs: lead_kernel(n_y, n_x - 1, *refs),
        (shape((elems, 2 * NB)), shape((elems, NB)), whole, face, face),
        [VM] * (7 + len(near)),
        [pltpu.VMEM((OVL * elems, CUT), F32)] * 2,
    )(ids, index, jac, high, low, fhigh, flow, *near)
    got, turn = swap_faces(piece, back, "gx", n_x)
    face = shape((EX * EZ, 4 * PAD))
    parts, piece, back = call(x_kernel, (whole, face, face), [VM] * 3)(parts, got, turn)
    got, turn = swap_faces(piece, back, "gy", n_y)
    scratch = pltpu.VMEM((OVL * elems, width - CUT + 128), F32)
    fields = call(
        lambda *refs: tail_kernel(len(near), *refs),
        shape((elems, width)),
        [VM] * (7 + 2 * len(near)),
        [scratch] * 2,
        heavy,
    )(ids, index, jac, high, low, lumped, lead, *near, *far)
    got, turn, fields = lax.optimization_barrier((got, turn, fields))
    parts = call(y_kernel, whole, [VM] * 3)(parts, got, turn)
    if n_z == 2:
        before = after = lax.ppermute(parts, "gz", [(0, 1), (1, 0)])
    else:
        before = lax.ppermute(parts, "gz", [(i, i + 1) for i in range(n_z - 1)])
        after = lax.ppermute(parts, "gz", [(i + 1, i) for i in range(n_z - 1)])
    accel = call(z_kernel, shape((elems, 3 * NB)), [VM] * 3)(parts, before, after)
    return fields, accel


def solution(mesh):
    rows = ("gx", "gy", "gz")
    placed = (P(rows, None), P(rows, None, None), P(rows, None), P(rows, None))

    return jax.shard_map(
        per_device,
        mesh=mesh,
        in_specs=placed,
        out_specs=(P(rows, None), P(rows, None)),
        check_vma=False,
    )
```

```python
import math

import jax
import jax.numpy as jnp
import numpy as np
from jax import lax
from jax.experimental import pallas as pl
from jax.experimental.pallas import tpu as pltpu
from jax.sharding import PartitionSpec as P

EX = 4
EY = 4
EZ = 2
FIELDS = 5
NB = 216
QP = 512
OVL = 8
PAD = 256
CUT = 512
BF = jnp.bfloat16
F32 = jnp.float32


def three_way(table):
    parts = []
    rest = np.asarray(table, np.float32)
    for _ in range(3):
        part = rest.astype(jnp.bfloat16)
        parts.append(part)
        rest = rest - part.astype(np.float32)
    return parts


def lower_integral(first, second):
    if first < 0 or first > 4:
        return 0.0
    return math.comb(4, first) * math.comb(5, second) / (10.0 * math.comb(9, first + second))


def force_table():
    mass_one = np.zeros((6, 6))
    grad_one = np.zeros((6, 6))
    for left in range(6):
        for right in range(6):
            mass_one[left, right] = (
                math.comb(5, left) * math.comb(5, right) / (11.0 * math.comb(10, left + right))
            )
            grad_one[left, right] = 5.0 * (
                lower_integral(left - 1, right) - lower_integral(left, right)
            )
    grad_x = np.kron(grad_one, np.kron(mass_one, mass_one))
    grad_y = np.kron(mass_one, np.kron(grad_one, mass_one))
    grad_z = np.kron(mass_one, np.kron(mass_one, grad_one))
    joined = np.zeros((NB, 3 * PAD), np.float32)
    for c, grad in enumerate((grad_x, grad_y, grad_z)):
        joined[:, c * PAD : c * PAD + NB] = grad.T * 8.0
    high, low, _ = three_way(joined)
    return jnp.asarray(high, BF), jnp.asarray(low, BF)


def split(value):
    high = value.astype(BF)
    return high, (value - high.astype(F32)).astype(BF)


def dot(a, b, dims=((1,), (0,))):
    return lax.dot_general(a, b, (dims, ((), ())), preferred_element_type=F32)


def dot3(a, b, dims=((1,), (0,))):
    return dot(a[0], b[0], dims) + (dot(a[0], b[1], dims) + dot(a[1], b[0], dims))


NT = ((1,), (1,))


def bern_rows(stride, bit):
    row = lax.broadcasted_iota(jnp.int32, (8, QP), 0)
    point = lax.broadcasted_iota(jnp.int32, (8, QP), 1) // stride % 8
    u = point.astype(F32) * (1.0 / 16.0) + (1.0 / 32.0 + 0.5 - 0.5 * bit)
    value = jnp.zeros((8, QP), F32)
    for i in range(6):
        value = jnp.where(row == i, float(math.comb(5, i)), value)
    for n in range(5):
        value = value * jnp.where(row > n, u, 1.0 - u)
    return value


def prep_kernel(high_ref, low_ref):
    coef = lax.broadcasted_iota(jnp.int32, (NB, 24), 0)
    col = lax.broadcasted_iota(jnp.int32, (NB, 24), 1)
    factors = []
    for stride, spacing in ((36, 64), (6, 8), (1, 1)):
        pick = jnp.where(coef // stride % 6 == col % 8, 1.0, 0.0).astype(BF)
        pair = []
        for bit in range(2):
            rows = bern_rows(spacing, bit)
            high = rows.astype(BF)
            middle, low = split(rows - high.astype(F32))
            parts = [part.astype(F32) for part in (high, middle, low)]
            pair.append(dot(pick, jnp.concatenate(parts, 0).astype(BF)))
        factors.append(pair)
    for k in range(OVL):
        table = factors[0][k >> 2 & 1] * factors[1][k >> 1 & 1] * factors[2][k & 1]
        high, low = split(table)
        high_ref[k] = high
        low_ref[k] = low


def hits(index_ref, wanted, spans):
    elems = index_ref.shape[0]
    out = []
    for k in spans:
        column = jnp.broadcast_to(index_ref[:, k : k + 1], (elems, wanted.shape[1]))
        out.append(jnp.where(column == wanted, 1.0, 0.0))
    return out


def packing(mask, capacity, elems, owners):
    width = owners * elems
    row = lax.broadcasted_iota(jnp.int32, (width, width), 0)
    col = lax.broadcasted_iota(jnp.int32, (width, width), 1)
    earlier = jnp.where((row // elems == col // elems) & (row < col), 1.0, 0.0).astype(BF)
    rank = dot(jnp.broadcast_to(mask, (8, width)).astype(BF), earlier)[:1]
    slots = owners * capacity
    spot = lax.broadcasted_iota(jnp.int32, (slots, width), 0)
    lane = lax.broadcasted_iota(jnp.int32, (slots, width), 1)
    wanted = (lane // elems * capacity).astype(F32) + rank
    hit = (spot.astype(F32) == wanted) & (jnp.broadcast_to(mask, (slots, width)) > 0.5)
    return jnp.where(hit, 1.0, 0.0).astype(BF)


def front_kernel(owners, capacity, rows, owner, local, near_ref, far_ref, ids_ref, index_ref, *refs):
    *mask_refs, owner_ref, local_ref, sems = refs
    pairs = (
        (owner, owner_ref),
        (local, local_ref),
        (rows.at[:, :CUT], near_ref),
        (rows.at[:, CUT:], far_ref),
    )
    copies = [
        pltpu.make_async_copy(source, target, sems.at[n]) for n, (source, target) in enumerate(pairs)
    ]
    for copy in copies:
        copy.start()
    elems = owner.shape[1]
    copies[0].wait()
    copies[1].wait()
    owner = owner_ref[...]
    outer = slot_of(owner // owners, lax.axis_index("gx"), lax.axis_size("gx"))
    inner = slot_of(owner % owners, lax.axis_index("gy"), owners)
    index_ref[...] = ((outer * owners + inner) * elems + local_ref[...]).T
    width = owners * elems
    lane = lax.broadcasted_iota(jnp.int32, (elems, (1 + len(mask_refs)) * width), 1)
    named = sum(hits(index_ref, lane, range(OVL)))
    named = jnp.sum(named, 0, keepdims=True)
    mask = jnp.where(named > 0.5, 1.0, 0.0)
    ids_ref[:, :width] = lane[:1, :width]
    local = lax.broadcasted_iota(jnp.int32, (8, width), 1) + 1
    slots = owners * capacity
    for s, mask_ref in enumerate(mask_refs):
        part = mask[:, (s + 1) * width : (s + 2) * width]
        mask_ref[...] = jnp.broadcast_to(part, mask_ref.shape)
        order = packing(part, capacity, elems, owners)
        ids = dot(local.astype(F32).astype(BF), order, NT)[:1].astype(jnp.int32)
        ids = jnp.where(ids > 0, ids + ((s + 1) * width - 1), -1)
        ids_ref[:, width + s * slots : width + (s + 1) * slots] = ids
    copies[2].wait()
    copies[3].wait()


def lanes_of(pieces, width, part):
    span = slice(0, CUT) if part == 0 else slice(CUT, width)
    return [ref[:, span] if ref.shape[1] == width else ref[...] for ref in pieces]


def pack_kernel(owners, capacity, count, width, part, *refs):
    masks = refs[:count]
    column = refs[count : count + owners]
    outs = refs[count + owners :]
    elems = column[0].shape[0]
    order = jnp.concatenate(
        [packing(mask[:1], capacity, elems, owners) for mask in masks], 0
    )
    rows = jnp.concatenate(lanes_of(column, width, part), 0)
    high = rows.astype(BF)
    rest = rows - high.astype(F32)
    middle, low = split(rest)
    packed = (dot(order, high) + dot(order, middle)) + dot(order, low)
    slots = owners * capacity
    for s in range(count):
        outs[s][...] = packed[s * slots : (s + 1) * slots]


def pick(hot, rows, outs):
    high, low = split(rows)
    outs[0][...] = dot(hot, high)
    outs[1][...] = dot(hot, low)


def mirror():
    row = lax.broadcasted_iota(jnp.int32, (NB, NB), 0)
    col = lax.broadcasted_iota(jnp.int32, (NB, NB), 1)
    return jnp.where(row + col // 36 * 72 == col + 180, 1.0, 0.0).astype(BF)


def project(offset, picked, jac_ref, high_ref, low_ref, extra):
    elems = jac_ref.shape[0]
    count = (picked[0].shape[1] - offset) // NB
    half = OVL // 2
    flip = mirror()

    def apply(pair, table, dims=((1,), (0,))):
        size = pair[0].shape[0]
        both = dot(jnp.concatenate(pair, 0), high_ref[table], dims)
        return both[:size] + (both[size:] + dot(pair[0], low_ref[table], dims))

    def fields_of(ref, first, last):
        at = slice(first * elems, last * elems)
        return [
            ref[at, offset + f * NB : offset + (f + 1) * NB].astype(BF) for f in range(count)
        ]

    turned = jnp.concatenate([x for ref in picked for x in fields_of(ref, 0, half)], 0)
    turned = dot(turned, flip).astype(BF)
    total = None
    for n in range(half):
        source = []
        for m, ref in enumerate(picked):
            rows = fields_of(ref, half + n, half + n + 1)
            for f in range(count):
                base = ((m * count + f) * half + n) * elems
                rows.append(turned[base : base + elems])
            source.append(jnp.concatenate(rows, 0))
        values = apply(source, half + n)
        weights = jac_ref[:, (half + n) * QP : (half + n + 1) * QP]
        other = [
            pltpu.roll(jac_ref[:, base : base + 128], 64, 1)
            for base in range((n + 1) * QP - 128, n * QP - 128, -128)
        ]
        other = jnp.concatenate(other, 1)
        scaled = values * jnp.concatenate([weights] * count + [other] * count, 0)
        if extra:
            scaled = jnp.concatenate([scaled, weights, other], 0)
        part = apply(split(scaled), half - 1 - n, NT)
        total = part if total is None else total + part
    own = [total[: count * elems]]
    turned = [total[count * elems : 2 * count * elems]]
    if extra:
        own.append(total[2 * count * elems : (2 * count + 1) * elems])
        turned.append(total[(2 * count + 1) * elems :])
    own, turned = jnp.concatenate(own, 0), jnp.concatenate(turned, 0)
    high = turned.astype(BF)
    middle, low = split(turned - high.astype(F32))
    size = turned.shape[0]
    back = dot(jnp.concatenate([high, middle, low], 0), flip)
    return own + ((back[:size] + back[size : 2 * size]) + back[2 * size :])


def fold(rows, stride, end):
    lane = lax.broadcasted_iota(jnp.int32, (rows.shape[0], PAD), 1)
    keep = (lane // stride % 6 == end) & (lane < NB)
    out = []
    for c in range(4):
        face = jnp.where(keep, rows[:, c * PAD : (c + 1) * PAD], 0.0)
        out.append(face[:, : PAD // 2] + face[:, PAD // 2 :])
    return jnp.concatenate(out, 1)


def unfold(face):
    half = PAD // 2
    out = []
    for c in range(4):
        out += [face[:, c * half : (c + 1) * half]] * 2
    return jnp.concatenate(out, 1)


def send_faces(even, first, last, stride, send_ref, back_ref):
    first, last = fold(first, stride, 0), fold(last, stride, 5)
    send_ref[...] = jnp.where(even, last, first)
    back_ref[...] = jnp.where(even, first, last)


def take_faces(axis, got, back):
    me, count = lax.axis_index(axis), lax.axis_size(axis)
    even = me % 2 == 0
    got, back = unfold(got), unfold(back)
    before = jnp.where(even, back, got)
    after = jnp.where(even, got, back)
    return jnp.where(me > 0, before, 0.0), jnp.where(me < count - 1, after, 0.0)


def lead_kernel(owners, count, ids_ref, index_ref, jac_ref, high_ref, low_ref, fhigh_ref, flow_ref, *refs):
    column = refs[:owners]
    packed = refs[owners : owners + count]
    refs = refs[owners + count :]
    fields_ref, lumped_ref, parts_ref, send_ref, back_ref, *picked = refs
    elems = jac_ref.shape[0]
    hot = jnp.concatenate(hits(index_ref, ids_ref[...], range(OVL)), 0).astype(BF)
    rows = lanes_of((*column, *packed), NB * FIELDS, 0)
    pick(hot, jnp.concatenate(rows, 0), picked)
    total = project(0, picked, jac_ref, high_ref, low_ref, True)
    lumped = total[2 * elems :]
    lumped_ref[...] = lumped
    fields = [total[f * elems : (f + 1) * elems] / lumped for f in range(2)]
    for f in range(2):
        fields_ref[:, f * NB : (f + 1) * NB] = fields[f]
    pressure = fields[0] * fields[1]
    force = dot3(split(pressure), (fhigh_ref[...], flow_ref[...]))
    mass = jnp.concatenate([lumped * (1.0 / 4096.0), jnp.zeros((elems, PAD - NB), F32)], 1)
    parts = jnp.concatenate([force, mass], 1)
    parts_ref[...] = parts
    width = EY * EZ
    even = lax.axis_index("gx") % 2 == 0
    send_faces(even, parts[:width], parts[-width:], 36, send_ref, back_ref)


def tail_kernel(count, ids_ref, index_ref, jac_ref, high_ref, low_ref, lumped_ref, lead_ref, *refs):
    near, far = refs[:count], refs[count : 2 * count]
    out_ref, *picked = refs[2 * count :]
    elems = jac_ref.shape[0]
    start = CUT - 128
    hot = jnp.concatenate(hits(index_ref, ids_ref[...], range(OVL)), 0).astype(BF)
    rows = []
    for a, b in zip(near, far):
        if a.shape[1] == NB * FIELDS:
            rows.append(a[:, start:])
        else:
            rows.append(jnp.concatenate([a[:, start:], b[...]], 1))
    pick(hot, jnp.concatenate(rows, 0), picked)
    total = project(2 * NB - start, picked, jac_ref, high_ref, low_ref, False)
    lumped = lumped_ref[...]
    out_ref[:, : 2 * NB] = lead_ref[...]
    for f in range(3):
        out_ref[:, (f + 2) * NB : (f + 3) * NB] = total[f * elems : (f + 1) * elems] / lumped


def face_add(parts, before, after, shift, stride):
    comps = []
    elems = parts.shape[0]
    lane = lax.broadcasted_iota(jnp.int32, (elems, PAD), 1)
    spot = lane // stride % 6
    inside = lane < NB
    for c in range(4):
        at = slice(c * PAD, (c + 1) * PAD)
        low = pltpu.roll(before[:, at], PAD - shift, 1)
        high = pltpu.roll(after[:, at], shift, 1)
        low = jnp.where((spot == 0) & inside, low, 0.0)
        high = jnp.where((spot == 5) & inside, high, 0.0)
        comps.append(parts[:, at] + (low + high))
    return jnp.concatenate(comps, 1)


def x_kernel(parts_ref, got_ref, turn_ref, out_ref, send_ref, back_ref):
    parts = parts_ref[...]
    width = EY * EZ
    before, after = take_faces("gx", got_ref[...], turn_ref[...])
    before = jnp.concatenate([before, parts[:-width]], 0)
    after = jnp.concatenate([parts[width:], after], 0)
    parts = face_add(parts, before, after, 180, 36)
    out_ref[...] = parts
    first = [parts[x * width : x * width + EZ] for x in range(EX)]
    last = [parts[(x + 1) * width - EZ : (x + 1) * width] for x in range(EX)]
    first, last = jnp.concatenate(first, 0), jnp.concatenate(last, 0)
    send_faces(lax.axis_index("gy") % 2 == 0, first, last, 6, send_ref, back_ref)


def y_kernel(parts_ref, got_ref, turn_ref, out_ref, *face_refs):
    parts = parts_ref[...]
    width = EY * EZ
    far_before, far_after = take_faces("gy", got_ref[...], turn_ref[...])
    before = []
    after = []
    for x in range(EX):
        base = x * width
        near = slice(x * EZ, (x + 1) * EZ)
        before += [far_before[near], parts[base : base + width - EZ]]
        after += [parts[base + EZ : base + width], far_after[near]]
    before = jnp.concatenate(before, 0)
    after = jnp.concatenate(after, 0)
    parts = face_add(parts, before, after, 30, 6)
    out_ref[...] = parts
    last, first = fold(parts, 1, 5), fold(parts, 1, 0)
    if len(face_refs) == 1:
        face_refs[0][...] = jnp.where(lax.axis_index("gz") % 2 == 0, last, first)
    else:
        face_refs[0][...] = last
        face_refs[1][...] = first


def z_kernel(parts_ref, before_ref, after_ref, out_ref):
    parts = parts_ref[...]
    elems = parts.shape[0]
    odd = lax.broadcasted_iota(jnp.int32, parts.shape, 0) % EZ == EZ - 1
    has_before = lax.axis_index("gz") > 0
    has_after = lax.axis_index("gz") < lax.axis_size("gz") - 1
    far_before = jnp.where(has_before, pltpu.roll(unfold(before_ref[...]), elems - 1, 0), 0.0)
    far_after = jnp.where(has_after, pltpu.roll(unfold(after_ref[...]), 1, 0), 0.0)
    before = jnp.where(odd, pltpu.roll(parts, 1, 0), far_before)
    after = jnp.where(odd, far_after, pltpu.roll(parts, elems - 1, 0))
    parts = face_add(parts, before, after, 5, 1)
    mass = parts[:, 3 * PAD :]
    for c in range(3):
        accel = parts[:, c * PAD : c * PAD + NB] / mass[:, :NB]
        out_ref[:, c * NB : (c + 1) * NB] = accel


VM = pl.BlockSpec(memory_space=pltpu.VMEM)
HB = pl.BlockSpec(memory_space=pltpu.HBM)


def call(kernel, shapes, specs, scratch=(), cost=None):
    return pl.pallas_call(
        kernel,
        out_shape=shapes,
        in_specs=specs,
        out_specs=jax.tree.map(lambda _: VM, shapes),
        scratch_shapes=scratch,
        cost_estimate=cost,
        compiler_params=pltpu.CompilerParams(vmem_limit_bytes=16 << 20),
    )


def partner(count, step):
    if count & (count - 1) == 0:
        return [(i, i ^ step) for i in range(count)]
    return [(i, (i + step) % count) for i in range(count)]


def slot_of(owner, me, count):
    if count & (count - 1) == 0:
        return owner ^ me
    return (me - owner) % count


def shape(dims, dtype=F32):
    return jax.ShapeDtypeStruct(dims, dtype)


def swap_faces(piece, back, axis, count):
    near = [(i, i ^ 1) for i in range(count)]
    across = [(i, (i + 1) % count if i % 2 else (i - 1) % count) for i in range(count)]
    return lax.ppermute(piece, axis, near), lax.ppermute(back, axis, across)


def per_device(src_fields, owner_peer, src_local, jac):
    n_x = lax.axis_size("gx")
    n_y = lax.axis_size("gy")
    n_z = lax.axis_size("gz")
    elems = src_fields.shape[0]
    width = src_fields.shape[1]
    capacity = max(2, 9 * elems // (n_x * n_y))
    slots = n_y * capacity
    nearest = lax.ppermute(src_fields, "gy", partner(n_y, 1))
    total = n_y * elems + (n_x - 1) * slots
    turned = (OVL, elems)
    own_a, own_b, ids, index, *masks = call(
        lambda *refs: front_kernel(n_y, capacity, *refs),
        (
            shape((elems, CUT)),
            shape((elems, width - CUT)),
            shape((1, total), jnp.int32),
            shape(src_local.shape, jnp.int32),
        )
        + (shape((8, n_y * elems)),) * (n_x - 1),
        [HB] * 3,
        [pltpu.VMEM(turned, jnp.int32)] * 2 + [pltpu.SemaphoreType.DMA((4,))],
    )(*[
        pltpu.with_memory_space_constraint(operand, pltpu.HBM)
        for operand in (src_fields, owner_peer[:, :, 0].T, src_local.T)
    ])
    columns = [
        [piece, nearest] + [lax.ppermute(piece, "gy", partner(n_y, step)) for step in range(2, n_y)]
        for piece in (own_a, own_b)
    ]
    fhigh, flow = force_table()
    table = shape((OVL, NB, QP), BF)
    heavy = pl.CostEstimate(flops=2_000_000_000, bytes_accessed=8_000_000, transcendentals=0)
    high, low = call(prep_kernel, (table, table), [], cost=heavy)()
    asked = [lax.ppermute(mask, "gx", partner(n_x, step + 1)) for step, mask in enumerate(masks)]
    gathered = []
    for part in range(2):
        span = (CUT, width - CUT)[part]
        packed = call(
            lambda *refs: pack_kernel(n_y, capacity, n_x - 1, width, part, *refs),
            (shape((slots, span)),) * (n_x - 1),
            [VM] * (n_x - 1 + n_y),
        )(*asked, *columns[part])
        arrived = [
            lax.ppermute(piece, "gx", partner(n_x, step + 1))
            for step, piece in enumerate(packed)
        ]
        gathered.append(columns[part] + arrived)
    near, far = gathered
    face = shape((EY * EZ, 2 * PAD))
    whole = shape((elems, 4 * PAD))
    lead, lumped, parts, piece, back = call(
        lambda *refs: lead_kernel(n_y, n_x - 1, *refs),
        (shape((elems, 2 * NB)), shape((elems, NB)), whole, face, face),
        [VM] * (7 + len(near)),
        [pltpu.VMEM((OVL * elems, CUT), F32)] * 2,
    )(ids, index, jac, high, low, fhigh, flow, *near)
    got, turn = swap_faces(piece, back, "gx", n_x)
    face = shape((EX * EZ, 2 * PAD))
    parts, piece, back = call(x_kernel, (whole, face, face), [VM] * 3)(parts, got, turn)
    got, turn = swap_faces(piece, back, "gy", n_y)
    scratch = pltpu.VMEM((OVL * elems, width - CUT + 128), F32)
    fields = call(
        lambda *refs: tail_kernel(len(near), *refs),
        shape((elems, width)),
        [VM] * (7 + 2 * len(near)),
        [scratch] * 2,
        heavy,
    )(ids, index, jac, high, low, lumped, lead, *near, *far)
    got, turn, fields = lax.optimization_barrier((got, turn, fields))
    ends = (shape((elems, 2 * PAD)),) * (1 if n_z == 2 else 2)
    parts, *ends = call(y_kernel, (whole, *ends), [VM] * 3)(parts, got, turn)
    if n_z == 2:
        before = after = lax.ppermute(ends[0], "gz", [(0, 1), (1, 0)])
    else:
        before = lax.ppermute(ends[0], "gz", [(i, i + 1) for i in range(n_z - 1)])
        after = lax.ppermute(ends[1], "gz", [(i + 1, i) for i in range(n_z - 1)])
    accel = call(z_kernel, shape((elems, 3 * NB)), [VM] * 3)(parts, before, after)
    return fields, accel


def solution(mesh):
    rows = ("gx", "gy", "gz")
    placed = (P(rows, None), P(rows, None, None), P(rows, None), P(rows, None))

    return jax.shard_map(
        per_device,
        mesh=mesh,
        in_specs=placed,
        out_specs=(P(rows, None), P(rows, None)),
        check_vma=False,
    )
```

```python
import math

import jax
import jax.numpy as jnp
import numpy as np
from jax import lax
from jax.experimental import pallas as pl
from jax.experimental.pallas import tpu as pltpu
from jax.sharding import PartitionSpec as P

EX = 4
EY = 4
EZ = 2
FIELDS = 5
NB = 216
QP = 512
OVL = 8
PAD = 256
CUT = 512
BF = jnp.bfloat16
F32 = jnp.float32


def three_way(table):
    parts = []
    rest = np.asarray(table, np.float32)
    for _ in range(3):
        part = rest.astype(jnp.bfloat16)
        parts.append(part)
        rest = rest - part.astype(np.float32)
    return parts


def lower_integral(first, second):
    if first < 0 or first > 4:
        return 0.0
    return math.comb(4, first) * math.comb(5, second) / (10.0 * math.comb(9, first + second))


def force_table():
    mass_one = np.zeros((6, 6))
    grad_one = np.zeros((6, 6))
    for left in range(6):
        for right in range(6):
            mass_one[left, right] = (
                math.comb(5, left) * math.comb(5, right) / (11.0 * math.comb(10, left + right))
            )
            grad_one[left, right] = 5.0 * (
                lower_integral(left - 1, right) - lower_integral(left, right)
            )
    grad_x = np.kron(grad_one, np.kron(mass_one, mass_one))
    grad_y = np.kron(mass_one, np.kron(grad_one, mass_one))
    grad_z = np.kron(mass_one, np.kron(mass_one, grad_one))
    joined = np.zeros((NB, 3 * PAD), np.float32)
    for c, grad in enumerate((grad_x, grad_y, grad_z)):
        joined[:, c * PAD : c * PAD + NB] = grad.T * 8.0
    high, low, _ = three_way(joined)
    return jnp.asarray(high, BF), jnp.asarray(low, BF)


def split(value):
    high = value.astype(BF)
    return high, (value - high.astype(F32)).astype(BF)


def dot(a, b, dims=((1,), (0,))):
    return lax.dot_general(a, b, (dims, ((), ())), preferred_element_type=F32)


def dot3(a, b, dims=((1,), (0,))):
    return dot(a[0], b[0], dims) + (dot(a[0], b[1], dims) + dot(a[1], b[0], dims))


NT = ((1,), (1,))


def bern_rows(stride, bit):
    row = lax.broadcasted_iota(jnp.int32, (8, QP), 0)
    point = lax.broadcasted_iota(jnp.int32, (8, QP), 1) // stride % 8
    u = point.astype(F32) * (1.0 / 16.0) + (1.0 / 32.0 + 0.5 - 0.5 * bit)
    value = jnp.zeros((8, QP), F32)
    for i in range(6):
        value = jnp.where(row == i, float(math.comb(5, i)), value)
    for n in range(5):
        value = value * jnp.where(row > n, u, 1.0 - u)
    return value


def prep_kernel(high_ref, low_ref):
    coef = lax.broadcasted_iota(jnp.int32, (NB, 24), 0)
    col = lax.broadcasted_iota(jnp.int32, (NB, 24), 1)
    factors = []
    for stride, spacing in ((36, 64), (6, 8), (1, 1)):
        pick = jnp.where(coef // stride % 6 == col % 8, 1.0, 0.0).astype(BF)
        pair = []
        for bit in range(2):
            rows = bern_rows(spacing, bit)
            high = rows.astype(BF)
            middle, low = split(rows - high.astype(F32))
            parts = [part.astype(F32) for part in (high, middle, low)]
            pair.append(dot(pick, jnp.concatenate(parts, 0).astype(BF)))
        factors.append(pair)
    for k in range(OVL):
        table = factors[0][k >> 2 & 1] * factors[1][k >> 1 & 1] * factors[2][k & 1]
        high, low = split(table)
        high_ref[k] = high
        low_ref[k] = low


def hits(index_ref, wanted, spans):
    elems = index_ref.shape[0]
    out = []
    for k in spans:
        column = jnp.broadcast_to(index_ref[:, k : k + 1], (elems, wanted.shape[1]))
        out.append(jnp.where(column == wanted, 1.0, 0.0))
    return out


def packing(mask, capacity, elems, owners):
    width = owners * elems
    row = lax.broadcasted_iota(jnp.int32, (width, width), 0)
    col = lax.broadcasted_iota(jnp.int32, (width, width), 1)
    earlier = jnp.where((row // elems == col // elems) & (row < col), 1.0, 0.0).astype(BF)
    rank = dot(jnp.broadcast_to(mask, (8, width)).astype(BF), earlier)[:1]
    slots = owners * capacity
    spot = lax.broadcasted_iota(jnp.int32, (slots, width), 0)
    lane = lax.broadcasted_iota(jnp.int32, (slots, width), 1)
    wanted = (lane // elems * capacity).astype(F32) + rank
    hit = (spot.astype(F32) == wanted) & (jnp.broadcast_to(mask, (slots, width)) > 0.5)
    return jnp.where(hit, 1.0, 0.0).astype(BF)


def front_kernel(owners, capacity, rows, owner, local, near_ref, far_ref, ids_ref, index_ref, *refs):
    *mask_refs, owner_ref, local_ref, sems = refs
    pairs = (
        (owner, owner_ref),
        (local, local_ref),
        (rows.at[:, :CUT], near_ref),
        (rows.at[:, CUT:], far_ref),
    )
    copies = [
        pltpu.make_async_copy(source, target, sems.at[n]) for n, (source, target) in enumerate(pairs)
    ]
    for copy in copies:
        copy.start()
    elems = owner.shape[1]
    copies[0].wait()
    copies[1].wait()
    owner = owner_ref[...]
    outer = slot_of(owner // owners, lax.axis_index("gx"), lax.axis_size("gx"))
    inner = slot_of(owner % owners, lax.axis_index("gy"), owners)
    index_ref[...] = ((outer * owners + inner) * elems + local_ref[...]).T
    width = owners * elems
    lane = lax.broadcasted_iota(jnp.int32, (elems, (1 + len(mask_refs)) * width), 1)
    named = sum(hits(index_ref, lane, range(OVL)))
    named = jnp.sum(named, 0, keepdims=True)
    mask = jnp.where(named > 0.5, 1.0, 0.0)
    ids_ref[:, :width] = lane[:1, :width]
    local = lax.broadcasted_iota(jnp.int32, (8, width), 1) + 1
    slots = owners * capacity
    for s, mask_ref in enumerate(mask_refs):
        part = mask[:, (s + 1) * width : (s + 2) * width]
        mask_ref[...] = jnp.broadcast_to(part, mask_ref.shape)
        order = packing(part, capacity, elems, owners)
        ids = dot(local.astype(F32).astype(BF), order, NT)[:1].astype(jnp.int32)
        ids = jnp.where(ids > 0, ids + ((s + 1) * width - 1), -1)
        ids_ref[:, width + s * slots : width + (s + 1) * slots] = ids
    copies[2].wait()
    copies[3].wait()


def lanes_of(pieces, width, part):
    span = slice(0, CUT) if part == 0 else slice(CUT, width)
    return [ref[:, span] if ref.shape[1] == width else ref[...] for ref in pieces]


def pack_kernel(owners, capacity, count, width, part, *refs):
    masks = refs[:count]
    column = refs[count : count + owners]
    outs = refs[count + owners :]
    elems = column[0].shape[0]
    order = jnp.concatenate(
        [packing(mask[:1], capacity, elems, owners) for mask in masks], 0
    )
    rows = jnp.concatenate(lanes_of(column, width, part), 0)
    high = rows.astype(BF)
    rest = rows - high.astype(F32)
    middle, low = split(rest)
    packed = (dot(order, high) + dot(order, middle)) + dot(order, low)
    slots = owners * capacity
    for s in range(count):
        outs[s][...] = packed[s * slots : (s + 1) * slots]


def pick(hot, rows, outs):
    high, low = split(rows)
    outs[0][...] = dot(hot, high)
    outs[1][...] = dot(hot, low)


def mirror():
    row = lax.broadcasted_iota(jnp.int32, (NB, NB), 0)
    col = lax.broadcasted_iota(jnp.int32, (NB, NB), 1)
    return jnp.where(row + col // 36 * 72 == col + 180, 1.0, 0.0).astype(BF)


def project(offset, picked, jac_ref, high_ref, low_ref, extra):
    elems = jac_ref.shape[0]
    count = (picked[0].shape[1] - offset) // NB
    half = OVL // 2
    flip = mirror()

    def apply(pair, table, dims=((1,), (0,))):
        size = pair[0].shape[0]
        both = dot(jnp.concatenate(pair, 0), high_ref[table], dims)
        return both[:size] + (both[size:] + dot(pair[0], low_ref[table], dims))

    def fields_of(ref, first, last):
        at = slice(first * elems, last * elems)
        return [
            ref[at, offset + f * NB : offset + (f + 1) * NB].astype(BF) for f in range(count)
        ]

    turned = jnp.concatenate([x for ref in picked for x in fields_of(ref, 0, half)], 0)
    turned = dot(turned, flip).astype(BF)
    total = None
    for n in range(half):
        source = []
        for m, ref in enumerate(picked):
            rows = fields_of(ref, half + n, half + n + 1)
            for f in range(count):
                base = ((m * count + f) * half + n) * elems
                rows.append(turned[base : base + elems])
            source.append(jnp.concatenate(rows, 0))
        values = apply(source, half + n)
        weights = jac_ref[:, (half + n) * QP : (half + n + 1) * QP]
        other = [
            pltpu.roll(jac_ref[:, base : base + 128], 64, 1)
            for base in range((n + 1) * QP - 128, n * QP - 128, -128)
        ]
        other = jnp.concatenate(other, 1)
        scaled = values * jnp.concatenate([weights] * count + [other] * count, 0)
        if extra:
            scaled = jnp.concatenate([scaled, weights, other], 0)
        part = apply(split(scaled), half - 1 - n, NT)
        total = part if total is None else total + part
    own = [total[: count * elems]]
    turned = [total[count * elems : 2 * count * elems]]
    if extra:
        own.append(total[2 * count * elems : (2 * count + 1) * elems])
        turned.append(total[(2 * count + 1) * elems :])
    own, turned = jnp.concatenate(own, 0), jnp.concatenate(turned, 0)
    high = turned.astype(BF)
    middle, low = split(turned - high.astype(F32))
    size = turned.shape[0]
    back = dot(jnp.concatenate([high, middle, low], 0), flip)
    return own + ((back[:size] + back[size : 2 * size]) + back[2 * size :])


def fold(rows, stride, end):
    lane = lax.broadcasted_iota(jnp.int32, (rows.shape[0], PAD), 1)
    keep = (lane // stride % 6 == end) & (lane < NB)
    out = []
    for c in range(4):
        face = jnp.where(keep, rows[:, c * PAD : (c + 1) * PAD], 0.0)
        out.append(face[:, : PAD // 2] + face[:, PAD // 2 :])
    return jnp.concatenate(out, 1)


def unfold(face):
    half = PAD // 2
    out = []
    for c in range(4):
        out += [face[:, c * half : (c + 1) * half]] * 2
    return jnp.concatenate(out, 1)


def send_faces(even, first, last, stride, send_ref, back_ref):
    first, last = fold(first, stride, 0), fold(last, stride, 5)
    send_ref[...] = jnp.where(even, last, first)
    back_ref[...] = jnp.where(even, first, last)


def take_faces(axis, got, back):
    me, count = lax.axis_index(axis), lax.axis_size(axis)
    even = me % 2 == 0
    got, back = unfold(got), unfold(back)
    before = jnp.where(even, back, got)
    after = jnp.where(even, got, back)
    return jnp.where(me > 0, before, 0.0), jnp.where(me < count - 1, after, 0.0)


def lead_kernel(owners, count, ids_ref, index_ref, jac_ref, high_ref, low_ref, fhigh_ref, flow_ref, *refs):
    column = refs[:owners]
    packed = refs[owners : owners + count]
    refs = refs[owners + count :]
    fields_ref, lumped_ref, parts_ref, send_ref, back_ref, *picked = refs
    elems = jac_ref.shape[0]
    hot = jnp.concatenate(hits(index_ref, ids_ref[...], range(OVL)), 0).astype(BF)
    rows = lanes_of((*column, *packed), NB * FIELDS, 0)
    pick(hot, jnp.concatenate(rows, 0), picked)
    total = project(0, picked, jac_ref, high_ref, low_ref, True)
    lumped = total[2 * elems :]
    lumped_ref[...] = lumped
    fields = [total[f * elems : (f + 1) * elems] / lumped for f in range(2)]
    for f in range(2):
        fields_ref[:, f * NB : (f + 1) * NB] = fields[f]
    pressure = fields[0] * fields[1]
    force = dot3(split(pressure), (fhigh_ref[...], flow_ref[...]))
    mass = jnp.concatenate([lumped * (1.0 / 4096.0), jnp.zeros((elems, PAD - NB), F32)], 1)
    parts = jnp.concatenate([force, mass], 1)
    parts_ref[...] = parts
    width = EY * EZ
    even = lax.axis_index("gx") % 2 == 0
    send_faces(even, parts[:width], parts[-width:], 36, send_ref, back_ref)


def tail_rows(near, far):
    start = CUT - 128
    rows = []
    for a, b in zip(near, far):
        if a.shape[1] == NB * FIELDS:
            rows.append(a[:, start:])
        else:
            rows.append(jnp.concatenate([a[:, start:], b[...]], 1))
    return jnp.concatenate(rows, 0)


def ready_kernel(owners, ids_ref, index_ref, *refs):
    near, far = refs[:owners], refs[owners : 2 * owners]
    high_ref, low_ref = refs[2 * owners :]
    rows = tail_rows(near, far)
    wanted = ids_ref[:, : rows.shape[0]]
    hot = jnp.concatenate(hits(index_ref, wanted, range(OVL)), 0).astype(BF)
    high, low = split(rows)
    high_ref[...] = dot(hot, high).astype(BF)
    low_ref[...] = dot(hot, low).astype(BF)


def tail_kernel(count, ids_ref, index_ref, jac_ref, high_ref, low_ref, lumped_ref, lead_ref, *refs):
    base_high, base_low = refs[:2]
    near, far = refs[2 : 2 + count], refs[2 + count : 2 + 2 * count]
    out_ref, *picked = refs[2 + 2 * count :]
    elems = jac_ref.shape[0]
    rows = tail_rows(near, far)
    wanted = ids_ref[:, ids_ref.shape[1] - rows.shape[0] :]
    hot = jnp.concatenate(hits(index_ref, wanted, range(OVL)), 0).astype(BF)
    high, low = split(rows)
    picked[0][...] = base_high[...].astype(F32) + dot(hot, high)
    picked[1][...] = base_low[...].astype(F32) + dot(hot, low)
    total = project(2 * NB - CUT + 128, picked, jac_ref, high_ref, low_ref, False)
    lumped = lumped_ref[...]
    out_ref[:, : 2 * NB] = lead_ref[...]
    for f in range(3):
        out_ref[:, (f + 2) * NB : (f + 3) * NB] = total[f * elems : (f + 1) * elems] / lumped


def face_add(parts, before, after, shift, stride):
    comps = []
    elems = parts.shape[0]
    lane = lax.broadcasted_iota(jnp.int32, (elems, PAD), 1)
    spot = lane // stride % 6
    inside = lane < NB
    for c in range(4):
        at = slice(c * PAD, (c + 1) * PAD)
        low = pltpu.roll(before[:, at], PAD - shift, 1)
        high = pltpu.roll(after[:, at], shift, 1)
        low = jnp.where((spot == 0) & inside, low, 0.0)
        high = jnp.where((spot == 5) & inside, high, 0.0)
        comps.append(parts[:, at] + (low + high))
    return jnp.concatenate(comps, 1)


def x_kernel(parts_ref, got_ref, turn_ref, out_ref, send_ref, back_ref):
    parts = parts_ref[...]
    width = EY * EZ
    before, after = take_faces("gx", got_ref[...], turn_ref[...])
    before = jnp.concatenate([before, parts[:-width]], 0)
    after = jnp.concatenate([parts[width:], after], 0)
    parts = face_add(parts, before, after, 180, 36)
    out_ref[...] = parts
    first = [parts[x * width : x * width + EZ] for x in range(EX)]
    last = [parts[(x + 1) * width - EZ : (x + 1) * width] for x in range(EX)]
    first, last = jnp.concatenate(first, 0), jnp.concatenate(last, 0)
    send_faces(lax.axis_index("gy") % 2 == 0, first, last, 6, send_ref, back_ref)


def y_kernel(parts_ref, got_ref, turn_ref, out_ref, *face_refs):
    parts = parts_ref[...]
    width = EY * EZ
    far_before, far_after = take_faces("gy", got_ref[...], turn_ref[...])
    before = []
    after = []
    for x in range(EX):
        base = x * width
        near = slice(x * EZ, (x + 1) * EZ)
        before += [far_before[near], parts[base : base + width - EZ]]
        after += [parts[base + EZ : base + width], far_after[near]]
    before = jnp.concatenate(before, 0)
    after = jnp.concatenate(after, 0)
    parts = face_add(parts, before, after, 30, 6)
    out_ref[...] = parts
    last, first = fold(parts, 1, 5), fold(parts, 1, 0)
    if len(face_refs) == 1:
        face_refs[0][...] = jnp.where(lax.axis_index("gz") % 2 == 0, last, first)
    else:
        face_refs[0][...] = last
        face_refs[1][...] = first


def z_kernel(parts_ref, before_ref, after_ref, out_ref):
    parts = parts_ref[...]
    elems = parts.shape[0]
    odd = lax.broadcasted_iota(jnp.int32, parts.shape, 0) % EZ == EZ - 1
    has_before = lax.axis_index("gz") > 0
    has_after = lax.axis_index("gz") < lax.axis_size("gz") - 1
    far_before = jnp.where(has_before, pltpu.roll(unfold(before_ref[...]), elems - 1, 0), 0.0)
    far_after = jnp.where(has_after, pltpu.roll(unfold(after_ref[...]), 1, 0), 0.0)
    before = jnp.where(odd, pltpu.roll(parts, 1, 0), far_before)
    after = jnp.where(odd, far_after, pltpu.roll(parts, elems - 1, 0))
    parts = face_add(parts, before, after, 5, 1)
    mass = parts[:, 3 * PAD :]
    for c in range(3):
        accel = parts[:, c * PAD : c * PAD + NB] / mass[:, :NB]
        out_ref[:, c * NB : (c + 1) * NB] = accel


VM = pl.BlockSpec(memory_space=pltpu.VMEM)
HB = pl.BlockSpec(memory_space=pltpu.HBM)


def call(kernel, shapes, specs, scratch=(), cost=None):
    return pl.pallas_call(
        kernel,
        out_shape=shapes,
        in_specs=specs,
        out_specs=jax.tree.map(lambda _: VM, shapes),
        scratch_shapes=scratch,
        cost_estimate=cost,
        compiler_params=pltpu.CompilerParams(vmem_limit_bytes=16 << 20),
    )


def partner(count, step):
    if count & (count - 1) == 0:
        return [(i, i ^ step) for i in range(count)]
    return [(i, (i + step) % count) for i in range(count)]


def slot_of(owner, me, count):
    if count & (count - 1) == 0:
        return owner ^ me
    return (me - owner) % count


def shape(dims, dtype=F32):
    return jax.ShapeDtypeStruct(dims, dtype)


def swap_faces(piece, back, axis, count):
    near = [(i, i ^ 1) for i in range(count)]
    across = [(i, (i + 1) % count if i % 2 else (i - 1) % count) for i in range(count)]
    return lax.ppermute(piece, axis, near), lax.ppermute(back, axis, across)


def per_device(src_fields, owner_peer, src_local, jac):
    n_x = lax.axis_size("gx")
    n_y = lax.axis_size("gy")
    n_z = lax.axis_size("gz")
    elems = src_fields.shape[0]
    width = src_fields.shape[1]
    capacity = max(2, 9 * elems // (n_x * n_y))
    slots = n_y * capacity
    nearest = lax.ppermute(src_fields, "gy", partner(n_y, 1))
    total = n_y * elems + (n_x - 1) * slots
    turned = (OVL, elems)
    own_a, own_b, ids, index, *masks = call(
        lambda *refs: front_kernel(n_y, capacity, *refs),
        (
            shape((elems, CUT)),
            shape((elems, width - CUT)),
            shape((1, total), jnp.int32),
            shape(src_local.shape, jnp.int32),
        )
        + (shape((8, n_y * elems)),) * (n_x - 1),
        [HB] * 3,
        [pltpu.VMEM(turned, jnp.int32)] * 2 + [pltpu.SemaphoreType.DMA((4,))],
    )(*[
        pltpu.with_memory_space_constraint(operand, pltpu.HBM)
        for operand in (src_fields, owner_peer[:, :, 0].T, src_local.T)
    ])
    columns = [
        [piece, nearest] + [lax.ppermute(piece, "gy", partner(n_y, step)) for step in range(2, n_y)]
        for piece in (own_a, own_b)
    ]
    fhigh, flow = force_table()
    table = shape((OVL, NB, QP), BF)
    heavy = pl.CostEstimate(flops=2_000_000_000, bytes_accessed=8_000_000, transcendentals=0)
    high, low = call(prep_kernel, (table, table), [], cost=heavy)()
    asked = [lax.ppermute(mask, "gx", partner(n_x, step + 1)) for step, mask in enumerate(masks)]
    gathered = []
    for part in range(2):
        span = (CUT, width - CUT)[part]
        packed = call(
            lambda *refs: pack_kernel(n_y, capacity, n_x - 1, width, part, *refs),
            (shape((slots, span)),) * (n_x - 1),
            [VM] * (n_x - 1 + n_y),
        )(*asked, *columns[part])
        arrived = [
            lax.ppermute(piece, "gx", partner(n_x, step))
            for step, piece in enumerate(packed, 1)
        ]
        gathered.append(columns[part] + arrived)
    near, far = gathered
    face = shape((EY * EZ, 2 * PAD))
    whole = shape((elems, 4 * PAD))
    lead, lumped, parts, piece, back = call(
        lambda *refs: lead_kernel(n_y, n_x - 1, *refs),
        (shape((elems, 2 * NB)), shape((elems, NB)), whole, face, face),
        [VM] * (7 + len(near)),
        [pltpu.VMEM((OVL * elems, CUT), F32)] * 2,
    )(ids, index, jac, high, low, fhigh, flow, *near)
    got, turn = swap_faces(piece, back, "gx", n_x)
    rows_here = (*near[:n_y], *far[:n_y])
    picks = shape((OVL * elems, width - CUT + 128), BF)
    base = call(
        lambda *refs: ready_kernel(n_y, *refs),
        (picks, picks),
        [VM] * (2 + len(rows_here)),
        cost=heavy,
    )(ids, index, *rows_here)
    got, turn, base = lax.optimization_barrier((got, turn, base))
    face = shape((EX * EZ, 2 * PAD))
    parts, piece, back = call(x_kernel, (whole, face, face), [VM] * 3)(parts, got, turn)
    got, turn = swap_faces(piece, back, "gy", n_y)
    scratch = pltpu.VMEM((OVL * elems, width - CUT + 128), F32)
    fields = call(
        lambda *refs: tail_kernel(n_x - 1, *refs),
        shape((elems, width)),
        [VM] * (9 + 2 * (n_x - 1)),
        [scratch] * 2,
        heavy,
    )(ids, index, jac, high, low, lumped, lead, *base, *near[n_y:], *far[n_y:])
    got, turn, fields = lax.optimization_barrier((got, turn, fields))
    ends = (shape((elems, 2 * PAD)),) * (1 if n_z == 2 else 2)
    parts, *ends = call(y_kernel, (whole, *ends), [VM] * 3)(parts, got, turn)
    if n_z == 2:
        before = after = lax.ppermute(ends[0], "gz", [(0, 1), (1, 0)])
    else:
        before = lax.ppermute(ends[0], "gz", [(i, i + 1) for i in range(n_z - 1)])
        after = lax.ppermute(ends[1], "gz", [(i + 1, i) for i in range(n_z - 1)])
    accel = call(z_kernel, shape((elems, 3 * NB)), [VM] * 3)(parts, before, after)
    return fields, accel


def solution(mesh):
    rows = ("gx", "gy", "gz")
    placed = (P(rows, None), P(rows, None, None), P(rows, None), P(rows, None))

    return jax.shard_map(
        per_device,
        mesh=mesh,
        in_specs=placed,
        out_specs=(P(rows, None), P(rows, None)),
        check_vma=False,
    )
```

```python
import math

import jax
import jax.numpy as jnp
import numpy as np
from jax import lax
from jax.experimental import pallas as pl
from jax.experimental.pallas import tpu as pltpu
from jax.sharding import PartitionSpec as P

EX = 4
EY = 4
EZ = 2
FIELDS = 5
NB = 216
QP = 512
OVL = 8
PAD = 256
CUT = 512
BF = jnp.bfloat16
F32 = jnp.float32


def three_way(table):
    parts = []
    rest = np.asarray(table, np.float32)
    for _ in range(3):
        part = rest.astype(jnp.bfloat16)
        parts.append(part)
        rest = rest - part.astype(np.float32)
    return parts


def lower_integral(first, second):
    if first < 0 or first > 4:
        return 0.0
    return math.comb(4, first) * math.comb(5, second) / (10.0 * math.comb(9, first + second))


def force_table():
    mass_one = np.zeros((6, 6))
    grad_one = np.zeros((6, 6))
    for left in range(6):
        for right in range(6):
            mass_one[left, right] = (
                math.comb(5, left) * math.comb(5, right) / (11.0 * math.comb(10, left + right))
            )
            grad_one[left, right] = 5.0 * (
                lower_integral(left - 1, right) - lower_integral(left, right)
            )
    grad_x = np.kron(grad_one, np.kron(mass_one, mass_one))
    grad_y = np.kron(mass_one, np.kron(grad_one, mass_one))
    grad_z = np.kron(mass_one, np.kron(mass_one, grad_one))
    joined = np.zeros((NB, 3 * PAD), np.float32)
    for c, grad in enumerate((grad_x, grad_y, grad_z)):
        joined[:, c * PAD : c * PAD + NB] = grad.T * 8.0
    high, low, _ = three_way(joined)
    return jnp.asarray(high, BF), jnp.asarray(low, BF)


def split(value):
    high = value.astype(BF)
    return high, (value - high.astype(F32)).astype(BF)


def dot(a, b, dims=((1,), (0,))):
    return lax.dot_general(a, b, (dims, ((), ())), preferred_element_type=F32)


def dot3(a, b, dims=((1,), (0,))):
    return dot(a[0], b[0], dims) + (dot(a[0], b[1], dims) + dot(a[1], b[0], dims))


NT = ((1,), (1,))


def bern_rows(stride, bit):
    row = lax.broadcasted_iota(jnp.int32, (8, QP), 0)
    point = lax.broadcasted_iota(jnp.int32, (8, QP), 1) // stride % 8
    u = point.astype(F32) * (1.0 / 16.0) + (1.0 / 32.0 + 0.5 - 0.5 * bit)
    value = jnp.zeros((8, QP), F32)
    for i in range(6):
        value = jnp.where(row == i, float(math.comb(5, i)), value)
    for n in range(5):
        value = value * jnp.where(row > n, u, 1.0 - u)
    return value


def prep_kernel(high_ref, low_ref):
    coef = lax.broadcasted_iota(jnp.int32, (NB, 24), 0)
    col = lax.broadcasted_iota(jnp.int32, (NB, 24), 1)
    factors = []
    for stride, spacing in ((36, 64), (6, 8), (1, 1)):
        pick = jnp.where(coef // stride % 6 == col % 8, 1.0, 0.0).astype(BF)
        pair = []
        for bit in range(2):
            rows = bern_rows(spacing, bit)
            high = rows.astype(BF)
            middle, low = split(rows - high.astype(F32))
            parts = [part.astype(F32) for part in (high, middle, low)]
            pair.append(dot(pick, jnp.concatenate(parts, 0).astype(BF)))
        factors.append(pair)
    for k in range(OVL):
        table = factors[0][k >> 2 & 1] * factors[1][k >> 1 & 1] * factors[2][k & 1]
        high, low = split(table)
        high_ref[k] = high
        low_ref[k] = low


def hits(index_ref, wanted, spans):
    elems = index_ref.shape[0]
    out = []
    for k in spans:
        column = jnp.broadcast_to(index_ref[:, k : k + 1], (elems, wanted.shape[1]))
        out.append(jnp.where(column == wanted, 1.0, 0.0))
    return out


def packing(mask, capacity, elems, owners):
    width = owners * elems
    row = lax.broadcasted_iota(jnp.int32, (width, width), 0)
    col = lax.broadcasted_iota(jnp.int32, (width, width), 1)
    earlier = jnp.where((row // elems == col // elems) & (row < col), 1.0, 0.0).astype(BF)
    rank = dot(jnp.broadcast_to(mask, (8, width)).astype(BF), earlier)[:1]
    slots = owners * capacity
    spot = lax.broadcasted_iota(jnp.int32, (slots, width), 0)
    lane = lax.broadcasted_iota(jnp.int32, (slots, width), 1)
    wanted = (lane // elems * capacity).astype(F32) + rank
    hit = (spot.astype(F32) == wanted) & (jnp.broadcast_to(mask, (slots, width)) > 0.5)
    return jnp.where(hit, 1.0, 0.0).astype(BF)


def front_kernel(owners, capacity, rows, owner, local, near_ref, far_ref, ids_ref, index_ref, *refs):
    *mask_refs, owner_ref, local_ref, sems = refs
    pairs = (
        (owner, owner_ref),
        (local, local_ref),
        (rows.at[:, :CUT], near_ref),
        (rows.at[:, CUT:], far_ref),
    )
    copies = [
        pltpu.make_async_copy(source, target, sems.at[n]) for n, (source, target) in enumerate(pairs)
    ]
    for copy in copies:
        copy.start()
    elems = owner.shape[1]
    copies[0].wait()
    copies[1].wait()
    owner = owner_ref[...]
    outer = slot_of(owner // owners, lax.axis_index("gx"), lax.axis_size("gx"))
    inner = slot_of(owner % owners, lax.axis_index("gy"), owners)
    index_ref[...] = ((outer * owners + inner) * elems + local_ref[...]).T
    width = owners * elems
    lane = lax.broadcasted_iota(jnp.int32, (elems, (1 + len(mask_refs)) * width), 1)
    named = sum(hits(index_ref, lane, range(OVL)))
    named = jnp.sum(named, 0, keepdims=True)
    mask = jnp.where(named > 0.5, 1.0, 0.0)
    ids_ref[:, :width] = lane[:1, :width]
    local = lax.broadcasted_iota(jnp.int32, (8, width), 1) + 1
    slots = owners * capacity
    for s, mask_ref in enumerate(mask_refs):
        part = mask[:, (s + 1) * width : (s + 2) * width]
        mask_ref[...] = jnp.broadcast_to(part, mask_ref.shape)
        order = packing(part, capacity, elems, owners)
        ids = dot(local.astype(F32).astype(BF), order, NT)[:1].astype(jnp.int32)
        ids = jnp.where(ids > 0, ids + ((s + 1) * width - 1), -1)
        ids_ref[:, width + s * slots : width + (s + 1) * slots] = ids
    copies[2].wait()
    copies[3].wait()


def lanes_of(pieces, width, part):
    span = slice(0, CUT) if part == 0 else slice(CUT, width)
    return [ref[:, span] if ref.shape[1] == width else ref[...] for ref in pieces]


def pack_kernel(owners, capacity, count, width, part, *refs):
    masks = refs[:count]
    column = refs[count : count + owners]
    outs = refs[count + owners :]
    elems = column[0].shape[0]
    order = jnp.concatenate(
        [packing(mask[:1], capacity, elems, owners) for mask in masks], 0
    )
    rows = jnp.concatenate(lanes_of(column, width, part), 0)
    high = rows.astype(BF)
    rest = rows - high.astype(F32)
    middle, low = split(rest)
    packed = (dot(order, high) + dot(order, middle)) + dot(order, low)
    slots = owners * capacity
    for s in range(count):
        outs[s][...] = packed[s * slots : (s + 1) * slots]


def pick(hot, rows, outs):
    high, low = split(rows)
    outs[0][...] = dot(hot, high)
    outs[1][...] = dot(hot, low)


def mirror():
    row = lax.broadcasted_iota(jnp.int32, (NB, NB), 0)
    col = lax.broadcasted_iota(jnp.int32, (NB, NB), 1)
    return jnp.where(row + col // 36 * 72 == col + 180, 1.0, 0.0).astype(BF)


def project(pairs, offset, picked, jac_ref, high_ref, low_ref, extra):
    elems = jac_ref.shape[0]
    count = (picked[0].shape[1] - offset) // NB
    half = OVL // 2
    flip = mirror()

    def apply(pair, table, dims=((1,), (0,))):
        size = pair[0].shape[0]
        both = dot(jnp.concatenate(pair, 0), high_ref[table], dims)
        return both[:size] + (both[size:] + dot(pair[0], low_ref[table], dims))

    def fields_of(ref, first, last):
        at = slice(first * elems, last * elems)
        return [
            ref[at, offset + f * NB : offset + (f + 1) * NB].astype(BF) for f in range(count)
        ]

    size = len(pairs)
    turned = jnp.concatenate([x for ref in picked for x in fields_of(ref, 0, size)], 0)
    turned = dot(turned, flip).astype(BF)
    total = None
    for spot, n in enumerate(pairs):
        source = []
        for m, ref in enumerate(picked):
            rows = fields_of(ref, size + spot, size + spot + 1)
            for f in range(count):
                base = ((m * count + f) * size + spot) * elems
                rows.append(turned[base : base + elems])
            source.append(jnp.concatenate(rows, 0))
        values = apply(source, half + n)
        weights = jac_ref[:, (half + n) * QP : (half + n + 1) * QP]
        other = [
            pltpu.roll(jac_ref[:, base : base + 128], 64, 1)
            for base in range((n + 1) * QP - 128, n * QP - 128, -128)
        ]
        other = jnp.concatenate(other, 1)
        scaled = values * jnp.concatenate([weights] * count + [other] * count, 0)
        if extra:
            scaled = jnp.concatenate([scaled, weights, other], 0)
        part = apply(split(scaled), half - 1 - n, NT)
        total = part if total is None else total + part
    own = [total[: count * elems]]
    turned = [total[count * elems : 2 * count * elems]]
    if extra:
        own.append(total[2 * count * elems : (2 * count + 1) * elems])
        turned.append(total[(2 * count + 1) * elems :])
    own, turned = jnp.concatenate(own, 0), jnp.concatenate(turned, 0)
    high = turned.astype(BF)
    middle, low = split(turned - high.astype(F32))
    size = turned.shape[0]
    back = dot(jnp.concatenate([high, middle, low], 0), flip)
    return own + ((back[:size] + back[size : 2 * size]) + back[2 * size :])


def fold(rows, stride, end):
    lane = lax.broadcasted_iota(jnp.int32, (rows.shape[0], PAD), 1)
    keep = (lane // stride % 6 == end) & (lane < NB)
    out = []
    for c in range(4):
        face = jnp.where(keep, rows[:, c * PAD : (c + 1) * PAD], 0.0)
        out.append(face[:, : PAD // 2] + face[:, PAD // 2 :])
    return jnp.concatenate(out, 1)


def unfold(face):
    half = PAD // 2
    out = []
    for c in range(4):
        out += [face[:, c * half : (c + 1) * half]] * 2
    return jnp.concatenate(out, 1)


def send_faces(even, first, last, stride, send_ref, back_ref):
    first, last = fold(first, stride, 0), fold(last, stride, 5)
    send_ref[...] = jnp.where(even, last, first)
    back_ref[...] = jnp.where(even, first, last)


def take_faces(axis, got, back):
    me, count = lax.axis_index(axis), lax.axis_size(axis)
    even = me % 2 == 0
    got, back = unfold(got), unfold(back)
    before = jnp.where(even, back, got)
    after = jnp.where(even, got, back)
    return jnp.where(me > 0, before, 0.0), jnp.where(me < count - 1, after, 0.0)


def lead_kernel(owners, count, ids_ref, index_ref, jac_ref, high_ref, low_ref, fhigh_ref, flow_ref, *refs):
    column = refs[:owners]
    packed = refs[owners : owners + count]
    refs = refs[owners + count :]
    fields_ref, lumped_ref, parts_ref, send_ref, back_ref, *picked = refs
    elems = jac_ref.shape[0]
    hot = jnp.concatenate(hits(index_ref, ids_ref[...], range(OVL)), 0).astype(BF)
    rows = lanes_of((*column, *packed), NB * FIELDS, 0)
    pick(hot, jnp.concatenate(rows, 0), picked)
    total = project(range(OVL // 2), 0, picked, jac_ref, high_ref, low_ref, True)
    lumped = total[2 * elems :]
    lumped_ref[...] = lumped
    fields = [total[f * elems : (f + 1) * elems] / lumped for f in range(2)]
    for f in range(2):
        fields_ref[:, f * NB : (f + 1) * NB] = fields[f]
    pressure = fields[0] * fields[1]
    force = dot3(split(pressure), (fhigh_ref[...], flow_ref[...]))
    mass = jnp.concatenate([lumped * (1.0 / 4096.0), jnp.zeros((elems, PAD - NB), F32)], 1)
    parts = jnp.concatenate([force, mass], 1)
    parts_ref[...] = parts
    width = EY * EZ
    even = lax.axis_index("gx") % 2 == 0
    send_faces(even, parts[:width], parts[-width:], 36, send_ref, back_ref)


def tail_kernel(count, pairs, ids_ref, index_ref, jac_ref, high_ref, low_ref, *refs):
    near, far = refs[:count], refs[count : 2 * count]
    refs = refs[2 * count :]
    first = pairs[0] == 0
    if not first:
        sum_ref, lumped_ref, lead_ref, *refs = refs
    out_ref, *picked = refs
    elems = jac_ref.shape[0]
    start = CUT - 128
    spans = [*pairs, *[OVL // 2 + n for n in pairs]]
    hot = jnp.concatenate(hits(index_ref, ids_ref[...], spans), 0).astype(BF)
    rows = []
    for a, b in zip(near, far):
        if a.shape[1] == NB * FIELDS:
            rows.append(a[:, start:])
        else:
            rows.append(jnp.concatenate([a[:, start:], b[...]], 1))
    pick(hot, jnp.concatenate(rows, 0), picked)
    total = project(pairs, 2 * NB - start, picked, jac_ref, high_ref, low_ref, False)
    if first:
        out_ref[...] = total
        return
    total = total + sum_ref[...]
    lumped = lumped_ref[...]
    out_ref[:, : 2 * NB] = lead_ref[...]
    for f in range(3):
        out_ref[:, (f + 2) * NB : (f + 3) * NB] = total[f * elems : (f + 1) * elems] / lumped


def face_add(parts, before, after, shift, stride):
    comps = []
    elems = parts.shape[0]
    lane = lax.broadcasted_iota(jnp.int32, (elems, PAD), 1)
    spot = lane // stride % 6
    inside = lane < NB
    for c in range(4):
        at = slice(c * PAD, (c + 1) * PAD)
        low = pltpu.roll(before[:, at], PAD - shift, 1)
        high = pltpu.roll(after[:, at], shift, 1)
        low = jnp.where((spot == 0) & inside, low, 0.0)
        high = jnp.where((spot == 5) & inside, high, 0.0)
        comps.append(parts[:, at] + (low + high))
    return jnp.concatenate(comps, 1)


def x_kernel(parts_ref, got_ref, turn_ref, out_ref, send_ref, back_ref):
    parts = parts_ref[...]
    width = EY * EZ
    before, after = take_faces("gx", got_ref[...], turn_ref[...])
    before = jnp.concatenate([before, parts[:-width]], 0)
    after = jnp.concatenate([parts[width:], after], 0)
    parts = face_add(parts, before, after, 180, 36)
    out_ref[...] = parts
    first = [parts[x * width : x * width + EZ] for x in range(EX)]
    last = [parts[(x + 1) * width - EZ : (x + 1) * width] for x in range(EX)]
    first, last = jnp.concatenate(first, 0), jnp.concatenate(last, 0)
    send_faces(lax.axis_index("gy") % 2 == 0, first, last, 6, send_ref, back_ref)


def y_kernel(parts_ref, got_ref, turn_ref, out_ref, *face_refs):
    parts = parts_ref[...]
    width = EY * EZ
    far_before, far_after = take_faces("gy", got_ref[...], turn_ref[...])
    before = []
    after = []
    for x in range(EX):
        base = x * width
        near = slice(x * EZ, (x + 1) * EZ)
        before += [far_before[near], parts[base : base + width - EZ]]
        after += [parts[base + EZ : base + width], far_after[near]]
    before = jnp.concatenate(before, 0)
    after = jnp.concatenate(after, 0)
    parts = face_add(parts, before, after, 30, 6)
    out_ref[...] = parts
    last, first = fold(parts, 1, 5), fold(parts, 1, 0)
    if len(face_refs) == 1:
        face_refs[0][...] = jnp.where(lax.axis_index("gz") % 2 == 0, last, first)
    else:
        face_refs[0][...] = last
        face_refs[1][...] = first


def z_kernel(parts_ref, before_ref, after_ref, out_ref):
    parts = parts_ref[...]
    elems = parts.shape[0]
    odd = lax.broadcasted_iota(jnp.int32, parts.shape, 0) % EZ == EZ - 1
    has_before = lax.axis_index("gz") > 0
    has_after = lax.axis_index("gz") < lax.axis_size("gz") - 1
    far_before = jnp.where(has_before, pltpu.roll(unfold(before_ref[...]), elems - 1, 0), 0.0)
    far_after = jnp.where(has_after, pltpu.roll(unfold(after_ref[...]), 1, 0), 0.0)
    before = jnp.where(odd, pltpu.roll(parts, 1, 0), far_before)
    after = jnp.where(odd, far_after, pltpu.roll(parts, elems - 1, 0))
    parts = face_add(parts, before, after, 5, 1)
    mass = parts[:, 3 * PAD :]
    for c in range(3):
        accel = parts[:, c * PAD : c * PAD + NB] / mass[:, :NB]
        out_ref[:, c * NB : (c + 1) * NB] = accel


VM = pl.BlockSpec(memory_space=pltpu.VMEM)
HB = pl.BlockSpec(memory_space=pltpu.HBM)


def call(kernel, shapes, specs, scratch=(), cost=None):
    return pl.pallas_call(
        kernel,
        out_shape=shapes,
        in_specs=specs,
        out_specs=jax.tree.map(lambda _: VM, shapes),
        scratch_shapes=scratch,
        cost_estimate=cost,
        compiler_params=pltpu.CompilerParams(vmem_limit_bytes=16 << 20),
    )


def partner(count, step):
    if count & (count - 1) == 0:
        return [(i, i ^ step) for i in range(count)]
    return [(i, (i + step) % count) for i in range(count)]


def slot_of(owner, me, count):
    if count & (count - 1) == 0:
        return owner ^ me
    return (me - owner) % count


def shape(dims, dtype=F32):
    return jax.ShapeDtypeStruct(dims, dtype)


def swap_faces(piece, back, axis, count):
    near = [(i, i ^ 1) for i in range(count)]
    across = [(i, (i + 1) % count if i % 2 else (i - 1) % count) for i in range(count)]
    return lax.ppermute(piece, axis, near), lax.ppermute(back, axis, across)


def per_device(src_fields, owner_peer, src_local, jac):
    n_x = lax.axis_size("gx")
    n_y = lax.axis_size("gy")
    n_z = lax.axis_size("gz")
    elems = src_fields.shape[0]
    width = src_fields.shape[1]
    capacity = max(2, 9 * elems // (n_x * n_y))
    slots = n_y * capacity
    nearest = lax.ppermute(src_fields, "gy", partner(n_y, 1))
    total = n_y * elems + (n_x - 1) * slots
    turned = (OVL, elems)
    own_a, own_b, ids, index, *masks = call(
        lambda *refs: front_kernel(n_y, capacity, *refs),
        (
            shape((elems, CUT)),
            shape((elems, width - CUT)),
            shape((1, total), jnp.int32),
            shape(src_local.shape, jnp.int32),
        )
        + (shape((8, n_y * elems)),) * (n_x - 1),
        [HB] * 3,
        [pltpu.VMEM(turned, jnp.int32)] * 2 + [pltpu.SemaphoreType.DMA((4,))],
    )(*[
        pltpu.with_memory_space_constraint(operand, pltpu.HBM)
        for operand in (src_fields, owner_peer[:, :, 0].T, src_local.T)
    ])
    columns = [
        [piece, nearest] + [lax.ppermute(piece, "gy", partner(n_y, step)) for step in range(2, n_y)]
        for piece in (own_a, own_b)
    ]
    fhigh, flow = force_table()
    table = shape((OVL, NB, QP), BF)
    heavy = pl.CostEstimate(flops=2_000_000_000, bytes_accessed=8_000_000, transcendentals=0)
    high, low = call(prep_kernel, (table, table), [], cost=heavy)()
    asked = [lax.ppermute(mask, "gx", partner(n_x, step + 1)) for step, mask in enumerate(masks)]
    gathered = []
    for part in range(2):
        span = (CUT, width - CUT)[part]
        packed = call(
            lambda *refs: pack_kernel(n_y, capacity, n_x - 1, width, part, *refs),
            (shape((slots, span)),) * (n_x - 1),
            [VM] * (n_x - 1 + n_y),
        )(*asked, *columns[part])
        arrived = [
            lax.ppermute(piece, "gx", partner(n_x, step + 1))
            for step, piece in enumerate(packed)
        ]
        gathered.append(columns[part] + arrived)
    near, far = gathered
    face = shape((EY * EZ, 2 * PAD))
    whole = shape((elems, 4 * PAD))
    lead, lumped, parts, piece, back = call(
        lambda *refs: lead_kernel(n_y, n_x - 1, *refs),
        (shape((elems, 2 * NB)), shape((elems, NB)), whole, face, face),
        [VM] * (7 + len(near)),
        [pltpu.VMEM((OVL * elems, CUT), F32)] * 2,
    )(ids, index, jac, high, low, fhigh, flow, *near)
    got, turn = swap_faces(piece, back, "gx", n_x)
    pairs = range(OVL // 2)
    split_at = OVL // 4

    def tail(pairs, out, *more):
        scratch = pltpu.VMEM((2 * len(pairs) * elems, width - CUT + 128), F32)
        return call(
            lambda *refs: tail_kernel(len(near), pairs, *refs),
            out,
            [VM] * (5 + 2 * len(near) + len(more)),
            [scratch] * 2,
            heavy,
        )(ids, index, jac, high, low, *near, *far, *more)

    partial = tail(pairs[:split_at], shape(((FIELDS - 2) * elems, NB)))
    got, turn, partial = lax.optimization_barrier((got, turn, partial))
    face = shape((EX * EZ, 2 * PAD))
    parts, piece, back = call(x_kernel, (whole, face, face), [VM] * 3)(parts, got, turn)
    got, turn = swap_faces(piece, back, "gy", n_y)
    fields = tail(pairs[split_at:], shape((elems, width)), partial, lumped, lead)
    got, turn, fields = lax.optimization_barrier((got, turn, fields))
    ends = (shape((elems, 2 * PAD)),) * (1 if n_z == 2 else 2)
    parts, *ends = call(y_kernel, (whole, *ends), [VM] * 3)(parts, got, turn)
    if n_z == 2:
        before = after = lax.ppermute(ends[0], "gz", [(0, 1), (1, 0)])
    else:
        before = lax.ppermute(ends[0], "gz", [(i, i + 1) for i in range(n_z - 1)])
        after = lax.ppermute(ends[1], "gz", [(i + 1, i) for i in range(n_z - 1)])
    accel = call(z_kernel, shape((elems, 3 * NB)), [VM] * 3)(parts, before, after)
    return fields, accel


def solution(mesh):
    rows = ("gx", "gy", "gz")
    placed = (P(rows, None), P(rows, None, None), P(rows, None), P(rows, None))

    return jax.shard_map(
        per_device,
        mesh=mesh,
        in_specs=placed,
        out_specs=(P(rows, None), P(rows, None)),
        check_vma=False,
    )
```

```python
import math

import jax
import jax.numpy as jnp
import numpy as np
from jax import lax
from jax.experimental import pallas as pl
from jax.experimental.pallas import tpu as pltpu
from jax.sharding import PartitionSpec as P

EX = 4
EY = 4
EZ = 2
FIELDS = 5
NB = 216
QP = 512
OVL = 8
PAD = 256
CUT = 440
BLOCKS = CUT // 128
EDGE = CUT % 128
BF = jnp.bfloat16
F32 = jnp.float32


def three_way(table):
    parts = []
    rest = np.asarray(table, np.float32)
    for _ in range(3):
        part = rest.astype(jnp.bfloat16)
        parts.append(part)
        rest = rest - part.astype(np.float32)
    return parts


def lower_integral(first, second):
    if first < 0 or first > 4:
        return 0.0
    return math.comb(4, first) * math.comb(5, second) / (10.0 * math.comb(9, first + second))


def force_table():
    mass_one = np.zeros((6, 6))
    grad_one = np.zeros((6, 6))
    for left in range(6):
        for right in range(6):
            mass_one[left, right] = (
                math.comb(5, left) * math.comb(5, right) / (11.0 * math.comb(10, left + right))
            )
            grad_one[left, right] = 5.0 * (
                lower_integral(left - 1, right) - lower_integral(left, right)
            )
    grad_x = np.kron(grad_one, np.kron(mass_one, mass_one))
    grad_y = np.kron(mass_one, np.kron(grad_one, mass_one))
    grad_z = np.kron(mass_one, np.kron(mass_one, grad_one))
    joined = np.zeros((NB, 3 * PAD), np.float32)
    for c, grad in enumerate((grad_x, grad_y, grad_z)):
        joined[:, c * PAD : c * PAD + NB] = grad.T * 8.0
    high, low, _ = three_way(joined)
    return jnp.asarray(high, BF), jnp.asarray(low, BF)


def split(value):
    high = value.astype(BF)
    return high, (value - high.astype(F32)).astype(BF)


def dot(a, b, dims=((1,), (0,))):
    return lax.dot_general(a, b, (dims, ((), ())), preferred_element_type=F32)


def dot3(a, b, dims=((1,), (0,))):
    return dot(a[0], b[0], dims) + (dot(a[0], b[1], dims) + dot(a[1], b[0], dims))


NT = ((1,), (1,))


def bern_rows(stride, bit):
    row = lax.broadcasted_iota(jnp.int32, (8, QP), 0)
    point = lax.broadcasted_iota(jnp.int32, (8, QP), 1) // stride % 8
    u = point.astype(F32) * (1.0 / 16.0) + (1.0 / 32.0 + 0.5 - 0.5 * bit)
    value = jnp.zeros((8, QP), F32)
    for i in range(6):
        value = jnp.where(row == i, float(math.comb(5, i)), value)
    for n in range(5):
        value = value * jnp.where(row > n, u, 1.0 - u)
    return value


def prep_kernel(high_ref, low_ref):
    coef = lax.broadcasted_iota(jnp.int32, (NB, 24), 0)
    col = lax.broadcasted_iota(jnp.int32, (NB, 24), 1)
    factors = []
    for stride, spacing in ((36, 64), (6, 8), (1, 1)):
        pick = jnp.where(coef // stride % 6 == col % 8, 1.0, 0.0).astype(BF)
        pair = []
        for bit in range(2):
            rows = bern_rows(spacing, bit)
            high = rows.astype(BF)
            middle, low = split(rows - high.astype(F32))
            parts = [part.astype(F32) for part in (high, middle, low)]
            pair.append(dot(pick, jnp.concatenate(parts, 0).astype(BF)))
        factors.append(pair)
    for k in range(OVL):
        table = factors[0][k >> 2 & 1] * factors[1][k >> 1 & 1] * factors[2][k & 1]
        high, low = split(table)
        high_ref[k] = high
        low_ref[k] = low


def hits(index_ref, wanted, spans):
    elems = index_ref.shape[0]
    out = []
    for k in spans:
        column = jnp.broadcast_to(index_ref[:, k : k + 1], (elems, wanted.shape[1]))
        out.append(jnp.where(column == wanted, 1.0, 0.0))
    return out


def packing(mask, capacity, elems, owners):
    width = owners * elems
    row = lax.broadcasted_iota(jnp.int32, (width, width), 0)
    col = lax.broadcasted_iota(jnp.int32, (width, width), 1)
    earlier = jnp.where((row // elems == col // elems) & (row < col), 1.0, 0.0).astype(BF)
    rank = dot(jnp.broadcast_to(mask, (8, width)).astype(BF), earlier)[:1]
    slots = owners * capacity
    spot = lax.broadcasted_iota(jnp.int32, (slots, width), 0)
    lane = lax.broadcasted_iota(jnp.int32, (slots, width), 1)
    wanted = (lane // elems * capacity).astype(F32) + rank
    hit = (spot.astype(F32) == wanted) & (jnp.broadcast_to(mask, (slots, width)) > 0.5)
    return jnp.where(hit, 1.0, 0.0).astype(BF)


def front_kernel(owners, capacity, rows, owner, local, near_ref, far_ref, ids_ref, index_ref, *refs):
    *mask_refs, owner_ref, local_ref, rows_ref, sems = refs
    pairs = (
        (owner, owner_ref),
        (local, local_ref),
        (rows, rows_ref),
    )
    copies = [
        pltpu.make_async_copy(source, target, sems.at[n]) for n, (source, target) in enumerate(pairs)
    ]
    for copy in copies:
        copy.start()
    elems = owner.shape[1]
    copies[0].wait()
    copies[1].wait()
    owner = owner_ref[...]
    outer = slot_of(owner // owners, lax.axis_index("gx"), lax.axis_size("gx"))
    inner = slot_of(owner % owners, lax.axis_index("gy"), owners)
    index_ref[...] = ((outer * owners + inner) * elems + local_ref[...]).T
    width = owners * elems
    lane = lax.broadcasted_iota(jnp.int32, (elems, (1 + len(mask_refs)) * width), 1)
    named = sum(hits(index_ref, lane, range(OVL)))
    named = jnp.sum(named, 0, keepdims=True)
    mask = jnp.where(named > 0.5, 1.0, 0.0)
    ids_ref[:, :width] = lane[:1, :width]
    local = lax.broadcasted_iota(jnp.int32, (8, width), 1) + 1
    slots = owners * capacity
    for s, mask_ref in enumerate(mask_refs):
        part = mask[:, (s + 1) * width : (s + 2) * width]
        mask_ref[...] = jnp.broadcast_to(part, mask_ref.shape)
        order = packing(part, capacity, elems, owners)
        ids = dot(local.astype(F32).astype(BF), order, NT)[:1].astype(jnp.int32)
        ids = jnp.where(ids > 0, ids + ((s + 1) * width - 1), -1)
        ids_ref[:, width + s * slots : width + (s + 1) * slots] = ids
    copies[2].wait()
    near_ref[...] = rows_ref[:, :CUT]
    far_ref[...] = rows_ref[:, CUT:]


def lanes_of(pieces, width, part):
    span = slice(0, CUT) if part == 0 else slice(CUT, width)
    return [ref[:, span] if ref.shape[1] == width else ref[...] for ref in pieces]


def pack_kernel(owners, capacity, count, width, part, *refs):
    masks = refs[:count]
    column = refs[count : count + owners]
    outs = refs[count + owners :]
    elems = column[0].shape[0]
    order = jnp.concatenate(
        [packing(mask[:1], capacity, elems, owners) for mask in masks], 0
    )
    rows = jnp.concatenate(lanes_of(column, width, part), 0)
    high = rows.astype(BF)
    rest = rows - high.astype(F32)
    middle, low = split(rest)
    packed = (dot(order, high) + dot(order, middle)) + dot(order, low)
    slots = owners * capacity
    for s in range(count):
        piece = packed[s * slots : (s + 1) * slots]
        if part:
            outs[s][...] = piece
            continue
        for n in range(BLOCKS):
            outs[s][n * slots : (n + 1) * slots] = piece[:, n * 128 : (n + 1) * 128]
        first = upper_rows(slots)
        edge = piece[:, BLOCKS * 128 :]
        fill = jnp.zeros((2 * first - slots, EDGE), F32)
        lower = jnp.concatenate([edge[first:], fill], 0) if 2 * first > slots else edge[first:]
        blank = jnp.zeros((first, 128 - 2 * EDGE), F32)
        outs[s][BLOCKS * slots :] = jnp.concatenate([edge[:first], lower, blank], 1)


def upper_rows(slots):
    return -(-slots // 16) * 8


def edge_lanes(ref, slots):
    first = upper_rows(slots)
    edge = ref[BLOCKS * slots :]
    return jnp.concatenate([edge[:, :EDGE], edge[: slots - first, EDGE : 2 * EDGE]], 0)


def dense_rows(ref, slots):
    blocks = [ref[n * slots : (n + 1) * slots] for n in range(BLOCKS)]
    return jnp.concatenate([*blocks, edge_lanes(ref, slots)], 1)


def pick(hot, rows, outs):
    high, low = split(rows)
    outs[0][...] = dot(hot, high)
    outs[1][...] = dot(hot, low)


def mirror():
    row = lax.broadcasted_iota(jnp.int32, (NB, NB), 0)
    col = lax.broadcasted_iota(jnp.int32, (NB, NB), 1)
    return jnp.where(row + col // 36 * 72 == col + 180, 1.0, 0.0).astype(BF)


def project(offset, picked, jac_ref, high_ref, low_ref, extra):
    elems = jac_ref.shape[0]
    count = (picked[0].shape[1] - offset) // NB
    half = OVL // 2
    flip = mirror()

    def apply(pair, table, dims=((1,), (0,))):
        size = pair[0].shape[0]
        both = dot(jnp.concatenate(pair, 0), high_ref[table], dims)
        return both[:size] + (both[size:] + dot(pair[0], low_ref[table], dims))

    def fields_of(ref, first, last):
        at = slice(first * elems, last * elems)
        return [
            ref[at, offset + f * NB : offset + (f + 1) * NB].astype(BF) for f in range(count)
        ]

    turned = jnp.concatenate([x for ref in picked for x in fields_of(ref, 0, half)], 0)
    turned = dot(turned, flip).astype(BF)
    total = None
    for n in range(half):
        source = []
        for m, ref in enumerate(picked):
            rows = fields_of(ref, half + n, half + n + 1)
            for f in range(count):
                base = ((m * count + f) * half + n) * elems
                rows.append(turned[base : base + elems])
            source.append(jnp.concatenate(rows, 0))
        values = apply(source, half + n)
        weights = jac_ref[:, (half + n) * QP : (half + n + 1) * QP]
        other = [
            pltpu.roll(jac_ref[:, base : base + 128], 64, 1)
            for base in range((n + 1) * QP - 128, n * QP - 128, -128)
        ]
        other = jnp.concatenate(other, 1)
        scaled = values * jnp.concatenate([weights] * count + [other] * count, 0)
        if extra:
            scaled = jnp.concatenate([scaled, weights, other], 0)
        part = apply(split(scaled), half - 1 - n, NT)
        total = part if total is None else total + part
    own = [total[: count * elems]]
    turned = [total[count * elems : 2 * count * elems]]
    if extra:
        own.append(total[2 * count * elems : (2 * count + 1) * elems])
        turned.append(total[(2 * count + 1) * elems :])
    own, turned = jnp.concatenate(own, 0), jnp.concatenate(turned, 0)
    high = turned.astype(BF)
    middle, low = split(turned - high.astype(F32))
    size = turned.shape[0]
    back = dot(jnp.concatenate([high, middle, low], 0), flip)
    return own + ((back[:size] + back[size : 2 * size]) + back[2 * size :])


def fold(rows, stride, end):
    lane = lax.broadcasted_iota(jnp.int32, (rows.shape[0], PAD), 1)
    keep = (lane // stride % 6 == end) & (lane < NB)
    out = []
    for c in range(4):
        face = jnp.where(keep, rows[:, c * PAD : (c + 1) * PAD], 0.0)
        out.append(face[:, : PAD // 2] + face[:, PAD // 2 :])
    return jnp.concatenate(out, 1)


def unfold(face):
    half = PAD // 2
    out = []
    for c in range(4):
        out += [face[:, c * half : (c + 1) * half]] * 2
    return jnp.concatenate(out, 1)


def send_faces(even, first, last, stride, send_ref, back_ref):
    first, last = fold(first, stride, 0), fold(last, stride, 5)
    send_ref[...] = jnp.where(even, last, first)
    back_ref[...] = jnp.where(even, first, last)


def take_faces(axis, got, back):
    me, count = lax.axis_index(axis), lax.axis_size(axis)
    even = me % 2 == 0
    got, back = unfold(got), unfold(back)
    before = jnp.where(even, back, got)
    after = jnp.where(even, got, back)
    return jnp.where(me > 0, before, 0.0), jnp.where(me < count - 1, after, 0.0)


def lead_kernel(owners, count, slots, ids_ref, index_ref, jac_ref, high_ref, low_ref, fhigh_ref, flow_ref, *refs):
    column = refs[:owners]
    packed = refs[owners : owners + count]
    refs = refs[owners + count :]
    fields_ref, lumped_ref, parts_ref, send_ref, back_ref, *picked = refs
    elems = jac_ref.shape[0]
    hot = jnp.concatenate(hits(index_ref, ids_ref[...], range(OVL)), 0).astype(BF)
    rows = lanes_of(column, NB * FIELDS, 0) + [dense_rows(ref, slots) for ref in packed]
    pick(hot, jnp.concatenate(rows, 0), picked)
    total = project(0, picked, jac_ref, high_ref, low_ref, True)
    lumped = total[2 * elems :]
    lumped_ref[...] = lumped
    fields = [total[f * elems : (f + 1) * elems] / lumped for f in range(2)]
    for f in range(2):
        fields_ref[:, f * NB : (f + 1) * NB] = fields[f]
    pressure = fields[0] * fields[1]
    force = dot3(split(pressure), (fhigh_ref[...], flow_ref[...]))
    mass = jnp.concatenate([lumped * (1.0 / 4096.0), jnp.zeros((elems, PAD - NB), F32)], 1)
    parts = jnp.concatenate([force, mass], 1)
    parts_ref[...] = parts
    width = EY * EZ
    even = lax.axis_index("gx") % 2 == 0
    send_faces(even, parts[:width], parts[-width:], 36, send_ref, back_ref)


def tail_kernel(count, slots, ids_ref, index_ref, jac_ref, high_ref, low_ref, lumped_ref, lead_ref, *refs):
    near, far = refs[:count], refs[count : 2 * count]
    out_ref, *picked = refs[2 * count :]
    elems = jac_ref.shape[0]
    hot = jnp.concatenate(hits(index_ref, ids_ref[...], range(OVL)), 0).astype(BF)
    rows = []
    for a, b in zip(near, far):
        if a.shape[1] == NB * FIELDS:
            rows.append(a[:, 2 * NB :])
        elif a.shape[1] == CUT:
            rows.append(jnp.concatenate([a[:, 2 * NB :], b[...]], 1))
        else:
            edge = edge_lanes(a, slots)[:, 2 * NB - BLOCKS * 128 :]
            rows.append(jnp.concatenate([edge, b[...]], 1))
    pick(hot, jnp.concatenate(rows, 0), picked)
    total = project(0, picked, jac_ref, high_ref, low_ref, False)
    lumped = lumped_ref[...]
    out_ref[:, : 2 * NB] = lead_ref[...]
    for f in range(3):
        out_ref[:, (f + 2) * NB : (f + 3) * NB] = total[f * elems : (f + 1) * elems] / lumped


def face_add(parts, before, after, shift, stride):
    comps = []
    elems = parts.shape[0]
    lane = lax.broadcasted_iota(jnp.int32, (elems, PAD), 1)
    spot = lane // stride % 6
    inside = lane < NB
    for c in range(4):
        at = slice(c * PAD, (c + 1) * PAD)
        low = pltpu.roll(before[:, at], PAD - shift, 1)
        high = pltpu.roll(after[:, at], shift, 1)
        low = jnp.where((spot == 0) & inside, low, 0.0)
        high = jnp.where((spot == 5) & inside, high, 0.0)
        comps.append(parts[:, at] + (low + high))
    return jnp.concatenate(comps, 1)


def x_kernel(parts_ref, got_ref, turn_ref, out_ref, send_ref, back_ref):
    parts = parts_ref[...]
    width = EY * EZ
    before, after = take_faces("gx", got_ref[...], turn_ref[...])
    before = jnp.concatenate([before, parts[:-width]], 0)
    after = jnp.concatenate([parts[width:], after], 0)
    parts = face_add(parts, before, after, 180, 36)
    out_ref[...] = parts
    first = [parts[x * width : x * width + EZ] for x in range(EX)]
    last = [parts[(x + 1) * width - EZ : (x + 1) * width] for x in range(EX)]
    first, last = jnp.concatenate(first, 0), jnp.concatenate(last, 0)
    send_faces(lax.axis_index("gy") % 2 == 0, first, last, 6, send_ref, back_ref)


def y_kernel(parts_ref, got_ref, turn_ref, out_ref, *face_refs):
    parts = parts_ref[...]
    width = EY * EZ
    far_before, far_after = take_faces("gy", got_ref[...], turn_ref[...])
    before = []
    after = []
    for x in range(EX):
        base = x * width
        near = slice(x * EZ, (x + 1) * EZ)
        before += [far_before[near], parts[base : base + width - EZ]]
        after += [parts[base + EZ : base + width], far_after[near]]
    before = jnp.concatenate(before, 0)
    after = jnp.concatenate(after, 0)
    parts = face_add(parts, before, after, 30, 6)
    out_ref[...] = parts
    last, first = fold(parts, 1, 5), fold(parts, 1, 0)
    if len(face_refs) == 1:
        face_refs[0][...] = jnp.where(lax.axis_index("gz") % 2 == 0, last, first)
    else:
        face_refs[0][...] = last
        face_refs[1][...] = first


def z_kernel(parts_ref, before_ref, after_ref, out_ref):
    parts = parts_ref[...]
    elems = parts.shape[0]
    odd = lax.broadcasted_iota(jnp.int32, parts.shape, 0) % EZ == EZ - 1
    has_before = lax.axis_index("gz") > 0
    has_after = lax.axis_index("gz") < lax.axis_size("gz") - 1
    far_before = jnp.where(has_before, pltpu.roll(unfold(before_ref[...]), elems - 1, 0), 0.0)
    far_after = jnp.where(has_after, pltpu.roll(unfold(after_ref[...]), 1, 0), 0.0)
    before = jnp.where(odd, pltpu.roll(parts, 1, 0), far_before)
    after = jnp.where(odd, far_after, pltpu.roll(parts, elems - 1, 0))
    parts = face_add(parts, before, after, 5, 1)
    mass = parts[:, 3 * PAD :]
    for c in range(3):
        accel = parts[:, c * PAD : c * PAD + NB] / mass[:, :NB]
        out_ref[:, c * NB : (c + 1) * NB] = accel


VM = pl.BlockSpec(memory_space=pltpu.VMEM)
HB = pl.BlockSpec(memory_space=pltpu.HBM)


def call(kernel, shapes, specs, scratch=(), cost=None):
    return pl.pallas_call(
        kernel,
        out_shape=shapes,
        in_specs=specs,
        out_specs=jax.tree.map(lambda _: VM, shapes),
        scratch_shapes=scratch,
        cost_estimate=cost,
        compiler_params=pltpu.CompilerParams(vmem_limit_bytes=16 << 20),
    )


def partner(count, step):
    if count & (count - 1) == 0:
        return [(i, i ^ step) for i in range(count)]
    return [(i, (i + step) % count) for i in range(count)]


def slot_of(owner, me, count):
    if count & (count - 1) == 0:
        return owner ^ me
    return (me - owner) % count


def shape(dims, dtype=F32):
    return jax.ShapeDtypeStruct(dims, dtype)


def swap_faces(piece, back, axis, count):
    near = [(i, i ^ 1) for i in range(count)]
    across = [(i, (i + 1) % count if i % 2 else (i - 1) % count) for i in range(count)]
    return lax.ppermute(piece, axis, near), lax.ppermute(back, axis, across)


def per_device(src_fields, owner_peer, src_local, jac):
    n_x = lax.axis_size("gx")
    n_y = lax.axis_size("gy")
    n_z = lax.axis_size("gz")
    elems = src_fields.shape[0]
    width = src_fields.shape[1]
    capacity = max(2, 9 * elems // (n_x * n_y))
    slots = n_y * capacity
    nearest = lax.ppermute(src_fields, "gy", partner(n_y, 1))
    total = n_y * elems + (n_x - 1) * slots
    turned = (OVL, elems)
    own_a, own_b, ids, index, *masks = call(
        lambda *refs: front_kernel(n_y, capacity, *refs),
        (
            shape((elems, CUT)),
            shape((elems, width - CUT)),
            shape((1, total), jnp.int32),
            shape(src_local.shape, jnp.int32),
        )
        + (shape((8, n_y * elems)),) * (n_x - 1),
        [HB] * 3,
        [pltpu.VMEM(turned, jnp.int32)] * 2
        + [pltpu.VMEM((elems, width), F32), pltpu.SemaphoreType.DMA((3,))],
    )(*[
        pltpu.with_memory_space_constraint(operand, pltpu.HBM)
        for operand in (src_fields, owner_peer[:, :, 0].T, src_local.T)
    ])
    columns = [
        [piece, nearest] + [lax.ppermute(piece, "gy", partner(n_y, step)) for step in range(2, n_y)]
        for piece in (own_a, own_b)
    ]
    fhigh, flow = force_table()
    table = shape((OVL, NB, QP), BF)
    heavy = pl.CostEstimate(flops=2_000_000_000, bytes_accessed=8_000_000, transcendentals=0)
    high, low = call(prep_kernel, (table, table), [], cost=heavy)()
    asked = [lax.ppermute(mask, "gx", partner(n_x, step + 1)) for step, mask in enumerate(masks)]
    gathered = []
    for part in range(2):
        dense = (BLOCKS * slots + upper_rows(slots), 128)
        piece_shape = (dense, (slots, width - CUT))[part]
        packed = call(
            lambda *refs: pack_kernel(n_y, capacity, n_x - 1, width, part, *refs),
            (shape(piece_shape),) * (n_x - 1),
            [VM] * (n_x - 1 + n_y),
        )(*asked, *columns[part])
        arrived = [
            lax.ppermute(piece, "gx", partner(n_x, step + 1))
            for step, piece in enumerate(packed)
        ]
        gathered.append(columns[part] + arrived)
    near, far = gathered
    face = shape((EY * EZ, 2 * PAD))
    whole = shape((elems, 4 * PAD))
    lead, lumped, parts, piece, back = call(
        lambda *refs: lead_kernel(n_y, n_x - 1, slots, *refs),
        (shape((elems, 2 * NB)), shape((elems, NB)), whole, face, face),
        [VM] * (7 + len(near)),
        [pltpu.VMEM((OVL * elems, CUT), F32)] * 2,
    )(ids, index, jac, high, low, fhigh, flow, *near)
    got, turn = swap_faces(piece, back, "gx", n_x)
    face = shape((EX * EZ, 2 * PAD))
    parts, piece, back = call(x_kernel, (whole, face, face), [VM] * 3)(parts, got, turn)
    got, turn = swap_faces(piece, back, "gy", n_y)
    scratch = pltpu.VMEM((OVL * elems, width - 2 * NB), F32)
    fields = call(
        lambda *refs: tail_kernel(len(near), slots, *refs),
        shape((elems, width)),
        [VM] * (7 + 2 * len(near)),
        [scratch] * 2,
        heavy,
    )(ids, index, jac, high, low, lumped, lead, *near, *far)
    got, turn, fields = lax.optimization_barrier((got, turn, fields))
    ends = (shape((elems, 2 * PAD)),) * (1 if n_z == 2 else 2)
    parts, *ends = call(y_kernel, (whole, *ends), [VM] * 3)(parts, got, turn)
    if n_z == 2:
        before = after = lax.ppermute(ends[0], "gz", [(0, 1), (1, 0)])
    else:
        before = lax.ppermute(ends[0], "gz", [(i, i + 1) for i in range(n_z - 1)])
        after = lax.ppermute(ends[1], "gz", [(i + 1, i) for i in range(n_z - 1)])
    accel = call(z_kernel, shape((elems, 3 * NB)), [VM] * 3)(parts, before, after)
    return fields, accel


def solution(mesh):
    rows = ("gx", "gy", "gz")
    placed = (P(rows, None), P(rows, None, None), P(rows, None), P(rows, None))

    return jax.shard_map(
        per_device,
        mesh=mesh,
        in_specs=placed,
        out_specs=(P(rows, None), P(rows, None)),
        check_vma=False,
    )
```

```python
import math

import jax
import jax.numpy as jnp
import numpy as np
from jax import lax
from jax.experimental import pallas as pl
from jax.experimental.pallas import tpu as pltpu
from jax.sharding import PartitionSpec as P

EX = 4
EY = 4
EZ = 2
FIELDS = 5
NB = 216
QP = 512
OVL = 8
PAD = 256
CUT = 512
BF = jnp.bfloat16
F32 = jnp.float32


def three_way(table):
    parts = []
    rest = np.asarray(table, np.float32)
    for _ in range(3):
        part = rest.astype(jnp.bfloat16)
        parts.append(part)
        rest = rest - part.astype(np.float32)
    return parts


def lower_integral(first, second):
    if first < 0 or first > 4:
        return 0.0
    return math.comb(4, first) * math.comb(5, second) / (10.0 * math.comb(9, first + second))


def force_table():
    mass_one = np.zeros((6, 6))
    grad_one = np.zeros((6, 6))
    for left in range(6):
        for right in range(6):
            mass_one[left, right] = (
                math.comb(5, left) * math.comb(5, right) / (11.0 * math.comb(10, left + right))
            )
            grad_one[left, right] = 5.0 * (
                lower_integral(left - 1, right) - lower_integral(left, right)
            )
    grad_x = np.kron(grad_one, np.kron(mass_one, mass_one))
    grad_y = np.kron(mass_one, np.kron(grad_one, mass_one))
    grad_z = np.kron(mass_one, np.kron(mass_one, grad_one))
    joined = np.zeros((NB, 3 * PAD), np.float32)
    for c, grad in enumerate((grad_x, grad_y, grad_z)):
        joined[:, c * PAD : c * PAD + NB] = grad.T * 8.0
    high, low, _ = three_way(joined)
    return jnp.asarray(high, BF), jnp.asarray(low, BF)


def split(value):
    high = value.astype(BF)
    return high, (value - high.astype(F32)).astype(BF)


def dot(a, b, dims=((1,), (0,))):
    return lax.dot_general(a, b, (dims, ((), ())), preferred_element_type=F32)


def dot3(a, b, dims=((1,), (0,))):
    return dot(a[0], b[0], dims) + (dot(a[0], b[1], dims) + dot(a[1], b[0], dims))


NT = ((1,), (1,))


def bern_rows(stride, bit):
    row = lax.broadcasted_iota(jnp.int32, (8, QP), 0)
    point = lax.broadcasted_iota(jnp.int32, (8, QP), 1) // stride % 8
    u = point.astype(F32) * (1.0 / 16.0) + (1.0 / 32.0 + 0.5 - 0.5 * bit)
    value = jnp.zeros((8, QP), F32)
    for i in range(6):
        value = jnp.where(row == i, float(math.comb(5, i)), value)
    for n in range(5):
        value = value * jnp.where(row > n, u, 1.0 - u)
    return value


def prep_kernel(high_ref, low_ref):
    coef = lax.broadcasted_iota(jnp.int32, (NB, 24), 0)
    col = lax.broadcasted_iota(jnp.int32, (NB, 24), 1)
    factors = []
    for stride, spacing in ((36, 64), (6, 8), (1, 1)):
        pick = jnp.where(coef // stride % 6 == col % 8, 1.0, 0.0).astype(BF)
        pair = []
        for bit in range(2):
            rows = bern_rows(spacing, bit)
            high = rows.astype(BF)
            middle, low = split(rows - high.astype(F32))
            parts = [part.astype(F32) for part in (high, middle, low)]
            pair.append(dot(pick, jnp.concatenate(parts, 0).astype(BF)))
        factors.append(pair)
    for k in range(OVL):
        table = factors[0][k >> 2 & 1] * factors[1][k >> 1 & 1] * factors[2][k & 1]
        high, low = split(table)
        high_ref[k] = high
        low_ref[k] = low


def hits(index_ref, wanted, spans):
    elems = index_ref.shape[0]
    out = []
    for k in spans:
        column = jnp.broadcast_to(index_ref[:, k : k + 1], (elems, wanted.shape[1]))
        out.append(jnp.where(column == wanted, 1.0, 0.0))
    return out


def packing(mask, capacity, elems, owners):
    width = owners * elems
    row = lax.broadcasted_iota(jnp.int32, (width, width), 0)
    col = lax.broadcasted_iota(jnp.int32, (width, width), 1)
    earlier = jnp.where((row // elems == col // elems) & (row < col), 1.0, 0.0).astype(BF)
    rank = dot(jnp.broadcast_to(mask, (8, width)).astype(BF), earlier)[:1]
    slots = owners * capacity
    spot = lax.broadcasted_iota(jnp.int32, (slots, width), 0)
    lane = lax.broadcasted_iota(jnp.int32, (slots, width), 1)
    wanted = (lane // elems * capacity).astype(F32) + rank
    hit = (spot.astype(F32) == wanted) & (jnp.broadcast_to(mask, (slots, width)) > 0.5)
    return jnp.where(hit, 1.0, 0.0).astype(BF)


def front_kernel(owners, capacity, rows, owner, local, near_ref, far_ref, ids_ref, index_ref, *refs):
    *mask_refs, owner_ref, local_ref, sems = refs
    pairs = (
        (owner, owner_ref),
        (local, local_ref),
        (rows.at[:, :CUT], near_ref),
        (rows.at[:, CUT:], far_ref),
    )
    copies = [
        pltpu.make_async_copy(source, target, sems.at[n]) for n, (source, target) in enumerate(pairs)
    ]
    for copy in copies:
        copy.start()
    elems = owner.shape[1]
    copies[0].wait()
    copies[1].wait()
    owner = owner_ref[...]
    outer = slot_of(owner // owners, lax.axis_index("gx"), lax.axis_size("gx"))
    inner = slot_of(owner % owners, lax.axis_index("gy"), owners)
    index_ref[...] = ((outer * owners + inner) * elems + local_ref[...]).T
    width = owners * elems
    lane = lax.broadcasted_iota(jnp.int32, (elems, (1 + len(mask_refs)) * width), 1)
    named = sum(hits(index_ref, lane, range(OVL)))
    named = jnp.sum(named, 0, keepdims=True)
    mask = jnp.where(named > 0.5, 1.0, 0.0)
    ids_ref[:, :width] = lane[:1, :width]
    local = lax.broadcasted_iota(jnp.int32, (8, width), 1) + 1
    slots = owners * capacity
    for s, mask_ref in enumerate(mask_refs):
        part = mask[:, (s + 1) * width : (s + 2) * width]
        mask_ref[...] = jnp.broadcast_to(part, mask_ref.shape)
        order = packing(part, capacity, elems, owners)
        ids = dot(local.astype(F32).astype(BF), order, NT)[:1].astype(jnp.int32)
        ids = jnp.where(ids > 0, ids + ((s + 1) * width - 1), -1)
        ids_ref[:, width + s * slots : width + (s + 1) * slots] = ids
    copies[2].wait()
    copies[3].wait()


def lanes_of(pieces, width, part):
    span = slice(0, CUT) if part == 0 else slice(CUT, width)
    return [ref[:, span] if ref.shape[1] == width else ref[...] for ref in pieces]


def pack_kernel(owners, capacity, count, width, part, *refs):
    masks = refs[:count]
    column = refs[count : count + owners]
    outs = refs[count + owners :]
    elems = column[0].shape[0]
    order = jnp.concatenate(
        [packing(mask[:1], capacity, elems, owners) for mask in masks], 0
    )
    rows = jnp.concatenate(lanes_of(column, width, part), 0)
    high = rows.astype(BF)
    rest = rows - high.astype(F32)
    middle, low = split(rest)
    packed = (dot(order, high) + dot(order, middle)) + dot(order, low)
    slots = owners * capacity
    for s in range(count):
        outs[s][...] = packed[s * slots : (s + 1) * slots]


def pick(hot, rows, outs):
    high, low = split(rows)
    outs[0][...] = dot(hot, high)
    outs[1][...] = dot(hot, low)


def mirror():
    row = lax.broadcasted_iota(jnp.int32, (NB, NB), 0)
    col = lax.broadcasted_iota(jnp.int32, (NB, NB), 1)
    return jnp.where(row + col // 36 * 72 == col + 180, 1.0, 0.0).astype(BF)


def project(offset, picked, jac_ref, high_ref, low_ref, extra):
    elems = jac_ref.shape[0]
    count = (picked[0].shape[1] - offset) // NB
    half = OVL // 2
    flip = mirror()

    def apply(pair, table, dims=((1,), (0,))):
        size = pair[0].shape[0]
        both = dot(jnp.concatenate(pair, 0), high_ref[table], dims)
        return both[:size] + (both[size:] + dot(pair[0], low_ref[table], dims))

    def fields_of(ref, first, last):
        at = slice(first * elems, last * elems)
        return [
            ref[at, offset + f * NB : offset + (f + 1) * NB].astype(BF) for f in range(count)
        ]

    turned = jnp.concatenate([x for ref in picked for x in fields_of(ref, 0, half)], 0)
    turned = dot(turned, flip).astype(BF)
    total = None
    for n in range(half):
        source = []
        for m, ref in enumerate(picked):
            rows = fields_of(ref, half + n, half + n + 1)
            for f in range(count):
                base = ((m * count + f) * half + n) * elems
                rows.append(turned[base : base + elems])
            source.append(jnp.concatenate(rows, 0))
        values = apply(source, half + n)
        weights = jac_ref[:, (half + n) * QP : (half + n + 1) * QP]
        other = [
            pltpu.roll(jac_ref[:, base : base + 128], 64, 1)
            for base in range((n + 1) * QP - 128, n * QP - 128, -128)
        ]
        other = jnp.concatenate(other, 1)
        scaled = values * jnp.concatenate([weights] * count + [other] * count, 0)
        if extra:
            scaled = jnp.concatenate([scaled, weights, other], 0)
        part = apply(split(scaled), half - 1 - n, NT)
        total = part if total is None else total + part
    own = [total[: count * elems]]
    turned = [total[count * elems : 2 * count * elems]]
    if extra:
        own.append(total[2 * count * elems : (2 * count + 1) * elems])
        turned.append(total[(2 * count + 1) * elems :])
    own, turned = jnp.concatenate(own, 0), jnp.concatenate(turned, 0)
    high = turned.astype(BF)
    middle, low = split(turned - high.astype(F32))
    size = turned.shape[0]
    back = dot(jnp.concatenate([high, middle, low], 0), flip)
    return own + ((back[:size] + back[size : 2 * size]) + back[2 * size :])


def fold(rows, stride, end):
    lane = lax.broadcasted_iota(jnp.int32, (rows.shape[0], PAD), 1)
    keep = (lane // stride % 6 == end) & (lane < NB)
    out = []
    for c in range(4):
        face = jnp.where(keep, rows[:, c * PAD : (c + 1) * PAD], 0.0)
        out.append(face[:, : PAD // 2] + face[:, PAD // 2 :])
    return jnp.concatenate(out, 1)


def unfold(face):
    half = PAD // 2
    out = []
    for c in range(4):
        out += [face[:, c * half : (c + 1) * half]] * 2
    return jnp.concatenate(out, 1)


def send_faces(even, first, last, stride, send_ref, back_ref):
    first, last = fold(first, stride, 0), fold(last, stride, 5)
    send_ref[...] = jnp.where(even, last, first)
    back_ref[...] = jnp.where(even, first, last)


def take_faces(axis, got, back):
    me, count = lax.axis_index(axis), lax.axis_size(axis)
    even = me % 2 == 0
    got, back = unfold(got), unfold(back)
    before = jnp.where(even, back, got)
    after = jnp.where(even, got, back)
    return jnp.where(me > 0, before, 0.0), jnp.where(me < count - 1, after, 0.0)


def lead_kernel(owners, count, ids_ref, index_ref, jac_ref, high_ref, low_ref, fhigh_ref, flow_ref, *refs):
    column = refs[:owners]
    packed = refs[owners : owners + count]
    refs = refs[owners + count :]
    fields_ref, lumped_ref, parts_ref, send_ref, back_ref, *picked = refs
    elems = jac_ref.shape[0]
    hot = jnp.concatenate(hits(index_ref, ids_ref[...], range(OVL)), 0).astype(BF)
    rows = lanes_of((*column, *packed), NB * FIELDS, 0)
    pick(hot, jnp.concatenate(rows, 0), picked)
    total = project(0, picked, jac_ref, high_ref, low_ref, True)
    lumped = total[2 * elems :]
    lumped_ref[...] = lumped
    fields = [total[f * elems : (f + 1) * elems] / lumped for f in range(2)]
    for f in range(2):
        fields_ref[:, f * NB : (f + 1) * NB] = fields[f]
    pressure = fields[0] * fields[1]
    force = dot3(split(pressure), (fhigh_ref[...], flow_ref[...]))
    mass = jnp.concatenate([lumped * (1.0 / 4096.0), jnp.zeros((elems, PAD - NB), F32)], 1)
    parts = jnp.concatenate([force, mass], 1)
    parts_ref[...] = parts
    width = EY * EZ
    even = lax.axis_index("gx") % 2 == 0
    send_faces(even, parts[:width], parts[-width:], 36, send_ref, back_ref)


def tail_kernel(count, ids_ref, index_ref, jac_ref, high_ref, low_ref, *refs):
    near, far = refs[:count], refs[count : 2 * count]
    out_ref, *picked = refs[2 * count :]
    start = CUT - 128
    hot = jnp.concatenate(hits(index_ref, ids_ref[...], range(OVL)), 0).astype(BF)
    rows = []
    for a, b in zip(near, far):
        if a.shape[1] == NB * FIELDS:
            rows.append(a[:, start:])
        else:
            rows.append(jnp.concatenate([a[:, start:], b[...]], 1))
    pick(hot, jnp.concatenate(rows, 0), picked)
    out_ref[...] = project(2 * NB - start, picked, jac_ref, high_ref, low_ref, False)


def finish_kernel(total_ref, lumped_ref, lead_ref, out_ref):
    elems = lumped_ref.shape[0]
    lumped = lumped_ref[...]
    out_ref[:, : 2 * NB] = lead_ref[...]
    for f in range(FIELDS - 2):
        part = total_ref[f * elems : (f + 1) * elems]
        out_ref[:, (f + 2) * NB : (f + 3) * NB] = part / lumped


def face_add(parts, before, after, shift, stride):
    comps = []
    elems = parts.shape[0]
    lane = lax.broadcasted_iota(jnp.int32, (elems, PAD), 1)
    spot = lane // stride % 6
    inside = lane < NB
    for c in range(4):
        at = slice(c * PAD, (c + 1) * PAD)
        low = pltpu.roll(before[:, at], PAD - shift, 1)
        high = pltpu.roll(after[:, at], shift, 1)
        low = jnp.where((spot == 0) & inside, low, 0.0)
        high = jnp.where((spot == 5) & inside, high, 0.0)
        comps.append(parts[:, at] + (low + high))
    return jnp.concatenate(comps, 1)


def x_kernel(parts_ref, got_ref, turn_ref, out_ref, send_ref, back_ref):
    parts = parts_ref[...]
    width = EY * EZ
    before, after = take_faces("gx", got_ref[...], turn_ref[...])
    before = jnp.concatenate([before, parts[:-width]], 0)
    after = jnp.concatenate([parts[width:], after], 0)
    parts = face_add(parts, before, after, 180, 36)
    out_ref[...] = parts
    first = [parts[x * width : x * width + EZ] for x in range(EX)]
    last = [parts[(x + 1) * width - EZ : (x + 1) * width] for x in range(EX)]
    first, last = jnp.concatenate(first, 0), jnp.concatenate(last, 0)
    send_faces(lax.axis_index("gy") % 2 == 0, first, last, 6, send_ref, back_ref)


def y_kernel(parts_ref, got_ref, turn_ref, out_ref, *face_refs):
    parts = parts_ref[...]
    width = EY * EZ
    far_before, far_after = take_faces("gy", got_ref[...], turn_ref[...])
    before = []
    after = []
    for x in range(EX):
        base = x * width
        near = slice(x * EZ, (x + 1) * EZ)
        before += [far_before[near], parts[base : base + width - EZ]]
        after += [parts[base + EZ : base + width], far_after[near]]
    before = jnp.concatenate(before, 0)
    after = jnp.concatenate(after, 0)
    parts = face_add(parts, before, after, 30, 6)
    out_ref[...] = parts
    last, first = fold(parts, 1, 5), fold(parts, 1, 0)
    if len(face_refs) == 1:
        face_refs[0][...] = jnp.where(lax.axis_index("gz") % 2 == 0, last, first)
    else:
        face_refs[0][...] = last
        face_refs[1][...] = first


def z_kernel(parts_ref, before_ref, after_ref, out_ref):
    parts = parts_ref[...]
    elems = parts.shape[0]
    odd = lax.broadcasted_iota(jnp.int32, parts.shape, 0) % EZ == EZ - 1
    has_before = lax.axis_index("gz") > 0
    has_after = lax.axis_index("gz") < lax.axis_size("gz") - 1
    far_before = jnp.where(has_before, pltpu.roll(unfold(before_ref[...]), elems - 1, 0), 0.0)
    far_after = jnp.where(has_after, pltpu.roll(unfold(after_ref[...]), 1, 0), 0.0)
    before = jnp.where(odd, pltpu.roll(parts, 1, 0), far_before)
    after = jnp.where(odd, far_after, pltpu.roll(parts, elems - 1, 0))
    parts = face_add(parts, before, after, 5, 1)
    mass = parts[:, 3 * PAD :]
    for c in range(3):
        accel = parts[:, c * PAD : c * PAD + NB] / mass[:, :NB]
        out_ref[:, c * NB : (c + 1) * NB] = accel


VM = pl.BlockSpec(memory_space=pltpu.VMEM)
HB = pl.BlockSpec(memory_space=pltpu.HBM)


def call(kernel, shapes, specs, scratch=(), cost=None):
    return pl.pallas_call(
        kernel,
        out_shape=shapes,
        in_specs=specs,
        out_specs=jax.tree.map(lambda _: VM, shapes),
        scratch_shapes=scratch,
        cost_estimate=cost,
        compiler_params=pltpu.CompilerParams(vmem_limit_bytes=16 << 20),
    )


def partner(count, step):
    if count & (count - 1) == 0:
        return [(i, i ^ step) for i in range(count)]
    return [(i, (i + step) % count) for i in range(count)]


def slot_of(owner, me, count):
    if count & (count - 1) == 0:
        return owner ^ me
    return (me - owner) % count


def shape(dims, dtype=F32):
    return jax.ShapeDtypeStruct(dims, dtype)


def swap_faces(piece, back, axis, count):
    near = [(i, i ^ 1) for i in range(count)]
    across = [(i, (i + 1) % count if i % 2 else (i - 1) % count) for i in range(count)]
    return lax.ppermute(piece, axis, near), lax.ppermute(back, axis, across)


def per_device(src_fields, owner_peer, src_local, jac):
    n_x = lax.axis_size("gx")
    n_y = lax.axis_size("gy")
    n_z = lax.axis_size("gz")
    elems = src_fields.shape[0]
    width = src_fields.shape[1]
    capacity = max(2, 9 * elems // (n_x * n_y))
    slots = n_y * capacity
    nearest = lax.ppermute(src_fields, "gy", partner(n_y, 1))
    total = n_y * elems + (n_x - 1) * slots
    turned = (OVL, elems)
    own_a, own_b, ids, index, *masks = call(
        lambda *refs: front_kernel(n_y, capacity, *refs),
        (
            shape((elems, CUT)),
            shape((elems, width - CUT)),
            shape((1, total), jnp.int32),
            shape(src_local.shape, jnp.int32),
        )
        + (shape((8, n_y * elems)),) * (n_x - 1),
        [HB] * 3,
        [pltpu.VMEM(turned, jnp.int32)] * 2 + [pltpu.SemaphoreType.DMA((4,))],
    )(*[
        pltpu.with_memory_space_constraint(operand, pltpu.HBM)
        for operand in (src_fields, owner_peer[:, :, 0].T, src_local.T)
    ])
    columns = [
        [piece, nearest] + [lax.ppermute(piece, "gy", partner(n_y, step)) for step in range(2, n_y)]
        for piece in (own_a, own_b)
    ]
    fhigh, flow = force_table()
    table = shape((OVL, NB, QP), BF)
    heavy = pl.CostEstimate(flops=2_000_000_000, bytes_accessed=8_000_000, transcendentals=0)
    high, low = call(prep_kernel, (table, table), [], cost=heavy)()
    asked = [lax.ppermute(mask, "gx", partner(n_x, step + 1)) for step, mask in enumerate(masks)]
    gathered = []
    for part in range(2):
        span = (CUT, width - CUT)[part]
        packed = call(
            lambda *refs: pack_kernel(n_y, capacity, n_x - 1, width, part, *refs),
            (shape((slots, span)),) * (n_x - 1),
            [VM] * (n_x - 1 + n_y),
        )(*asked, *columns[part])
        arrived = [
            lax.ppermute(piece, "gx", partner(n_x, step))
            for step, piece in enumerate(packed, 1)
        ]
        gathered.append(columns[part] + arrived)
    near, far = gathered
    face = shape((EY * EZ, 2 * PAD))
    whole = shape((elems, 4 * PAD))
    lead, lumped, parts, piece, back = call(
        lambda *refs: lead_kernel(n_y, n_x - 1, *refs),
        (shape((elems, 2 * NB)), shape((elems, NB)), whole, face, face),
        [VM] * (7 + len(near)),
        [pltpu.VMEM((OVL * elems, CUT), F32)] * 2,
    )(ids, index, jac, high, low, fhigh, flow, *near)
    got, turn = swap_faces(piece, back, "gx", n_x)
    face = shape((EX * EZ, 2 * PAD))
    parts, piece, back = call(x_kernel, (whole, face, face), [VM] * 3)(parts, got, turn)
    got, turn = swap_faces(piece, back, "gy", n_y)
    scratch = pltpu.VMEM((OVL * elems, width - CUT + 128), F32)
    rest = call(
        lambda *refs: tail_kernel(len(near), *refs),
        shape(((FIELDS - 2) * elems, NB)),
        [VM] * (5 + 2 * len(near)),
        [scratch] * 2,
        heavy,
    )(ids, index, jac, high, low, *near, *far)
    got, turn, rest = lax.optimization_barrier((got, turn, rest))
    ends = (shape((elems, 2 * PAD)),) * (1 if n_z == 2 else 2)
    parts, *ends = call(y_kernel, (whole, *ends), [VM] * 3)(parts, got, turn)
    if n_z == 2:
        before = after = lax.ppermute(ends[0], "gz", [(0, 1), (1, 0)])
    else:
        before = lax.ppermute(ends[0], "gz", [(i, i + 1) for i in range(n_z - 1)])
        after = lax.ppermute(ends[1], "gz", [(i + 1, i) for i in range(n_z - 1)])
    fields = call(finish_kernel, shape((elems, width)), [VM] * 3, cost=heavy)(rest, lumped, lead)
    before, after, fields = lax.optimization_barrier((before, after, fields))
    accel = call(z_kernel, shape((elems, 3 * NB)), [VM] * 3)(parts, before, after)
    return fields, accel


def solution(mesh):
    rows = ("gx", "gy", "gz")
    placed = (P(rows, None), P(rows, None, None), P(rows, None), P(rows, None))

    return jax.shard_map(
        per_device,
        mesh=mesh,
        in_specs=placed,
        out_specs=(P(rows, None), P(rows, None)),
        check_vma=False,
    )
```
